32 devices in a mesh: head: 2 (over y), view: 4 (over z), row: 4 (over x, core).
Axes of the slice: x: 2, y: 2, z: 4, core: 2. Of those that a mesh axis runs over, the one named last changes fastest.
Arguments:
- query_feats: bfloat16 [4, 32, 16, 1024], P('view', 'row', None, 'head'), may hold values from -125 to 125
- key_feats: bfloat16 [4, 32, 16, 1024], P('view', 'row', None, 'head'), may hold values from -7 to 7
- value_feats: bfloat16 [4, 32, 16, 1024], P('view', 'row', None, 'head'), may hold values from -6 to 6
- target: bfloat16 [4, 32, 16, 1024], P('view', 'row', None, 'head'), may hold values from -6 to 6
- token_rates: float32 [4, 2, 512], P('view', 'head', 'row'), may hold values from 5 to 100
- row_reach: int32 [32], P('row'), may hold values from 1 to 2
- view_counts: int32 [4], P('view'), may hold values from 170 to 512
- w_first: bfloat16 [2, 512, 512], P('head'), may hold values from -0.25 to 0.25
- w_third: bfloat16 [2, 512, 512], P('head'), may hold values from -0.25 to 0.25
- w_second: bfloat16 [2, 512, 512], P('head'), may hold values from -0.25 to 0.25
Outputs:
- fast_out: bfloat16 [4, 32, 16, 1024], P('view', 'row', None, 'head')
The draws below stay inside these ranges and needn't reach their ends.
All inputs are finite; a program needn't handle non-finite values.
Results may differ from the reference program's by a relative error of at most 0.03.
Values may be sent and summed in bfloat16 or wider, within the bound.
A program may use at most 64 MiB of HBM per device.

```python
import math
import jax
import jax.numpy as jnp
from jax import lax

HEADS = 2
HD = 512
ATT_HD = 128
COLS = 16
ROWS_DEV = 8
HALO = 2
NR = 32
VIEWS = 4
VIEW_TOK = 512


def draw_pair(key):
    grid_shape = (VIEWS, NR, COLS, HEADS * HD)
    keys_draw = jax.random.truncated_normal(jax.random.fold_in(key, 11), -6.0, 6.0, grid_shape, jnp.float32)
    query_draw = jax.random.truncated_normal(jax.random.fold_in(key, 12), -6.0, 6.0, grid_shape, jnp.float32)
    return (query_draw, keys_draw)


def draw_query_feats(key, part):
    return draw_pair(key)[0].astype(jnp.bfloat16)


def draw_key_feats(key, part):
    return draw_pair(key)[1].astype(jnp.bfloat16)


def draw_view_counts(key, part):
    position = jnp.arange(VIEWS, dtype=jnp.int32)
    lowest = VIEW_TOK // 3
    growth = (VIEW_TOK - lowest - VIEW_TOK // 8) * position // max(VIEWS - 1, 1)
    jitter = jax.random.randint(key, (VIEWS,), 0, VIEW_TOK // 8 + 1, jnp.int32)
    return jnp.minimum(lowest + growth + jitter, VIEW_TOK).astype(jnp.int32)


def plant(values, stream_key, low, high):
    spot = [jax.random.randint(jax.random.fold_in(stream_key, axis), (), 0, length) for axis, length in enumerate(values.shape)]
    widest = values.shape.index(max(values.shape))
    beside = spot[:widest] + [(spot[widest] + 1) % values.shape[widest]] + spot[widest + 1:]
    return values.at[tuple(spot)].set(low).at[tuple(beside)].set(high)


def block_levels(rng, dims, split, low, top_value):
    loudness, own = 1.0, jax.random.fold_in(rng, 6)
    for dim, shards_of in split:
        draws = jnp.exp(jax.random.uniform(jax.random.fold_in(own, dim), (shards_of,), jnp.float32, low / len(split), top_value / len(split)))
        loudness = loudness * jnp.repeat(draws, dims[dim] // shards_of).reshape([-1 if axis == dim else 1 for axis in range(len(dims))])
    return loudness


def noise(rng, dims, scale, reach, split=(), held_as=jnp.bfloat16):
    entries = scale * jax.random.normal(rng, dims, jnp.float32)
    if split:
        entries = entries * block_levels(rng, dims, split, -0.22, 0.18)
    return jnp.clip(entries, -reach, reach).astype(held_as)


def setup_inputs(seed: int = 0) -> dict:
    splits = jax.random.split(jax.random.key(seed), 11)
    return {
        "query_feats": draw_query_feats(jax.random.fold_in(splits[10], 71), 0),
        "key_feats": draw_key_feats(jax.random.fold_in(splits[10], 71), 0),
        "value_feats": noise(splits[2], (VIEWS, NR, COLS, HEADS * HD), 1.0, 6.0, ((0, 4), (1, 4), (3, 2))),
        "target": noise(splits[3], (VIEWS, NR, COLS, HEADS * HD), 1.0, 6.0, ((0, 4), (1, 4), (3, 2))),
        "token_rates": jnp.clip(jnp.exp(math.log(100.0) - 2.9957323 * jax.random.uniform(splits[4], (VIEWS, HEADS, NR * COLS), jnp.float32) ** block_levels(splits[4], (VIEWS, HEADS, NR * COLS), ((0, 4), (1, 2), (2, 4)), -0.2, 0.2)), 5.0, 100.0),
        "row_reach": plant(jax.random.randint(splits[5], (NR,), 1, 3), jax.random.fold_in(splits[5], 1), 1, 2).astype(jnp.int32),
        "view_counts": draw_view_counts(jax.random.fold_in(splits[10], 71), 0),
        "w_first": noise(splits[7], (HEADS, HD, HD), HD ** -0.5, 0.25, ((0, 2),)),
        "w_third": noise(splits[8], (HEADS, HD, HD), HD ** -0.5, 0.25, ((0, 2),)),
        "w_second": noise(splits[9], (HEADS, HD, HD), HD ** -0.5, 0.25, ((0, 2),)),
    }


def silu_slope(values_in):
    sigmoid_x = jax.nn.sigmoid(values_in)
    return sigmoid_x * (1.0 + values_in * (1.0 - sigmoid_x))

def attend(query_rows, key_rows, value_rows, q_row_ids, k_row_ids, q_tok, k_tok, k_valid, q_reach, grid_rows):
    count_q = query_rows.shape[0]
    count_k = key_rows.shape[0]
    groups = query_rows.shape[1] // ATT_HD
    query_heads = query_rows.reshape(count_q, groups, ATT_HD).astype(jnp.float32)
    key_heads = key_rows.reshape(count_k, groups, ATT_HD).astype(jnp.float32)
    value_heads = value_rows.reshape(count_k, groups, ATT_HD).astype(jnp.float32)
    scores = jnp.einsum('qhd,khd->hqk', query_heads, key_heads) / math.sqrt(ATT_HD)
    inside = (k_row_ids >= 0) & (k_row_ids < grid_rows)
    in_band = jnp.abs(k_row_ids[None, :] - q_row_ids[:, None]) <= q_reach[:, None]
    allowed = in_band & inside[None, :] & (k_valid[None, :] | (k_tok[None, :] == q_tok[:, None]))
    scores = jnp.where(allowed[None], scores, -1e+30)
    row_top = lax.optimization_barrier(jnp.max(scores, -1, keepdims=True))
    powers = jnp.exp(scores - row_top)
    weights = (powers / lax.optimization_barrier(jnp.sum(powers, -1, keepdims=True))).astype(jnp.bfloat16)
    output_rows = jnp.einsum('hqk,khd->qhd', weights.astype(jnp.float32), value_heads)
    return output_rows.reshape(count_q, groups * ATT_HD).astype(jnp.bfloat16)

def renorm(old_matrix, grad, total_valid):
    old_rows = old_matrix.astype(jnp.float32)
    raised = old_rows + grad / total_valid
    rescale = jnp.sqrt(lax.optimization_barrier(jnp.sum(old_rows * old_rows, -1, keepdims=True)) + 1e-06) / jnp.sqrt(lax.optimization_barrier(jnp.sum(raised * raised, -1, keepdims=True)) + 1e-06)
    return (raised * rescale).astype(jnp.bfloat16)

def reference(query_feats, key_feats, value_feats, target, token_rates, row_reach, view_counts, w_first, w_third, w_second):
    feat_width = HEADS * HD
    row_pad = ((0, 0), (HALO, HALO), (0, 0), (0, 0))
    key_pad = jnp.pad(key_feats, row_pad)
    value_pad = jnp.pad(value_feats, row_pad)
    blocks = NR // ROWS_DEV
    key_span = ROWS_DEV + 2 * HALO

    def attend_block(flat_index):
        view_index = (flat_index // blocks).astype(jnp.int32)
        row_start = (flat_index % blocks * ROWS_DEV).astype(jnp.int32)
        zero_index = jnp.zeros((), jnp.int32)
        q_blk = lax.dynamic_slice(query_feats, (view_index, row_start, zero_index, zero_index), (1, ROWS_DEV, COLS, feat_width))[0].reshape(ROWS_DEV * COLS, feat_width)
        k_blk = lax.dynamic_slice(key_pad, (view_index, row_start, zero_index, zero_index), (1, key_span, COLS, feat_width))[0].reshape(key_span * COLS, feat_width)
        v_blk = lax.dynamic_slice(value_pad, (view_index, row_start, zero_index, zero_index), (1, key_span, COLS, feat_width))[0].reshape(key_span * COLS, feat_width)
        q_row_ids = row_start + jnp.repeat(jnp.arange(ROWS_DEV, dtype=jnp.int32), COLS)
        k_row_ids = row_start - HALO + jnp.repeat(jnp.arange(key_span, dtype=jnp.int32), COLS)
        q_tok = q_row_ids * COLS + jnp.tile(jnp.arange(COLS, dtype=jnp.int32), ROWS_DEV)
        k_tok = k_row_ids * COLS + jnp.tile(jnp.arange(COLS, dtype=jnp.int32), key_span)
        view_total = view_counts[view_index]
        k_valid = k_tok < view_total
        q_reach = row_reach[q_row_ids]
        return attend(q_blk, k_blk, v_blk, q_row_ids, k_row_ids, q_tok, k_tok, k_valid, q_reach, NR)
    blocks_out = lax.map(attend_block, jnp.arange(VIEWS * blocks, dtype=jnp.int32))
    total_tok = VIEWS * NR * COLS
    attended = blocks_out.reshape(total_tok, HEADS, HD).astype(jnp.float32)
    fast_keys = (attended * lax.rsqrt(lax.optimization_barrier(jnp.mean(attended * attended, -1, keepdims=True)) + 1e-06)).astype(jnp.bfloat16)
    tok_index = jnp.arange(NR * COLS, dtype=jnp.int32)
    valid_mask = (tok_index[None, :] < view_counts[:, None]).reshape(total_tok).astype(jnp.float32)
    rates_tok = jnp.transpose(token_rates, (0, 2, 1)).reshape(total_tok, HEADS)
    scaled = (rates_tok[:, :, None] * valid_mask[:, None, None] * target.reshape(total_tok, HEADS, HD).astype(jnp.float32)).astype(jnp.bfloat16)
    total_valid = jnp.sum(view_counts).astype(jnp.float32)
    results = []
    for head in range(HEADS):
        key_rows = fast_keys[:, head]
        scaled_rows = scaled[:, head]
        first_proj = jnp.dot(key_rows, w_first[head], preferred_element_type=jnp.float32)
        third_proj = jnp.dot(key_rows, w_third[head], preferred_element_type=jnp.float32)
        gated_rows = (jax.nn.silu(first_proj) * third_proj).astype(jnp.bfloat16)
        back_rows = lax.dot_general(scaled_rows, w_second[head], (((1,), (1,)), ((), ())), preferred_element_type=jnp.float32)
        back_first = (back_rows * third_proj * silu_slope(first_proj)).astype(jnp.bfloat16)
        back_third = (back_rows * jax.nn.silu(first_proj)).astype(jnp.bfloat16)
        grad_first = jnp.dot(key_rows.T, back_first, preferred_element_type=jnp.float32)
        grad_third = jnp.dot(key_rows.T, back_third, preferred_element_type=jnp.float32)
        grad_second = jnp.dot(gated_rows.T, scaled_rows, preferred_element_type=jnp.float32)
        new_first = renorm(w_first[head], grad_first, total_valid)
        new_third = renorm(w_third[head], grad_third, total_valid)
        new_second = renorm(w_second[head], grad_second, total_valid)
        applied = (jax.nn.silu(jnp.dot(key_rows, new_first, preferred_element_type=jnp.float32)) * jnp.dot(key_rows, new_third, preferred_element_type=jnp.float32)).astype(jnp.bfloat16)
        results.append(jnp.dot(applied, new_second, preferred_element_type=jnp.float32).astype(jnp.bfloat16))
    return jnp.stack(results, 1).reshape(VIEWS, NR, COLS, HEADS * HD)
```

```python
import functools
import math

import jax
import jax.numpy as jnp
from jax import lax
from jax.experimental import pallas as pl
from jax.experimental.pallas import tpu as pltpu
from jax.sharding import PartitionSpec as P

HD = 512
ATT_HD = 128
HALO = 2
PER = 4
MESH = pl.DeviceIdType.MESH
BF16 = jnp.bfloat16
F32 = jnp.float32
NT = (((1,), (1,)), ((), ()))
TN = (((0,), (0,)), ((), ()))


def with_halo(value, sides, width):
    for axis, dim in sides:
        size, length = (lax.axis_size(axis), value.shape[dim])
        up = [(i, (i + 1) % size) for i in range(size - 1)]
        down = [(j, i) for i, j in up]
        last = lax.slice_in_dim(value, length - width, length, axis=dim)
        leading = lax.slice_in_dim(value, 0, width, axis=dim)
        before = lax.ppermute(last, axis, up)
        after = lax.ppermute(leading, axis, down)
        value = jnp.concatenate([before, value, after], axis=dim)
    return value


def silu_slope(values_in):
    sigmoid_x = jax.nn.sigmoid(values_in)
    return sigmoid_x * (1.0 + values_in * (1.0 - sigmoid_x))


def attend(
    query_rows,
    key_rows,
    value_rows,
    q_row_ids,
    k_row_ids,
    q_tok,
    k_tok,
    k_valid,
    q_reach,
    grid_rows,
):
    count_q = query_rows.shape[0]
    count_k = key_rows.shape[0]
    groups = query_rows.shape[1] // ATT_HD
    query_heads = query_rows.reshape(count_q, groups, ATT_HD)
    key_heads = key_rows.reshape(count_k, groups, ATT_HD)
    value_heads = value_rows.reshape(count_k, groups, ATT_HD)
    scores = jnp.einsum(
        "qhd,khd->hqk", query_heads, key_heads, preferred_element_type=jnp.float32
    ) / math.sqrt(ATT_HD)
    inside = (k_row_ids >= 0) & (k_row_ids < grid_rows)
    in_band = jnp.abs(k_row_ids[None, :] - q_row_ids[:, None]) <= q_reach[:, None]
    allowed = in_band & inside[None, :] & (k_valid[None, :] | (k_tok[None, :] == q_tok[:, None]))
    scores = jnp.where(allowed[None], scores, -1e30)
    row_top = jnp.max(scores, -1, keepdims=True)
    powers = jnp.exp(scores - row_top)
    weights = (powers / jnp.sum(powers, -1, keepdims=True)).astype(jnp.bfloat16)
    output_rows = jnp.einsum(
        "hqk,khd->qhd", weights, value_heads, preferred_element_type=jnp.float32
    )
    return output_rows.reshape(count_q, groups * ATT_HD).astype(jnp.bfloat16)


def renorm(old_matrix, grad, total_valid):
    old_rows = old_matrix.astype(jnp.float32)
    raised = old_rows + grad / total_valid
    rescale = jnp.sqrt(jnp.sum(old_rows * old_rows, -1, keepdims=True) + 1e-06) / jnp.sqrt(
        jnp.sum(raised * raised, -1, keepdims=True) + 1e-06
    )
    return (raised * rescale).astype(jnp.bfloat16)


def per_device(
    query_feats,
    key_feats,
    value_feats,
    target,
    token_rates,
    row_reach,
    view_counts,
    w_first,
    w_third,
    w_second,
):
    row_count = query_feats.shape[1]
    col_count = query_feats.shape[2]
    feat_width = query_feats.shape[3]
    heads_here = feat_width // HD
    tokens_here = row_count * col_count
    key_span = row_count + 2 * HALO
    grid_rows = lax.axis_size("row") * row_count
    row_base = lax.axis_index("row") * row_count
    view_total = view_counts[0]
    total_valid = lax.psum(view_total.astype(jnp.float32), "view")
    paired = jnp.stack([key_feats[0], value_feats[0]], 0)
    padded = with_halo(paired, (("row", 1),), HALO)
    q_row_ids = row_base + jnp.repeat(jnp.arange(row_count, dtype=jnp.int32), col_count)
    k_row_ids = row_base - HALO + jnp.repeat(jnp.arange(key_span, dtype=jnp.int32), col_count)
    q_tok = q_row_ids * col_count + jnp.tile(jnp.arange(col_count, dtype=jnp.int32), row_count)
    k_tok = k_row_ids * col_count + jnp.tile(jnp.arange(col_count, dtype=jnp.int32), key_span)
    k_valid = k_tok < view_total
    q_reach = jnp.repeat(row_reach, col_count)
    attended = attend(
        query_feats[0].reshape(tokens_here, feat_width),
        padded[0].reshape(key_span * col_count, feat_width),
        padded[1].reshape(key_span * col_count, feat_width),
        q_row_ids,
        k_row_ids,
        q_tok,
        k_tok,
        k_valid,
        q_reach,
        grid_rows,
    )
    attended = attended.reshape(tokens_here, heads_here, HD).astype(jnp.float32)
    fast_keys = (
        attended * lax.rsqrt(jnp.mean(attended * attended, -1, keepdims=True) + 1e-06)
    ).astype(jnp.bfloat16)
    valid_mask = (q_tok < view_total).astype(jnp.float32)
    rates_tok = token_rates[0].T
    scaled = (
        rates_tok[:, :, None]
        * valid_mask[:, None, None]
        * target[0].reshape(tokens_here, heads_here, HD).astype(jnp.float32)
    ).astype(jnp.bfloat16)
    first_proj = jnp.einsum("thi,hij->thj", fast_keys, w_first, preferred_element_type=jnp.float32)
    third_proj = jnp.einsum("thi,hij->thj", fast_keys, w_third, preferred_element_type=jnp.float32)
    gated_rows = (jax.nn.silu(first_proj) * third_proj).astype(jnp.bfloat16)
    back_rows = jnp.einsum("tho,hjo->thj", scaled, w_second, preferred_element_type=jnp.float32)
    back_first = (back_rows * third_proj * silu_slope(first_proj)).astype(jnp.bfloat16)
    back_third = (back_rows * jax.nn.silu(first_proj)).astype(jnp.bfloat16)
    grad_first = jnp.einsum(
        "thi,thj->hij", fast_keys, back_first, preferred_element_type=jnp.float32
    )
    grad_third = jnp.einsum(
        "thi,thj->hij", fast_keys, back_third, preferred_element_type=jnp.float32
    )
    grad_second = jnp.einsum("thj,tho->hjo", gated_rows, scaled, preferred_element_type=jnp.float32)
    grad_first, grad_third, grad_second = lax.psum(
        (grad_first, grad_third, grad_second), ("view", "row")
    )
    new_first = renorm(w_first, grad_first, total_valid)
    new_third = renorm(w_third, grad_third, total_valid)
    new_second = renorm(w_second, grad_second, total_valid)
    applied = (
        jax.nn.silu(
            jnp.einsum("thi,hij->thj", fast_keys, new_first, preferred_element_type=jnp.float32)
        )
        * jnp.einsum("thi,hij->thj", fast_keys, new_third, preferred_element_type=jnp.float32)
    ).astype(jnp.bfloat16)
    fast_out = jnp.einsum(
        "thj,hjo->tho", applied, new_second, preferred_element_type=jnp.float32
    ).astype(jnp.bfloat16)
    return fast_out.reshape(1, row_count, col_count, feat_width)


def halve(values_in, size):
    if size & (size - 1) == 0:
        return values_in >> (size.bit_length() - 1)
    return lax.div(values_in, jnp.int32(size))


def dot(left, right, dims=(((1,), (0,)), ((), ()))):
    return lax.dot_general(left, right, dims, preferred_element_type=F32)


def flip(index, bits):
    bit = 1
    while bit <= bits:
        if bits & bit:
            index = index + bit - 2 * bit * lax.rem(lax.div(index, bit), 2)
        bit *= 2
    return index


def step_kernel(
    nr, nz, cols,
    q_hbm, k_hbm, v_hbm, t_hbm, rates_hbm, reach_hbm, count_hbm, wf_hbm, wt_hbm, ws_hbm,
    out_ref,
    q_ref, kv_ref, t_ref, rates_ref, reach_ref, count_ref, wft, ws, halo, raw, sall, norms, cnt, gfull, gsum, gin, gtot,
    wold, wnew, ss, mixed, osend, orecv, load_sem, row_send, row_recv, k_recv, view_send, out_recv, total_recv,
):
    tokens, width = q_ref.shape
    rows_here = tokens // cols
    hid = width // nr
    edge = HALO * cols
    heads = width // ATT_HD
    pieces = total_recv.shape[0]
    piece = 3 * hid // pieces
    per = pieces // 3
    me = lax.axis_index("row")
    mz = lax.axis_index("view")
    mine = pl.ds(pl.multiple_of(me * hid, hid), hid)
    low = mz < nz // 2
    inner = jnp.where(low, mz + 1, mz - 1)
    outer = jnp.where(low, mz - 1, mz + 1)
    center = (mz > 0) & (mz < nz - 1)
    leaf = (mz == 0) | (mz == nz - 1)
    has_above = me < nr - 1
    has_below = me > 0

    barrier = pltpu.get_barrier_semaphore()
    for d in range(1, nr):
        pl.semaphore_signal(barrier, inc=1, device_id={"row": flip(me, d)}, device_id_type=MESH)
    pl.semaphore_signal(barrier, inc=1, device_id={"view": inner}, device_id_type=MESH)

    @pl.when(center)
    def _():
        pl.semaphore_signal(barrier, inc=1, device_id={"view": outer}, device_id_type=MESH)

    loads = [
        pltpu.make_async_copy(source, target, load_sem.at[i])
        for i, (source, target) in enumerate((
            (k_hbm, kv_ref.at[0]), (v_hbm, kv_ref.at[1]), (count_hbm, count_ref), (reach_hbm, reach_ref),
            (t_hbm, t_ref), (rates_hbm, rates_ref), (q_hbm, q_ref),
            (wf_hbm.at[:, mine], wft.at[:, pl.ds(0, hid)]), (wt_hbm.at[:, mine], wft.at[:, pl.ds(hid, hid)]),
            (ws_hbm.at[mine, :], ws),
        ))
    ]
    for load in loads:
        load.start()

    def remote(source, target, sends, receives, axis, peer):
        return pltpu.make_async_remote_copy(
            src_ref=source, dst_ref=target, send_sem=sends, recv_sem=receives,
            device_id={axis: peer}, device_id_type=MESH,
        )

    partner, across = flip(me, 1), flip(me, 2)
    above, below = me + 1, me - 1

    @pl.when(me == 0)
    def _():
        halo[:, :edge] = jnp.zeros((2, edge, width), BF16)

    @pl.when(me == nr - 1)
    def _():
        halo[:, edge:] = jnp.zeros((2, edge, width), BF16)

    row_base = me * rows_here
    tok_base = me * tokens
    for load in loads[2:4]:
        load.wait()
    view_total = count_ref[0]
    cnt[0] = jnp.full((8, 128), view_total, jnp.int32).astype(F32)
    sub = lax.broadcasted_iota(jnp.int32, (tokens, tokens), 0)
    lane = lax.broadcasted_iota(jnp.int32, (tokens, tokens), 1)
    tok_col = tok_base + lax.broadcasted_iota(jnp.int32, (tokens, 1), 0)
    valid_col = (tok_col < view_total).astype(F32)
    for load in loads[4:6]:
        load.wait()
    rate_col = jnp.sum(jnp.where(sub == lane, rates_ref[...], 0.0), axis=1, keepdims=True)
    sall[0] = (rate_col * valid_col * t_ref[...].astype(F32)).astype(BF16)
    for load in loads[:2]:
        load.wait()

    pl.semaphore_wait(barrier, nr + jnp.where(center, 1, 0))

    up_halo = remote(kv_ref.at[:, pl.ds(tokens - edge, edge)], halo.at[:, pl.ds(0, edge)], row_send.at[0], row_recv.at[0], "row", above)
    down_halo = remote(kv_ref.at[:, pl.ds(0, edge)], halo.at[:, pl.ds(edge, edge)], row_send.at[1], row_recv.at[1], "row", below)

    @pl.when(has_above)
    def _():
        up_halo.start()

    @pl.when(has_below)
    def _():
        down_halo.start()

    s_near = remote(sall.at[0], sall.at[1], row_send.at[2], row_recv.at[2], "row", partner)
    s_far = remote(sall.at[0], sall.at[2], row_send.at[2], row_recv.at[3], "row", across)
    s_on = remote(sall.at[2], sall.at[3], row_send.at[2], row_recv.at[4], "row", partner)
    s_near.start()
    s_far.start()
    cnt_up = remote(cnt.at[0], cnt.at[1], view_send.at[0], row_recv.at[8], "view", inner)
    cnt_mid = remote(cnt.at[2], cnt.at[3], view_send.at[0], row_recv.at[9], "view", inner)
    cnt_down = remote(cnt.at[3], cnt.at[3], view_send.at[1], row_recv.at[9], "view", outer)

    @pl.when(leaf)
    def _():
        cnt_up.start()

    def allowed(q_tok, k_tok):
        q_row = halve(q_tok, cols)
        k_row = halve(k_tok + edge, cols) - HALO
        reach = jnp.zeros(q_tok.shape, jnp.int32)
        for r in range(rows_here):
            reach = jnp.where(q_row == r, reach_ref[r], reach)
        k_abs = k_row + row_base
        return (
            (jnp.abs(k_row - q_row) <= reach)
            & (k_abs >= 0)
            & (k_abs < nr * rows_here)
            & ((k_tok + tok_base < view_total) | (k_tok == q_tok))
        )

    near_ok = allowed(sub, lane)
    far_q = lax.broadcasted_iota(jnp.int32, (tokens, 2 * edge), 0)
    far_k = lax.broadcasted_iota(jnp.int32, (tokens, 2 * edge), 1)
    far_ok = allowed(far_q, jnp.where(far_k < edge, far_k - edge, far_k - edge + tokens))
    root = 1.0 / math.sqrt(ATT_HD)
    spans = [slice(h * ATT_HD, (h + 1) * ATT_HD) for h in range(heads)]
    loads[6].wait()
    near = []
    for hs in spans:
        scores = jnp.where(near_ok, dot(q_ref[:, hs], kv_ref[0, :, hs], NT) * root, -1e30)
        top = jnp.max(scores, axis=-1, keepdims=True)
        power = jnp.exp(scores - top)
        near.append((top, jnp.sum(power, axis=-1, keepdims=True), dot(power.astype(BF16), kv_ref[1, :, hs])))
    for load in loads[7:]:
        load.wait()
    wold[0:hid] = wft[:, :hid].astype(F32).T
    wold[hid:2 * hid] = wft[:, hid:].astype(F32).T
    wold[2 * hid:] = ws[...].astype(F32)

    @pl.when(has_below)
    def _():
        up_halo.wait_recv()

    @pl.when(has_above)
    def _():
        down_halo.wait_recv()

    k_near, k_far, k_on = [], [], []
    for h, hs in enumerate(spans):
        near_top, near_sum, near_out = near[h]
        far = jnp.where(far_ok, dot(q_ref[:, hs], halo[0, :, hs], NT) * root, -1e30)
        top = jnp.maximum(near_top, jnp.max(far, axis=-1, keepdims=True))
        power = jnp.exp(far - top)
        keep = jnp.exp(near_top - top)
        inverse = 1.0 / (keep * near_sum + jnp.sum(power, axis=-1, keepdims=True))
        mix = keep * near_out + dot(power.astype(BF16), halo[1, :, hs])
        raw[0, h] = (mix * inverse).astype(BF16)
        k_near.append(remote(raw.at[0, h], raw.at[1, h], row_send.at[3], k_recv.at[0, h], "row", partner))
        k_far.append(remote(raw.at[0, h], raw.at[2, h], row_send.at[3], k_recv.at[1, h], "row", across))
        k_on.append(remote(raw.at[2, h], raw.at[3, h], row_send.at[3], k_recv.at[2, h], "row", partner))
        k_far[h].start()
        k_near[h].start()

    def block(d):
        keys = jnp.concatenate([raw[d, h] for h in range(heads)], axis=1)
        both = dot(keys, wft[...])
        back = dot(sall[d], ws[...], NT)
        total_sq = jnp.zeros((tokens, ATT_HD), F32)
        for h in range(heads):
            part = raw[d, h].astype(F32)
            total_sq = total_sq + part * part
        norm = lax.rsqrt(jnp.sum(total_sq, axis=-1, keepdims=True) * (1.0 / width) + 1e-06)
        norms[d] = jnp.broadcast_to(norm, (tokens, 128))
        first = both[:, :hid] * norm
        third = both[:, hid:] * norm
        sig = jax.nn.sigmoid(first)
        gate = first * sig
        pulled = back * norm
        left = jnp.concatenate(
            [
                (pulled * third * (sig * (1.0 + first * (1.0 - sig)))).astype(BF16),
                (pulled * gate).astype(BF16),
            ],
            axis=1,
        )
        return left, keys, (gate * third).astype(BF16)

    def grads(d, first_block):
        left, keys, gated = block(d)
        grad = dot(left, keys, TN)
        gfull[: 2 * hid] = grad if first_block else gfull[: 2 * hid] + grad
        grad = dot(gated, sall[d], TN)
        gfull[2 * hid:] = grad if first_block else gfull[2 * hid:] + grad

    grads(0, True)
    s_near.wait_recv()
    for copy in k_near:
        copy.wait_recv()
    grads(1, False)

    @pl.when(center)
    def _():
        cnt_up.wait_recv()
        cnt[2] = cnt[0] + cnt[1]
        cnt_mid.start()

    s_far.wait_recv()
    s_on.start()
    for h in range(heads):
        k_far[h].wait_recv()
        k_on[h].start()
    grads(2, False)

    @pl.when(center)
    def _():
        cnt_mid.wait_recv()
        cnt[3] = cnt[2] + cnt[3]
        cnt_down.start()

    s_on.wait_recv()
    for copy in k_on:
        copy.wait_recv()

    def rows(i):
        return pl.ds(i * piece, piece)

    def rise(i, target, receives):
        return remote(gsum.at[rows(i)], target.at[rows(i)], view_send.at[2], receives.at[i], "view", inner)

    def fall(i):
        return remote(gtot.at[rows(i)], gtot.at[rows(i)], view_send.at[3], total_recv.at[i], "view", outer)

    left, keys, gated = block(3)
    grad = gfull[: 2 * hid] + dot(left, keys, TN)
    gfull[: 2 * hid] = grad

    @pl.when(leaf)
    def _():
        for i in range(2 * per):
            gsum[rows(i)] = gfull[rows(i)].astype(BF16)
            rise(i, gin, out_recv).start()

    grad = gfull[2 * hid:] + dot(gated, sall[3], TN)
    gfull[2 * hid:] = grad

    @pl.when(leaf)
    def _():
        for i in range(2 * per, 3 * per):
            gsum[rows(i)] = gfull[rows(i)].astype(BF16)
            rise(i, gin, out_recv).start()
        cnt_down.wait_recv()

    ss[0, 2:3] = jnp.sum(wold[:hid] * wold[:hid], axis=0, keepdims=True)
    ss[0, 3:4] = jnp.sum(wold[hid:2 * hid] * wold[hid:2 * hid], axis=0, keepdims=True)
    second_old = wold[2 * hid:]
    second_size = jnp.sqrt(jnp.sum(second_old * second_old, axis=-1, keepdims=True) + 1e-06)
    share_total = 1.0 / cnt[3, 0:1, 0:1]

    def join(i):
        rise(i, gin, out_recv).wait_recv()
        gsum[rows(i)] = (gfull[rows(i)] + gin[rows(i)].astype(F32)).astype(BF16)
        rise(i, gtot, total_recv).start()

    def finish(i):
        rise(i, gtot, total_recv).wait_recv()
        gtot[rows(i)] = (gsum[rows(i)].astype(F32) + gtot[rows(i)].astype(F32)).astype(BF16)
        fall(i).start()

    lag = 3

    @pl.when(center)
    def _():
        for i in range(lag):
            join(i)

    def arrive(i):
        @pl.when(center)
        def _():
            if i + lag < pieces:
                join(i + lag)
            finish(i)

    def land(i):
        @pl.when(leaf)
        def _():
            fall(i).wait_recv()

    def raise_rows(i):
        raised = wold[rows(i)] + gtot[rows(i)].astype(F32) * share_total
        if i < 2 * per:
            wnew[rows(i)] = raised
            return jnp.sum(raised * raised, axis=0, keepdims=True)
        at = (i - 2 * per) * piece
        size = jnp.sqrt(jnp.sum(raised * raised, axis=-1, keepdims=True) + 1e-06)
        ws[at:at + piece] = (raised * (second_size[at:at + piece] / size)).astype(BF16)

    ss_copies = [
        remote(ss.at[0], ss.at[d], row_send.at[3 + d], row_recv.at[4 + d], "row", flip(me, d)) for d in range(1, nr)
    ]
    for i in range(pieces):
        arrive(i)
        if i == pieces - 1:
            break
        land(i)
        square = raise_rows(i)
        if i < 2 * per:
            running = square if i % per == 0 else running + square
            if i % per == per - 1:
                m = i // per
                ss[0, m:m + 1] = running
                if m == 1:
                    for copy in ss_copies:
                        copy.start()
    for copy in ss_copies:
        copy.wait_recv()
    sums = ss[0]
    for d in range(1, nr):
        sums = sums + ss[d]
    scales = jnp.sqrt(sums[2:4] + 1e-06) / jnp.sqrt(sums[0:2] + 1e-06)
    mixed[:hid] = (wnew[:hid] * scales[0:1]).astype(BF16)
    mixed[hid:] = (wnew[hid:] * scales[1:2]).astype(BF16)
    order = list(range(3, nr, 2)) + list(range(2, nr, 2)) + [1, 0]
    applied = {}
    for d in order:
        keys = jnp.concatenate([raw[d, h] for h in range(heads)], axis=1)
        both = dot(keys, mixed[...], NT)
        first = both[:, :hid] * norms[d][:, 0:1]
        third = both[:, hid:] * norms[d][:, 0:1]
        applied[d] = (first * jax.nn.sigmoid(first) * third).astype(BF16)
    land(pieces - 1)
    raise_rows(pieces - 1)

    def leave(d, peer):
        return remote(osend.at[d - 1], orecv.at[d - 1], row_send.at[nr + 3], row_recv.at[9 + d], "row", peer)

    o_copies = {1: leave(1, partner), 2: leave(2, across), 3: leave(3, partner)}
    for d in order:
        total = dot(applied[d], ws[...])
        if d == 0:
            continue
        if d % 2 == 0:
            o_copies[d + 1].wait_recv()
            total = total + orecv[d].astype(F32)
        osend[d - 1] = total.astype(BF16)
        o_copies[d].start()
    for d in [1] + list(range(2, nr, 2)):
        o_copies[d].wait_recv()
        total = total + orecv[d - 1].astype(F32)
    out_ref[...] = total.astype(BF16)

    @pl.when(has_above)
    def _():
        up_halo.wait_send()

    @pl.when(has_below)
    def _():
        down_halo.wait_send()

    remote(sall.at[pl.ds(0, nr - 1)], sall.at[pl.ds(0, nr - 1)], row_send.at[2], row_recv.at[2], "row", partner).wait_send()
    remote(raw.at[pl.ds(0, nr - 1)], raw.at[pl.ds(0, nr - 1)], row_send.at[3], row_recv.at[2], "row", partner).wait_send()
    remote(osend, orecv, row_send.at[nr + 3], row_recv.at[2], "row", partner).wait_send()
    for copy in ss_copies:
        copy.wait_send()
    remote(gsum, gin, view_send.at[2], row_recv.at[2], "view", inner).wait_send()
    cnt_up.wait_send()

    @pl.when(center)
    def _():
        cnt_down.wait_send()
        remote(gtot, gtot, view_send.at[3], row_recv.at[2], "view", outer).wait_send()


def fused_step(
    nr, nz,
    query_feats, key_feats, value_feats, target, token_rates, row_reach, view_counts,
    w_first, w_third, w_second,
):
    _, row_count, cols, width = query_feats.shape
    tokens = row_count * cols
    hid = width // nr
    edge = HALO * cols
    heads = width // ATT_HD
    pieces = 3 * PER
    anywhere = pl.BlockSpec(memory_space=pl.ANY)
    flat = lambda a: a.reshape(tokens, width)
    out = pl.pallas_call(
        functools.partial(step_kernel, nr, nz, cols),
        out_shape=pltpu.VMEM((tokens, width), BF16),
        in_specs=[anywhere] * 5 + [pl.BlockSpec(memory_space=pltpu.HBM)] * 2 + [anywhere] * 3,
        out_specs=pl.BlockSpec(memory_space=pltpu.VMEM),
        scratch_shapes=[
            pltpu.VMEM((tokens, width), BF16),
            pltpu.VMEM((2, tokens, width), BF16),
            pltpu.VMEM((tokens, width), BF16),
            pltpu.VMEM((1, tokens), F32),
            pltpu.SMEM((row_count,), jnp.int32),
            pltpu.SMEM((1,), jnp.int32),
            pltpu.VMEM((width, 2 * hid), BF16),
            pltpu.VMEM((hid, width), BF16),
            pltpu.VMEM((2, 2 * edge, width), BF16),
            pltpu.VMEM((nr, heads, tokens, ATT_HD), BF16),
            pltpu.VMEM((nr, tokens, width), BF16),
            pltpu.VMEM((nr, tokens, 128), F32),
            pltpu.VMEM((4, 8, 128), F32),
            pltpu.VMEM((3 * hid, width), F32),
            pltpu.VMEM((3 * hid, width), BF16),
            pltpu.VMEM((3 * hid, width), BF16),
            pltpu.VMEM((3 * hid, width), BF16),
            pltpu.VMEM((3 * hid, width), F32),
            pltpu.VMEM((2 * hid, width), F32),
            pltpu.VMEM((nr, 4, width), F32),
            pltpu.VMEM((2 * hid, width), BF16),
            pltpu.VMEM((nr - 1, tokens, width), BF16),
            pltpu.VMEM((nr - 1, tokens, width), BF16),
            pltpu.SemaphoreType.DMA((10,)),
            pltpu.SemaphoreType.DMA((4 + nr,)),
            pltpu.SemaphoreType.DMA((9 + nr,)),
            pltpu.SemaphoreType.DMA((nr - 1, heads)),
            pltpu.SemaphoreType.DMA((4,)),
            pltpu.SemaphoreType.DMA((pieces,)),
            pltpu.SemaphoreType.DMA((pieces,)),
        ],
        compiler_params=pltpu.CompilerParams(collective_id=0, has_side_effects=True),
    )(
        flat(query_feats), flat(key_feats), flat(value_feats), flat(target),
        token_rates.reshape(1, tokens), row_reach, view_counts,
        w_first.reshape(width, width), w_third.reshape(width, width), w_second.reshape(width, width),
    )
    return out.reshape(query_feats.shape)


def solution(mesh):
    placed = (
        P("view", "row", None, "head"),
        P("view", "row", None, "head"),
        P("view", "row", None, "head"),
        P("view", "row", None, "head"),
        P("view", "head", "row"),
        P("row"),
        P("view"),
        P("head", None, None),
        P("head", None, None),
        P("head", None, None),
    )
    nr, nz = mesh.shape["row"], mesh.shape["view"]
    fits = nr == 4 and nz == 4 and HD % (128 * nr) == 0 and HD % (16 * nr * PER) == 0
    return jax.shard_map(
        functools.partial(fused_step, nr, nz) if fits else per_device,
        mesh=mesh,
        in_specs=placed,
        out_specs=P("view", "row", None, "head"),
        check_vma=False,
    )
```

```python
import functools
import math

import jax
import jax.numpy as jnp
from jax import lax
from jax.experimental import pallas as pl
from jax.experimental.pallas import tpu as pltpu
from jax.sharding import PartitionSpec as P

HD = 512
ATT_HD = 128
HALO = 2
PER = 8
LAGS = (9, 8)
LEADS = (24, 24)
HOLD = 20
MESH = pl.DeviceIdType.MESH
BF16 = jnp.bfloat16
F32 = jnp.float32
NT = (((1,), (1,)), ((), ()))
TN = (((0,), (0,)), ((), ()))


def with_halo(value, sides, width):
    for axis, dim in sides:
        size, length = (lax.axis_size(axis), value.shape[dim])
        up = [(i, (i + 1) % size) for i in range(size - 1)]
        down = [(j, i) for i, j in up]
        last = lax.slice_in_dim(value, length - width, length, axis=dim)
        leading = lax.slice_in_dim(value, 0, width, axis=dim)
        before = lax.ppermute(last, axis, up)
        after = lax.ppermute(leading, axis, down)
        value = jnp.concatenate([before, value, after], axis=dim)
    return value


def silu_slope(values_in):
    sigmoid_x = jax.nn.sigmoid(values_in)
    return sigmoid_x * (1.0 + values_in * (1.0 - sigmoid_x))


def attend(
    query_rows,
    key_rows,
    value_rows,
    q_row_ids,
    k_row_ids,
    q_tok,
    k_tok,
    k_valid,
    q_reach,
    grid_rows,
):
    count_q = query_rows.shape[0]
    count_k = key_rows.shape[0]
    groups = query_rows.shape[1] // ATT_HD
    query_heads = query_rows.reshape(count_q, groups, ATT_HD)
    key_heads = key_rows.reshape(count_k, groups, ATT_HD)
    value_heads = value_rows.reshape(count_k, groups, ATT_HD)
    scores = jnp.einsum(
        "qhd,khd->hqk", query_heads, key_heads, preferred_element_type=jnp.float32
    ) / math.sqrt(ATT_HD)
    inside = (k_row_ids >= 0) & (k_row_ids < grid_rows)
    in_band = jnp.abs(k_row_ids[None, :] - q_row_ids[:, None]) <= q_reach[:, None]
    allowed = in_band & inside[None, :] & (k_valid[None, :] | (k_tok[None, :] == q_tok[:, None]))
    scores = jnp.where(allowed[None], scores, -1e30)
    row_top = jnp.max(scores, -1, keepdims=True)
    powers = jnp.exp(scores - row_top)
    weights = (powers / jnp.sum(powers, -1, keepdims=True)).astype(jnp.bfloat16)
    output_rows = jnp.einsum(
        "hqk,khd->qhd", weights, value_heads, preferred_element_type=jnp.float32
    )
    return output_rows.reshape(count_q, groups * ATT_HD).astype(jnp.bfloat16)


def renorm(old_matrix, grad, total_valid):
    old_rows = old_matrix.astype(jnp.float32)
    raised = old_rows + grad / total_valid
    rescale = jnp.sqrt(jnp.sum(old_rows * old_rows, -1, keepdims=True) + 1e-06) / jnp.sqrt(
        jnp.sum(raised * raised, -1, keepdims=True) + 1e-06
    )
    return (raised * rescale).astype(jnp.bfloat16)


def per_device(
    query_feats,
    key_feats,
    value_feats,
    target,
    token_rates,
    row_reach,
    view_counts,
    w_first,
    w_third,
    w_second,
):
    row_count = query_feats.shape[1]
    col_count = query_feats.shape[2]
    feat_width = query_feats.shape[3]
    heads_here = feat_width // HD
    tokens_here = row_count * col_count
    key_span = row_count + 2 * HALO
    grid_rows = lax.axis_size("row") * row_count
    row_base = lax.axis_index("row") * row_count
    view_total = view_counts[0]
    total_valid = lax.psum(view_total.astype(jnp.float32), "view")
    paired = jnp.stack([key_feats[0], value_feats[0]], 0)
    padded = with_halo(paired, (("row", 1),), HALO)
    q_row_ids = row_base + jnp.repeat(jnp.arange(row_count, dtype=jnp.int32), col_count)
    k_row_ids = row_base - HALO + jnp.repeat(jnp.arange(key_span, dtype=jnp.int32), col_count)
    q_tok = q_row_ids * col_count + jnp.tile(jnp.arange(col_count, dtype=jnp.int32), row_count)
    k_tok = k_row_ids * col_count + jnp.tile(jnp.arange(col_count, dtype=jnp.int32), key_span)
    k_valid = k_tok < view_total
    q_reach = jnp.repeat(row_reach, col_count)
    attended = attend(
        query_feats[0].reshape(tokens_here, feat_width),
        padded[0].reshape(key_span * col_count, feat_width),
        padded[1].reshape(key_span * col_count, feat_width),
        q_row_ids,
        k_row_ids,
        q_tok,
        k_tok,
        k_valid,
        q_reach,
        grid_rows,
    )
    attended = attended.reshape(tokens_here, heads_here, HD).astype(jnp.float32)
    fast_keys = (
        attended * lax.rsqrt(jnp.mean(attended * attended, -1, keepdims=True) + 1e-06)
    ).astype(jnp.bfloat16)
    valid_mask = (q_tok < view_total).astype(jnp.float32)
    rates_tok = token_rates[0].T
    scaled = (
        rates_tok[:, :, None]
        * valid_mask[:, None, None]
        * target[0].reshape(tokens_here, heads_here, HD).astype(jnp.float32)
    ).astype(jnp.bfloat16)
    first_proj = jnp.einsum("thi,hij->thj", fast_keys, w_first, preferred_element_type=jnp.float32)
    third_proj = jnp.einsum("thi,hij->thj", fast_keys, w_third, preferred_element_type=jnp.float32)
    gated_rows = (jax.nn.silu(first_proj) * third_proj).astype(jnp.bfloat16)
    back_rows = jnp.einsum("tho,hjo->thj", scaled, w_second, preferred_element_type=jnp.float32)
    back_first = (back_rows * third_proj * silu_slope(first_proj)).astype(jnp.bfloat16)
    back_third = (back_rows * jax.nn.silu(first_proj)).astype(jnp.bfloat16)
    grad_first = jnp.einsum(
        "thi,thj->hij", fast_keys, back_first, preferred_element_type=jnp.float32
    )
    grad_third = jnp.einsum(
        "thi,thj->hij", fast_keys, back_third, preferred_element_type=jnp.float32
    )
    grad_second = jnp.einsum("thj,tho->hjo", gated_rows, scaled, preferred_element_type=jnp.float32)
    grad_first, grad_third, grad_second = lax.psum(
        (grad_first, grad_third, grad_second), ("view", "row")
    )
    new_first = renorm(w_first, grad_first, total_valid)
    new_third = renorm(w_third, grad_third, total_valid)
    new_second = renorm(w_second, grad_second, total_valid)
    applied = (
        jax.nn.silu(
            jnp.einsum("thi,hij->thj", fast_keys, new_first, preferred_element_type=jnp.float32)
        )
        * jnp.einsum("thi,hij->thj", fast_keys, new_third, preferred_element_type=jnp.float32)
    ).astype(jnp.bfloat16)
    fast_out = jnp.einsum(
        "thj,hjo->tho", applied, new_second, preferred_element_type=jnp.float32
    ).astype(jnp.bfloat16)
    return fast_out.reshape(1, row_count, col_count, feat_width)


def halve(values_in, size):
    if size & (size - 1) == 0:
        return values_in >> (size.bit_length() - 1)
    return lax.div(values_in, jnp.int32(size))


def dot(left, right, dims=(((1,), (0,)), ((), ()))):
    return lax.dot_general(left, right, dims, preferred_element_type=F32)


def flip(index, bits):
    bit = 1
    while bit <= bits:
        if bits & bit:
            index = index + bit - 2 * bit * lax.rem(lax.div(index, bit), 2)
        bit *= 2
    return index


def step_kernel(
    nr, nz, cols,
    q_hbm, k_hbm, v_hbm, t_hbm, rates_hbm, reach_hbm, count_hbm, wf_hbm, wt_hbm, ws_hbm,
    out_ref,
    q_ref, kv_ref, t_ref, rates_ref, reach_ref, count_ref, wft, ws, halo, raw, sall, cnt, gout, gside, gfull, gsum, gin, gtot,
    wold, news, ss,
    load_sem, row_send, row_recv, k_recv, view_send, side_recv, out_recv, total_recv, near_recv, far_recv, on_recv,
):
    tokens, width = q_ref.shape
    rows_here = tokens // cols
    hid = width // nr
    edge = HALO * cols
    heads = width // ATT_HD
    pieces = total_recv.shape[0]
    piece = 3 * hid // pieces
    per = pieces // 3
    me = lax.axis_index("row")
    mz = lax.axis_index("view")
    partner, across = flip(me, 1), flip(me, 2)
    above, below = me + 1, me - 1
    mine = pl.ds(pl.multiple_of(me * hid, hid), hid)
    theirs = pl.ds(pl.multiple_of(across * hid, hid), hid)
    low = mz < nz // 2
    inner = jnp.where(low, mz + 1, mz - 1)
    outer = jnp.where(low, mz - 1, mz + 1)
    center = (mz > 0) & (mz < nz - 1)
    leaf = (mz == 0) | (mz == nz - 1)
    has_above = me < nr - 1
    has_below = me > 0

    barrier = pltpu.get_barrier_semaphore()
    for d in range(1, nr):
        pl.semaphore_signal(barrier, inc=1, device_id={"row": flip(me, d)}, device_id_type=MESH)
    pl.semaphore_signal(barrier, inc=1, device_id={"view": inner}, device_id_type=MESH)

    @pl.when(center)
    def _():
        pl.semaphore_signal(barrier, inc=1, device_id={"view": outer}, device_id_type=MESH)

    loads = [
        pltpu.make_async_copy(source, target, load_sem.at[min(i, 7) if i < 11 else 8])
        for i, (source, target) in enumerate((
            (k_hbm, kv_ref.at[0]), (v_hbm, kv_ref.at[1]), (count_hbm, count_ref), (reach_hbm, reach_ref),
            (t_hbm, t_ref), (rates_hbm, rates_ref), (q_hbm, q_ref),
            (wf_hbm.at[:, theirs], wft.at[:, pl.ds(0, hid)]), (wt_hbm.at[:, theirs], wft.at[:, pl.ds(hid, hid)]),
            (wf_hbm.at[:, mine], wft.at[:, pl.ds(2 * hid, hid)]), (wt_hbm.at[:, mine], wft.at[:, pl.ds(3 * hid, hid)]),
            (ws_hbm.at[theirs, :], ws.at[pl.ds(0, hid)]), (ws_hbm.at[mine, :], ws.at[pl.ds(hid, hid)]),
        ))
    ]
    for load in loads:
        load.start()

    def remote(source, target, sends, receives, axis, peer):
        return pltpu.make_async_remote_copy(
            src_ref=source, dst_ref=target, send_sem=sends, recv_sem=receives,
            device_id={axis: peer}, device_id_type=MESH,
        )

    @pl.when(me == 0)
    def _():
        halo[:, :edge] = jnp.zeros((2, edge, width), BF16)

    @pl.when(me == nr - 1)
    def _():
        halo[:, edge:] = jnp.zeros((2, edge, width), BF16)

    row_base = me * rows_here
    tok_base = me * tokens

    pl.semaphore_wait(barrier, nr + jnp.where(center, 1, 0))

    @pl.when(has_above)
    def _():
        for i, source in enumerate((k_hbm, v_hbm)):
            remote(
                source.at[pl.ds(tokens - edge, edge)], halo.at[i, pl.ds(0, edge)], row_send.at[0], row_recv.at[0], "row", above
            ).start()

    @pl.when(has_below)
    def _():
        for i, source in enumerate((k_hbm, v_hbm)):
            remote(
                source.at[pl.ds(0, edge)], halo.at[i, pl.ds(edge, edge)], row_send.at[1], row_recv.at[1], "row", below
            ).start()

    up_halo = remote(halo.at[:, pl.ds(edge, edge)], halo.at[:, pl.ds(0, edge)], row_send.at[0], row_recv.at[0], "row", above)
    down_halo = remote(halo.at[:, pl.ds(0, edge)], halo.at[:, pl.ds(edge, edge)], row_send.at[1], row_recv.at[1], "row", below)

    for load in loads[2:4]:
        load.wait()
    view_total = count_ref[0]
    cnt[0] = jnp.full((8, 128), view_total, jnp.int32).astype(F32)
    sub = lax.broadcasted_iota(jnp.int32, (tokens, tokens), 0)
    lane = lax.broadcasted_iota(jnp.int32, (tokens, tokens), 1)
    tok_col = tok_base + lax.broadcasted_iota(jnp.int32, (tokens, 1), 0)
    valid_col = (tok_col < view_total).astype(F32)
    for load in loads[4:6]:
        load.wait()
    rate_col = jnp.sum(jnp.where(sub == lane, rates_ref[...], 0.0), axis=1, keepdims=True)
    sall[0] = (rate_col * valid_col * t_ref[...].astype(F32)).astype(BF16)
    s_near = remote(sall.at[0], sall.at[1], row_send.at[2], row_recv.at[2], "row", partner)
    s_near.start()
    cnt_up = remote(cnt.at[0], cnt.at[1], view_send.at[0], row_recv.at[3], "view", inner)
    cnt_mid = remote(cnt.at[2], cnt.at[3], view_send.at[0], row_recv.at[4], "view", inner)
    cnt_down = remote(cnt.at[3], cnt.at[3], view_send.at[1], row_recv.at[4], "view", outer)

    @pl.when(leaf)
    def _():
        cnt_up.start()

    def allowed(q_tok, k_tok):
        q_row = halve(q_tok, cols)
        k_row = halve(k_tok + edge, cols) - HALO
        reach = jnp.zeros(q_tok.shape, jnp.int32)
        for r in range(rows_here):
            reach = jnp.where(q_row == r, reach_ref[r], reach)
        k_abs = k_row + row_base
        return (
            (jnp.abs(k_row - q_row) <= reach)
            & (k_abs >= 0)
            & (k_abs < nr * rows_here)
            & ((k_tok + tok_base < view_total) | (k_tok == q_tok))
        )

    near_ok = allowed(sub, lane)
    far_q = lax.broadcasted_iota(jnp.int32, (2 * edge, 2 * edge), 0)
    far_k = lax.broadcasted_iota(jnp.int32, (2 * edge, 2 * edge), 1)
    far_ok = allowed(
        jnp.where(far_q < edge, far_q, far_q - 2 * edge + tokens),
        jnp.where(far_k < edge, far_k - edge, far_k - edge + tokens),
    )
    root = 1.0 / math.sqrt(ATT_HD)
    spans = [slice(h * ATT_HD, (h + 1) * ATT_HD) for h in range(heads)]
    for load in loads[:2] + loads[6:7]:
        load.wait()
    inside = slice(edge, tokens - edge)
    ends = (slice(0, edge), slice(tokens - edge, tokens))

    def outer_rows(value):
        return jnp.concatenate([value[e] for e in ends], axis=0)

    def pass_keys(at, receives):
        return remote(raw.at[0, :, at], raw.at[1, :, at], row_send.at[3], receives, "row", partner)

    near = []
    for h, hs in enumerate(spans):
        scores = jnp.where(near_ok, dot(q_ref[:, hs], kv_ref[0, :, hs], NT) * root, -1e30)
        top = jnp.max(scores, axis=-1, keepdims=True)
        power = jnp.exp(scores - top)
        total = jnp.sum(power, axis=-1, keepdims=True)
        mix = dot(power.astype(BF16), kv_ref[1, :, hs])
        raw[0, h, inside] = (mix[inside] * (1.0 / total[inside])).astype(BF16)
        near.append((outer_rows(top), outer_rows(total), outer_rows(mix), outer_rows(q_ref.at[:, hs])))
    middle = pass_keys(pl.ds(edge, tokens - 2 * edge), k_recv.at[0])
    middle.start()
    pltpu.make_async_copy(wft, wft, load_sem.at[7]).wait()
    pltpu.make_async_copy(ws, ws, load_sem.at[8]).wait()
    wold[0:hid] = wft[:, 2 * hid:3 * hid].astype(F32).T
    wold[hid:2 * hid] = wft[:, 3 * hid:].astype(F32).T
    wold[2 * hid:] = ws[hid:].astype(F32)

    @pl.when(has_below)
    def _():
        up_halo.wait_recv()

    @pl.when(has_above)
    def _():
        down_halo.wait_recv()

    for h, hs in enumerate(spans):
        near_top, near_sum, near_out, queries = near[h]
        far = jnp.where(far_ok, dot(queries, halo[0, :, hs], NT) * root, -1e30)
        top = jnp.maximum(near_top, jnp.max(far, axis=-1, keepdims=True))
        power = jnp.exp(far - top)
        keep = jnp.exp(near_top - top)
        inverse = 1.0 / (keep * near_sum + jnp.sum(power, axis=-1, keepdims=True))
        mix = keep * near_out + dot(power.astype(BF16), halo[1, :, hs])
        mix = (mix * inverse).astype(BF16)
        raw[0, h, ends[0]] = mix[:edge]
        raw[0, h, ends[1]] = mix[edge:]
    for e in ends:
        pass_keys(pl.ds(e.start, edge), k_recv.at[1]).start()

    def token_norm(d):
        total_sq = jnp.zeros((tokens, ATT_HD), F32)
        for h in range(heads):
            part = raw[d, h].astype(F32)
            total_sq = total_sq + part * part
        return lax.rsqrt(jnp.sum(total_sq, axis=-1, keepdims=True) * (1.0 / width) + 1e-06)

    def keys_of(d):
        return jnp.concatenate([raw[d, h] for h in range(heads)], axis=1)

    def block(d, keys, norm, half):
        both = dot(keys, wft[:, half * 2 * hid:(half + 1) * 2 * hid])
        back = dot(sall[d], ws[half * hid:(half + 1) * hid], NT)
        first = both[:, :hid] * norm
        third = both[:, hid:] * norm
        sig = jax.nn.sigmoid(first)
        gate = first * sig
        pulled = back * norm
        left = jnp.concatenate(
            [
                (pulled * third * (sig * (1.0 + first * (1.0 - sig)))).astype(BF16),
                (pulled * gate).astype(BF16),
            ],
            axis=1,
        )
        return left, (gate * third).astype(BF16)

    def rows(i):
        return pl.ds(i * piece, piece)

    def aside(i):
        return remote(gout.at[rows(i)], gside.at[rows(i)], row_send.at[4], side_recv.at[i], "row", across)

    own_keys = keys_of(0)
    own_norm = token_norm(0)
    own_blocks = [block(0, own_keys, own_norm, half) for half in range(2)]

    @pl.when(center)
    def _():
        cnt_up.wait_recv()
        cnt[2] = cnt[0] + cnt[1]
        cnt_mid.start()

    s_near.wait_recv()
    middle.wait_recv()
    pass_keys(pl.ds(0, 2 * edge), k_recv.at[1]).wait_recv()
    next_keys = keys_of(1)
    next_norm = token_norm(1)
    keys = jnp.concatenate([own_keys, next_keys], axis=0)
    steps = jnp.concatenate([sall[0], sall[1]], axis=0)
    for half in range(2):
        left, gated = (
            jnp.concatenate(pair, axis=0) for pair in zip(own_blocks[half], block(1, next_keys, next_norm, half))
        )
        grad = dot(left, keys, TN)
        if half == 0:
            gout[: 2 * hid] = grad.astype(BF16)
            for i in range(2 * per):
                aside(i).start()
        else:
            gfull[: 2 * hid] = grad
        grad = dot(gated, steps, TN)
        if half == 0:
            gout[2 * hid:] = grad.astype(BF16)
            for i in range(2 * per, 3 * per):
                aside(i).start()
        else:
            gfull[2 * hid:] = grad

    @pl.when(center)
    def _():
        cnt_mid.wait_recv()
        cnt[3] = cnt[2] + cnt[3]
        cnt_down.start()

    ss[0, 2:3] = jnp.sum(wold[:hid] * wold[:hid], axis=0, keepdims=True)
    ss[0, 3:4] = jnp.sum(wold[hid:2 * hid] * wold[hid:2 * hid], axis=0, keepdims=True)
    second_old = wold[2 * hid:]
    second_size = jnp.sqrt(jnp.sum(second_old * second_old, axis=-1, keepdims=True) + 1e-06)

    def rise(i, target, receives):
        return remote(gsum.at[rows(i)], target.at[rows(i)], view_send.at[2], receives.at[i], "view", inner)

    def fall(i):
        return remote(gtot.at[rows(i)], gtot.at[rows(i)], view_send.at[3], total_recv.at[i], "view", outer)

    def lift(i):
        aside(i).wait_recv()
        gsum[rows(i)] = (gfull[rows(i)] + gside[rows(i)].astype(F32)).astype(BF16)
        rise(i, gin, out_recv).start()

    def join(i):
        aside(i).wait_recv()
        partial = gfull[rows(i)] + gside[rows(i)].astype(F32)
        rise(i, gin, out_recv).wait_recv()
        gsum[rows(i)] = (partial + gin[rows(i)].astype(F32)).astype(BF16)
        rise(i, gtot, total_recv).start()

    def finish(i):
        rise(i, gtot, total_recv).wait_recv()
        gtot[rows(i)] = (gsum[rows(i)].astype(F32) + gtot[rows(i)].astype(F32)).astype(BF16)
        fall(i).start()

    roles = (
        (low & center, join, finish, LAGS[0]),
        (~low & center, join, finish, LAGS[1]),
        (low & leaf, lift, None, LEADS[0]),
        (~low & leaf, lift, None, LEADS[1]),
    )
    for role, begin, _, ahead in roles:
        @pl.when(role)
        def _():
            for i in range(ahead):
                begin(i)
            if begin is lift:
                cnt_down.wait_recv()

    share_total = 1.0 / cnt[3, 0:1, 0:1]

    def arrive(i):
        for role, begin, end, ahead in roles:
            @pl.when(role)
            def _():
                if i + ahead < pieces:
                    begin(i + ahead)
                if end is None:
                    fall(i).wait_recv()
                else:
                    end(i)

    def raise_rows(i):
        raised = wold[rows(i)] + gtot[rows(i)].astype(F32) * share_total
        if i < 2 * per:
            news[0, rows(i)] = raised.astype(BF16)
            return jnp.sum(raised * raised, axis=0, keepdims=True)
        at = (i - 2 * per) * piece
        size = jnp.sqrt(jnp.sum(raised * raised, axis=-1, keepdims=True) + 1e-06)
        news[0, rows(i)] = (raised * (second_size[at:at + piece] / size)).astype(BF16)

    groups = [(0, per), (per, 2 * per), (2 * per, 3 * per - 2), (3 * per - 2, 3 * per - 1), (3 * per - 1, 3 * per)]

    def span(group):
        return pl.ds(group[0] * piece, (group[1] - group[0]) * piece)

    def lend(i):
        return remote(news.at[0, rows(i)], news.at[2, rows(i)], row_send.at[5], far_recv.at[i], "row", across)

    def pair(g, slot, receives):
        return remote(
            news.at[slot, span(groups[g])], news.at[slot + 1, span(groups[g])], row_send.at[5], receives.at[g], "row", partner
        )

    def relay(i):
        lend(i).wait_recv()
        for g, group in enumerate(groups):
            if group[1] == i + 1:
                pair(g, 2, on_recv).start()

    ss_copies = [
        remote(ss.at[0], ss.at[d], row_send.at[5 + d], row_recv.at[4 + d], "row", flip(me, d)) for d in range(1, nr)
    ]
    for i in range(pieces):
        arrive(i)
        square = raise_rows(i)
        lend(i).start()
        for g, group in enumerate(groups):
            if group[1] == i + 1:
                pair(g, 0, near_recv).start()
        if i < 2 * per:
            running = square if i % per == 0 else running + square
            if i % per == per - 1:
                m = i // per
                ss[0, m:m + 1] = running
                if m == 1:
                    for copy in ss_copies:
                        copy.start()
        if i >= HOLD:
            relay(i - HOLD)
    for i in range(pieces - HOLD, 2 * per):
        relay(i)
    for copy in ss_copies:
        copy.wait_recv()
    sums = ss[0]
    for d in range(1, nr):
        sums = sums + ss[d]
    scales = jnp.sqrt(sums[2:4] + 1e-06) / jnp.sqrt(sums[0:2] + 1e-06)
    wide = own_keys.astype(F32)
    scaled = [(wide * scales[m:m + 1]).astype(BF16) for m in range(2)]

    def apply(slot):
        first = dot(scaled[0], news[slot, :hid], NT) * own_norm
        third = dot(scaled[1], news[slot, hid:2 * hid], NT) * own_norm
        return (first * jax.nn.sigmoid(first) * third).astype(BF16)

    applied = [apply(0)]
    for g in range(2):
        pair(g, 0, near_recv).wait_recv()
    applied.append(apply(1))
    applied.append(apply(2))
    for i in range(max(pieces - HOLD, 2 * per), groups[2][1]):
        relay(i)
    for g in range(2):
        pair(g, 2, on_recv).wait_recv()
    applied.append(apply(3))
    for i in range(max(pieces - HOLD, groups[2][1]), pieces):
        relay(i)
    total = dot(applied[0], news[0, 2 * hid:])
    for g in range(2, len(groups)):
        pair(g, 0, near_recv).wait_recv()
    total = total + dot(applied[1], news[1, 2 * hid:])
    total = total + dot(applied[2], news[2, 2 * hid:])
    for g in range(2, len(groups)):
        pair(g, 2, on_recv).wait_recv()
    total = total + dot(applied[3], news[3, 2 * hid:])
    out_ref[...] = total.astype(BF16)

    @pl.when(has_above)
    def _():
        up_halo.wait_send()

    @pl.when(has_below)
    def _():
        down_halo.wait_send()

    s_near.wait_send()
    remote(raw.at[0], raw.at[1], row_send.at[3], row_recv.at[2], "row", partner).wait_send()
    remote(gout, gside, row_send.at[4], row_recv.at[2], "row", across).wait_send()
    remote(news.at[pl.ds(0, 3)], news.at[pl.ds(0, 3)], row_send.at[5], row_recv.at[2], "row", partner).wait_send()
    for copy in ss_copies:
        copy.wait_send()
    remote(gsum, gin, view_send.at[2], row_recv.at[2], "view", inner).wait_send()
    cnt_up.wait_send()

    @pl.when(center)
    def _():
        cnt_down.wait_send()
        remote(gtot, gtot, view_send.at[3], row_recv.at[2], "view", outer).wait_send()


def fused_step(
    nr, nz,
    query_feats, key_feats, value_feats, target, token_rates, row_reach, view_counts,
    w_first, w_third, w_second,
):
    _, row_count, cols, width = query_feats.shape
    tokens = row_count * cols
    hid = width // nr
    edge = HALO * cols
    heads = width // ATT_HD
    pieces = 3 * PER
    anywhere = pl.BlockSpec(memory_space=pl.ANY)
    flat = lambda a: a.reshape(tokens, width)
    out = pl.pallas_call(
        functools.partial(step_kernel, nr, nz, cols),
        out_shape=pltpu.VMEM((tokens, width), BF16),
        in_specs=[anywhere] * 5 + [pl.BlockSpec(memory_space=pltpu.HBM)] * 2 + [anywhere] * 3,
        out_specs=pl.BlockSpec(memory_space=pltpu.VMEM),
        scratch_shapes=[
            pltpu.VMEM((tokens, width), BF16),
            pltpu.VMEM((2, tokens, width), BF16),
            pltpu.VMEM((tokens, width), BF16),
            pltpu.VMEM((1, tokens), F32),
            pltpu.SMEM((row_count,), jnp.int32),
            pltpu.SMEM((1,), jnp.int32),
            pltpu.VMEM((width, 4 * hid), BF16),
            pltpu.VMEM((2 * hid, width), BF16),
            pltpu.VMEM((2, 2 * edge, width), BF16),
            pltpu.VMEM((2, heads, tokens, ATT_HD), BF16),
            pltpu.VMEM((2, tokens, width), BF16),
            pltpu.VMEM((4, 8, 128), F32),
            pltpu.VMEM((3 * hid, width), BF16),
            pltpu.VMEM((3 * hid, width), BF16),
            pltpu.VMEM((3 * hid, width), F32),
            pltpu.VMEM((3 * hid, width), BF16),
            pltpu.VMEM((3 * hid, width), BF16),
            pltpu.VMEM((3 * hid, width), BF16),
            pltpu.VMEM((3 * hid, width), F32),
            pltpu.VMEM((nr, 3 * hid, width), BF16),
            pltpu.VMEM((nr, 4, width), F32),
            pltpu.SemaphoreType.DMA((9,)),
            pltpu.SemaphoreType.DMA((5 + nr,)),
            pltpu.SemaphoreType.DMA((4 + nr,)),
            pltpu.SemaphoreType.DMA((2,)),
            pltpu.SemaphoreType.DMA((4,)),
            pltpu.SemaphoreType.DMA((pieces,)),
            pltpu.SemaphoreType.DMA((pieces,)),
            pltpu.SemaphoreType.DMA((pieces,)),
            pltpu.SemaphoreType.DMA((5,)),
            pltpu.SemaphoreType.DMA((pieces,)),
            pltpu.SemaphoreType.DMA((5,)),
        ],
        compiler_params=pltpu.CompilerParams(collective_id=0, has_side_effects=True),
    )(
        flat(query_feats), flat(key_feats), flat(value_feats), flat(target),
        token_rates.reshape(1, tokens), row_reach, view_counts,
        w_first.reshape(width, width), w_third.reshape(width, width), w_second.reshape(width, width),
    )
    return out.reshape(query_feats.shape)


def solution(mesh):
    placed = (
        P("view", "row", None, "head"),
        P("view", "row", None, "head"),
        P("view", "row", None, "head"),
        P("view", "row", None, "head"),
        P("view", "head", "row"),
        P("row"),
        P("view"),
        P("head", None, None),
        P("head", None, None),
        P("head", None, None),
    )
    nr, nz = mesh.shape["row"], mesh.shape["view"]
    fits = nr == 4 and nz == 4 and HD % (128 * nr) == 0 and HD % (16 * nr * PER) == 0
    return jax.shard_map(
        functools.partial(fused_step, nr, nz) if fits else per_device,
        mesh=mesh,
        in_specs=placed,
        out_specs=P("view", "row", None, "head"),
        check_vma=False,
    )
```

```python
import functools
import math

import jax
import jax.numpy as jnp
from jax import lax
from jax.experimental import pallas as pl
from jax.experimental.pallas import tpu as pltpu
from jax.sharding import PartitionSpec as P

HD = 512
ATT_HD = 128
HALO = 2
PER = 8
SKIP = 4
LAGS = (9, 9)
LEADS = (24, 24)
MESH = pl.DeviceIdType.MESH
BF16 = jnp.bfloat16
F32 = jnp.float32
NT = (((1,), (1,)), ((), ()))
TN = (((0,), (0,)), ((), ()))


def with_halo(value, sides, width):
    for axis, dim in sides:
        size, length = (lax.axis_size(axis), value.shape[dim])
        up = [(i, (i + 1) % size) for i in range(size - 1)]
        down = [(j, i) for i, j in up]
        last = lax.slice_in_dim(value, length - width, length, axis=dim)
        leading = lax.slice_in_dim(value, 0, width, axis=dim)
        before = lax.ppermute(last, axis, up)
        after = lax.ppermute(leading, axis, down)
        value = jnp.concatenate([before, value, after], axis=dim)
    return value


def silu_slope(values_in):
    sigmoid_x = jax.nn.sigmoid(values_in)
    return sigmoid_x * (1.0 + values_in * (1.0 - sigmoid_x))


def attend(
    query_rows,
    key_rows,
    value_rows,
    q_row_ids,
    k_row_ids,
    q_tok,
    k_tok,
    k_valid,
    q_reach,
    grid_rows,
):
    count_q = query_rows.shape[0]
    count_k = key_rows.shape[0]
    groups = query_rows.shape[1] // ATT_HD
    query_heads = query_rows.reshape(count_q, groups, ATT_HD)
    key_heads = key_rows.reshape(count_k, groups, ATT_HD)
    value_heads = value_rows.reshape(count_k, groups, ATT_HD)
    scores = jnp.einsum(
        "qhd,khd->hqk", query_heads, key_heads, preferred_element_type=jnp.float32
    ) / math.sqrt(ATT_HD)
    inside = (k_row_ids >= 0) & (k_row_ids < grid_rows)
    in_band = jnp.abs(k_row_ids[None, :] - q_row_ids[:, None]) <= q_reach[:, None]
    allowed = in_band & inside[None, :] & (k_valid[None, :] | (k_tok[None, :] == q_tok[:, None]))
    scores = jnp.where(allowed[None], scores, -1e30)
    row_top = jnp.max(scores, -1, keepdims=True)
    powers = jnp.exp(scores - row_top)
    weights = (powers / jnp.sum(powers, -1, keepdims=True)).astype(jnp.bfloat16)
    output_rows = jnp.einsum(
        "hqk,khd->qhd", weights, value_heads, preferred_element_type=jnp.float32
    )
    return output_rows.reshape(count_q, groups * ATT_HD).astype(jnp.bfloat16)


def renorm(old_matrix, grad, total_valid):
    old_rows = old_matrix.astype(jnp.float32)
    raised = old_rows + grad / total_valid
    rescale = jnp.sqrt(jnp.sum(old_rows * old_rows, -1, keepdims=True) + 1e-06) / jnp.sqrt(
        jnp.sum(raised * raised, -1, keepdims=True) + 1e-06
    )
    return (raised * rescale).astype(jnp.bfloat16)


def per_device(
    query_feats,
    key_feats,
    value_feats,
    target,
    token_rates,
    row_reach,
    view_counts,
    w_first,
    w_third,
    w_second,
):
    row_count = query_feats.shape[1]
    col_count = query_feats.shape[2]
    feat_width = query_feats.shape[3]
    heads_here = feat_width // HD
    tokens_here = row_count * col_count
    key_span = row_count + 2 * HALO
    grid_rows = lax.axis_size("row") * row_count
    row_base = lax.axis_index("row") * row_count
    view_total = view_counts[0]
    total_valid = lax.psum(view_total.astype(jnp.float32), "view")
    paired = jnp.stack([key_feats[0], value_feats[0]], 0)
    padded = with_halo(paired, (("row", 1),), HALO)
    q_row_ids = row_base + jnp.repeat(jnp.arange(row_count, dtype=jnp.int32), col_count)
    k_row_ids = row_base - HALO + jnp.repeat(jnp.arange(key_span, dtype=jnp.int32), col_count)
    q_tok = q_row_ids * col_count + jnp.tile(jnp.arange(col_count, dtype=jnp.int32), row_count)
    k_tok = k_row_ids * col_count + jnp.tile(jnp.arange(col_count, dtype=jnp.int32), key_span)
    k_valid = k_tok < view_total
    q_reach = jnp.repeat(row_reach, col_count)
    attended = attend(
        query_feats[0].reshape(tokens_here, feat_width),
        padded[0].reshape(key_span * col_count, feat_width),
        padded[1].reshape(key_span * col_count, feat_width),
        q_row_ids,
        k_row_ids,
        q_tok,
        k_tok,
        k_valid,
        q_reach,
        grid_rows,
    )
    attended = attended.reshape(tokens_here, heads_here, HD).astype(jnp.float32)
    fast_keys = (
        attended * lax.rsqrt(jnp.mean(attended * attended, -1, keepdims=True) + 1e-06)
    ).astype(jnp.bfloat16)
    valid_mask = (q_tok < view_total).astype(jnp.float32)
    rates_tok = token_rates[0].T
    scaled = (
        rates_tok[:, :, None]
        * valid_mask[:, None, None]
        * target[0].reshape(tokens_here, heads_here, HD).astype(jnp.float32)
    ).astype(jnp.bfloat16)
    first_proj = jnp.einsum("thi,hij->thj", fast_keys, w_first, preferred_element_type=jnp.float32)
    third_proj = jnp.einsum("thi,hij->thj", fast_keys, w_third, preferred_element_type=jnp.float32)
    gated_rows = (jax.nn.silu(first_proj) * third_proj).astype(jnp.bfloat16)
    back_rows = jnp.einsum("tho,hjo->thj", scaled, w_second, preferred_element_type=jnp.float32)
    back_first = (back_rows * third_proj * silu_slope(first_proj)).astype(jnp.bfloat16)
    back_third = (back_rows * jax.nn.silu(first_proj)).astype(jnp.bfloat16)
    grad_first = jnp.einsum(
        "thi,thj->hij", fast_keys, back_first, preferred_element_type=jnp.float32
    )
    grad_third = jnp.einsum(
        "thi,thj->hij", fast_keys, back_third, preferred_element_type=jnp.float32
    )
    grad_second = jnp.einsum("thj,tho->hjo", gated_rows, scaled, preferred_element_type=jnp.float32)
    grad_first, grad_third, grad_second = lax.psum(
        (grad_first, grad_third, grad_second), ("view", "row")
    )
    new_first = renorm(w_first, grad_first, total_valid)
    new_third = renorm(w_third, grad_third, total_valid)
    new_second = renorm(w_second, grad_second, total_valid)
    applied = (
        jax.nn.silu(
            jnp.einsum("thi,hij->thj", fast_keys, new_first, preferred_element_type=jnp.float32)
        )
        * jnp.einsum("thi,hij->thj", fast_keys, new_third, preferred_element_type=jnp.float32)
    ).astype(jnp.bfloat16)
    fast_out = jnp.einsum(
        "thj,hjo->tho", applied, new_second, preferred_element_type=jnp.float32
    ).astype(jnp.bfloat16)
    return fast_out.reshape(1, row_count, col_count, feat_width)


def halve(values_in, size):
    if size & (size - 1) == 0:
        return values_in >> (size.bit_length() - 1)
    return lax.div(values_in, jnp.int32(size))


def dot(left, right, dims=(((1,), (0,)), ((), ()))):
    return lax.dot_general(left, right, dims, preferred_element_type=F32)


def flip(index, bits):
    bit = 1
    while bit <= bits:
        if bits & bit:
            index = index + bit - 2 * bit * lax.rem(lax.div(index, bit), 2)
        bit *= 2
    return index


def step_kernel(
    nr, nz, cols,
    q_hbm, k_hbm, v_hbm, t_hbm, rates_hbm, reach_hbm, count_hbm, wf_hbm, wt_hbm, ws_hbm,
    out_ref,
    q_ref, kv_ref, t_ref, rates_ref, reach_ref, count_ref, wft, ws, halo, raw, sall, cnt, gout, gside, gslant, gfull, gsum, gin, gtot,
    wold, news, ss,
    load_sem, row_send, row_recv, halo_recv, k_recv, view_send, side_recv, total_recv, near_recv, far_recv, on_recv,
):
    tokens, width = q_ref.shape
    rows_here = tokens // cols
    hid = width // nr
    edge = HALO * cols
    heads = width // ATT_HD
    pieces = total_recv.shape[0]
    piece = 3 * hid // pieces
    per = pieces // 3
    me = lax.axis_index("row")
    mz = lax.axis_index("view")
    partner, across = flip(me, 1), flip(me, 2)
    above, below = me + 1, me - 1
    mine = pl.ds(pl.multiple_of(me * hid, hid), hid)
    theirs = pl.ds(pl.multiple_of(across * hid, hid), hid)
    low = mz < nz // 2
    inner = jnp.where(low, mz + 1, mz - 1)
    outer = jnp.where(low, mz - 1, mz + 1)
    center = (mz > 0) & (mz < nz - 1)
    leaf = (mz == 0) | (mz == nz - 1)
    has_above = me < nr - 1
    has_below = me > 0

    barrier = pltpu.get_barrier_semaphore()
    for d in range(1, nr):
        pl.semaphore_signal(barrier, inc=1, device_id={"row": flip(me, d)}, device_id_type=MESH)
    pl.semaphore_signal(barrier, inc=1, device_id={"view": inner}, device_id_type=MESH)

    slant = jnp.where(center, outer, inner)
    pl.semaphore_signal(barrier, inc=1, device_id={"row": across, "view": slant}, device_id_type=MESH)

    @pl.when(center)
    def _():
        pl.semaphore_signal(barrier, inc=1, device_id={"view": outer}, device_id_type=MESH)

    loads = [
        pltpu.make_async_copy(source, target, load_sem.at[min(i, 7) if i < 11 else 8])
        for i, (source, target) in enumerate((
            (k_hbm, kv_ref.at[0]), (v_hbm, kv_ref.at[1]), (count_hbm, count_ref), (reach_hbm, reach_ref),
            (t_hbm, t_ref), (rates_hbm, rates_ref), (q_hbm, q_ref),
            (wf_hbm.at[:, theirs], wft.at[:, pl.ds(0, hid)]), (wt_hbm.at[:, theirs], wft.at[:, pl.ds(hid, hid)]),
            (wf_hbm.at[:, mine], wft.at[:, pl.ds(2 * hid, hid)]), (wt_hbm.at[:, mine], wft.at[:, pl.ds(3 * hid, hid)]),
            (ws_hbm.at[theirs, :], ws.at[pl.ds(0, hid)]), (ws_hbm.at[mine, :], ws.at[pl.ds(hid, hid)]),
        ))
    ]
    for load in loads:
        load.start()

    def remote(source, target, sends, receives, axis, peer):
        return pltpu.make_async_remote_copy(
            src_ref=source, dst_ref=target, send_sem=sends, recv_sem=receives,
            device_id={axis: peer}, device_id_type=MESH,
        )

    @pl.when(me == 0)
    def _():
        halo[:, :edge] = jnp.zeros((2, edge, width), BF16)

    @pl.when(me == nr - 1)
    def _():
        halo[:, edge:] = jnp.zeros((2, edge, width), BF16)

    row_base = me * rows_here
    tok_base = me * tokens

    pl.semaphore_wait(barrier, nr + 1 + jnp.where(center, 1, 0))

    @pl.when(has_above)
    def _():
        for i, source in enumerate((k_hbm, v_hbm)):
            remote(
                source.at[pl.ds(tokens - edge, edge)], halo.at[i, pl.ds(0, edge)], row_send.at[0], halo_recv.at[0, i], "row", above
            ).start()

    @pl.when(has_below)
    def _():
        for i, source in enumerate((k_hbm, v_hbm)):
            remote(
                source.at[pl.ds(0, edge)], halo.at[i, pl.ds(edge, edge)], row_send.at[1], halo_recv.at[1, i], "row", below
            ).start()

    up_halo = remote(halo.at[:, pl.ds(edge, edge)], halo.at[:, pl.ds(0, edge)], row_send.at[0], row_recv.at[0], "row", above)
    down_halo = remote(halo.at[:, pl.ds(0, edge)], halo.at[:, pl.ds(edge, edge)], row_send.at[1], row_recv.at[1], "row", below)

    for load in loads[2:4]:
        load.wait()
    view_total = count_ref[0]
    cnt[0] = jnp.full((8, 128), view_total, jnp.int32).astype(F32)
    sub = lax.broadcasted_iota(jnp.int32, (tokens, tokens), 0)
    lane = lax.broadcasted_iota(jnp.int32, (tokens, tokens), 1)
    tok_col = tok_base + lax.broadcasted_iota(jnp.int32, (tokens, 1), 0)
    valid_col = (tok_col < view_total).astype(F32)
    for load in loads[4:6]:
        load.wait()
    rate_col = jnp.sum(jnp.where(sub == lane, rates_ref[...], 0.0), axis=1, keepdims=True)
    sall[0] = (rate_col * valid_col * t_ref[...].astype(F32)).astype(BF16)
    s_near = remote(sall.at[0], sall.at[1], row_send.at[2], row_recv.at[0], "row", partner)
    s_near.start()
    cnt_up = remote(cnt.at[0], cnt.at[1], view_send.at[0], row_recv.at[1], "view", inner)
    cnt_mid = remote(cnt.at[2], cnt.at[3], view_send.at[0], row_recv.at[2], "view", inner)
    cnt_down = remote(cnt.at[3], cnt.at[3], view_send.at[1], row_recv.at[2], "view", outer)

    @pl.when(leaf)
    def _():
        cnt_up.start()

    def allowed(q_tok, k_tok):
        q_row = halve(q_tok, cols)
        k_row = halve(k_tok + edge, cols) - HALO
        reach = jnp.zeros(q_tok.shape, jnp.int32)
        for r in range(rows_here):
            reach = jnp.where(q_row == r, reach_ref[r], reach)
        k_abs = k_row + row_base
        return (
            (jnp.abs(k_row - q_row) <= reach)
            & (k_abs >= 0)
            & (k_abs < nr * rows_here)
            & ((k_tok + tok_base < view_total) | (k_tok == q_tok))
        )

    near_ok = allowed(sub, lane)
    far_q = lax.broadcasted_iota(jnp.int32, (2 * edge, 2 * edge), 0)
    far_k = lax.broadcasted_iota(jnp.int32, (2 * edge, 2 * edge), 1)
    far_ok = allowed(
        jnp.where(far_q < edge, far_q, far_q - 2 * edge + tokens),
        jnp.where(far_k < edge, far_k - edge, far_k - edge + tokens),
    )
    root = 1.0 / math.sqrt(ATT_HD)
    spans = [slice(h * ATT_HD, (h + 1) * ATT_HD) for h in range(heads)]
    for load in loads[:2] + loads[6:7]:
        load.wait()
    inside = slice(edge, tokens - edge)
    ends = (slice(0, edge), slice(tokens - edge, tokens))

    def outer_rows(value):
        return jnp.concatenate([value[e] for e in ends], axis=0)

    def pass_keys(at, receives):
        return remote(raw.at[0, :, at], raw.at[1, :, at], row_send.at[3], receives, "row", partner)

    near = []
    for h, hs in enumerate(spans):
        scores = jnp.where(near_ok, dot(q_ref[:, hs], kv_ref[0, :, hs], NT) * root, -1e30)
        top = jnp.max(scores, axis=-1, keepdims=True)
        power = jnp.exp(scores - top)
        total = jnp.sum(power, axis=-1, keepdims=True)
        mix = dot(power.astype(BF16), kv_ref[1, :, hs])
        raw[0, h, inside] = (mix[inside] * (1.0 / total[inside])).astype(BF16)
        near.append((outer_rows(top), outer_rows(total), outer_rows(mix), outer_rows(q_ref.at[:, hs])))
    middle = pass_keys(pl.ds(edge, tokens - 2 * edge), k_recv.at[0])
    middle.start()
    pltpu.make_async_copy(wft, wft, load_sem.at[7]).wait()
    pltpu.make_async_copy(ws, ws, load_sem.at[8]).wait()
    def halo_here(i):
        @pl.when(has_below)
        def _():
            remote(halo.at[i, pl.ds(edge, edge)], halo.at[i, pl.ds(0, edge)], row_send.at[0], halo_recv.at[0, i], "row", above).wait_recv()

        @pl.when(has_above)
        def _():
            remote(halo.at[i, pl.ds(0, edge)], halo.at[i, pl.ds(edge, edge)], row_send.at[1], halo_recv.at[1, i], "row", below).wait_recv()

    def keys_of(d, rows_at):
        return jnp.concatenate(
            [jnp.concatenate([raw[d, h, at] for h in range(heads)], axis=1) for at in rows_at], axis=0
        )

    def token_norm(keys):
        total_sq = jnp.zeros((keys.shape[0], ATT_HD), F32)
        for hs in spans:
            part = keys[:, hs].astype(F32)
            total_sq = total_sq + part * part
        return lax.rsqrt(jnp.sum(total_sq, axis=-1, keepdims=True) * (1.0 / width) + 1e-06)

    def block(keys, steps, norm, half):
        both = dot(keys, wft[:, half * 2 * hid:(half + 1) * 2 * hid])
        back = dot(steps, ws[half * hid:(half + 1) * hid], NT)
        first = both[:, :hid] * norm
        third = both[:, hid:] * norm
        sig = jax.nn.sigmoid(first)
        gate = first * sig
        pulled = back * norm
        left = jnp.concatenate(
            [
                (pulled * third * (sig * (1.0 + first * (1.0 - sig)))).astype(BF16),
                (pulled * gate).astype(BF16),
            ],
            axis=1,
        )
        return left, (gate * third).astype(BF16)

    def token_set(rows_at):
        keys = jnp.concatenate([keys_of(d, rows_at) for d in range(2)], axis=0)
        steps = jnp.concatenate([sall[d, at] for d in range(2) for at in rows_at], axis=0)
        return keys, steps, token_norm(keys)

    s_near.wait_recv()
    middle.wait_recv()
    inner_set = token_set((inside,))
    inner_blocks = [block(*inner_set, half) for half in range(2)]
    halo_here(0)
    partly = []
    for h, hs in enumerate(spans):
        near_top, near_sum, near_out, queries = near[h]
        far = jnp.where(far_ok, dot(queries, halo[0, :, hs], NT) * root, -1e30)
        top = jnp.maximum(near_top, jnp.max(far, axis=-1, keepdims=True))
        power = jnp.exp(far - top)
        keep = jnp.exp(near_top - top)
        inverse = 1.0 / (keep * near_sum + jnp.sum(power, axis=-1, keepdims=True))
        partly.append((power.astype(BF16), keep * near_out, inverse))
    halo_here(1)
    for h, hs in enumerate(spans):
        power, kept, inverse = partly[h]
        mix = ((kept + dot(power, halo[1, :, hs])) * inverse).astype(BF16)
        raw[0, h, ends[0]] = mix[:edge]
        raw[0, h, ends[1]] = mix[edge:]
    for e in ends:
        pass_keys(pl.ds(e.start, edge), k_recv.at[1]).start()

    def rows(i):
        return pl.ds(i * piece, piece)

    def skew(i):
        return pltpu.make_async_remote_copy(
            src_ref=gout.at[rows(i)], dst_ref=gslant.at[rows(i)], send_sem=row_send.at[4], recv_sem=side_recv.at[i],
            device_id={"row": across, "view": inner}, device_id_type=MESH,
        )

    def early(i):
        return remote(gsum.at[rows(i)], gin.at[rows(i)], view_send.at[2], side_recv.at[i], "view", inner)

    def aside(i):
        return remote(gout.at[rows(i)], gside.at[rows(i)], row_send.at[4], side_recv.at[i], "row", across)

    @pl.when(center)
    def _():
        cnt_up.wait_recv()
        cnt[2] = cnt[0] + cnt[1]
        cnt_mid.start()

    pass_keys(pl.ds(0, 2 * edge), k_recv.at[1]).wait_recv()
    outer_set = token_set(ends)
    keys, steps = (jnp.concatenate(pair, axis=0) for pair in zip(inner_set[:2], outer_set[:2]))
    for half in range(2):
        left, gated = (
            jnp.concatenate(pair, axis=0) for pair in zip(inner_blocks[half], block(*outer_set, half))
        )
        grad = dot(left, keys, TN)
        if half == 0:
            gout[: 2 * hid] = grad.astype(BF16)

            @pl.when(leaf)
            def _():
                for i in range(SKIP):
                    skew(i).start()

            @pl.when(center)
            def _():
                for i in range(SKIP):
                    aside(i).start()

            for i in range(SKIP, 2 * per):
                aside(i).start()
        else:
            gfull[: 2 * hid] = grad

            @pl.when(leaf)
            def _():
                for i in range(SKIP):
                    gsum[rows(i)] = gfull[rows(i)].astype(BF16)
                    early(i).start()

        grad = dot(gated, steps, TN)
        if half == 0:
            gout[2 * hid:] = grad.astype(BF16)
            for i in range(2 * per, 3 * per):
                aside(i).start()
        else:
            gfull[2 * hid:] = grad

    @pl.when(center)
    def _():
        cnt_mid.wait_recv()
        cnt[3] = cnt[2] + cnt[3]
        cnt_down.start()

    wold[0:hid] = wft[:, 2 * hid:3 * hid].astype(F32).T
    wold[hid:2 * hid] = wft[:, 3 * hid:].astype(F32).T
    wold[2 * hid:] = ws[hid:].astype(F32)
    ss[0, 2:3] = jnp.sum(wold[:hid] * wold[:hid], axis=0, keepdims=True)
    ss[0, 3:4] = jnp.sum(wold[hid:2 * hid] * wold[hid:2 * hid], axis=0, keepdims=True)
    second_old = wold[2 * hid:]
    second_size = jnp.sqrt(jnp.sum(second_old * second_old, axis=-1, keepdims=True) + 1e-06)

    def here(i, count):
        at = gin.at[pl.ds(0, count * piece)]
        return remote(at, at, view_send.at[2], side_recv.at[i], "view", inner)

    def rise(i, target, receives):
        return remote(gsum.at[rows(i)], target.at[rows(i)], view_send.at[2], receives.at[i], "view", inner)

    def fall(i):
        return remote(gtot.at[rows(i)], gtot.at[rows(i)], view_send.at[3], total_recv.at[i], "view", outer)

    def lift(i):
        if i < SKIP:
            return
        aside(i).wait_recv()
        gsum[rows(i)] = (gfull[rows(i)] + gside[rows(i)].astype(F32)).astype(BF16)
        rise(i, gin, side_recv).start()

    def join(i):
        here(i, 3 if i < SKIP else 2).wait_recv()
        partial = gfull[rows(i)] + gside[rows(i)].astype(F32)
        if i < SKIP:
            partial = partial + gslant[rows(i)].astype(F32)
        gsum[rows(i)] = (partial + gin[rows(i)].astype(F32)).astype(BF16)
        rise(i, gtot, total_recv).start()

    def finish(i):
        rise(i, gtot, total_recv).wait_recv()
        gtot[rows(i)] = (gsum[rows(i)].astype(F32) + gtot[rows(i)].astype(F32)).astype(BF16)
        fall(i).start()

    roles = (
        (low & center, join, finish, LAGS[0]),
        (~low & center, join, finish, LAGS[1]),
        (low & leaf, lift, None, LEADS[0]),
        (~low & leaf, lift, None, LEADS[1]),
    )
    for role, begin, _, ahead in roles:
        @pl.when(role)
        def _():
            for i in range(ahead):
                begin(i)
            if begin is lift:
                cnt_down.wait_recv()

    share_total = 1.0 / cnt[3, 0:1, 0:1]

    def arrive(i):
        for role, begin, end, ahead in roles:
            @pl.when(role)
            def _():
                if i + ahead < pieces:
                    begin(i + ahead)
                if end is None:
                    fall(i).wait_recv()
                else:
                    end(i)

    def raise_rows(i):
        raised = wold[rows(i)] + gtot[rows(i)].astype(F32) * share_total
        if i < 2 * per:
            news[0, rows(i)] = raised.astype(BF16)
            return jnp.sum(raised * raised, axis=0, keepdims=True)
        at = (i - 2 * per) * piece
        size = jnp.sqrt(jnp.sum(raised * raised, axis=-1, keepdims=True) + 1e-06)
        news[0, rows(i)] = (raised * (second_size[at:at + piece] / size)).astype(BF16)

    tail = per // 8
    groups = [(0, per), (per, 2 * per), (2 * per, 3 * per - 2 * tail), (3 * per - 2 * tail, 3 * per - tail), (3 * per - tail, 3 * per)]

    def span(group):
        return pl.ds(group[0] * piece, (group[1] - group[0]) * piece)

    def group_of(i):
        return [g for g, group in enumerate(groups) if group[0] <= i < group[1]][0]

    def lend(i):
        return remote(news.at[0, rows(i)], news.at[2, rows(i)], row_send.at[5], far_recv.at[min(group_of(i), 3)], "row", across)

    def lend_over(i):
        return remote(news.at[0, rows(i)], news.at[3, rows(i)], row_send.at[5 + nr], on_recv.at[1], "row", flip(me, 3))

    def pair(g, slot, receives, sends=5):
        return remote(
            news.at[slot, span(groups[g])], news.at[slot + 1, span(groups[g])], row_send.at[sends], receives.at[g // 2 if g < 2 else 1], "row", partner
        )

    def parts_here(part, slot, receives):
        at = pl.ds(part * 2 * hid, (2 - part) * hid)
        remote(news.at[slot, at], news.at[slot + 1, at], row_send.at[5], receives.at[part], "row", partner).wait_recv()

    def relay(g):
        remote(
            news.at[0, span(groups[g])], news.at[2, span(groups[g])], row_send.at[5], far_recv.at[g], "row", across
        ).wait_recv()
        pair(g, 2, on_recv, 6 + nr).start()

    ss_copies = [
        remote(ss.at[0], ss.at[d], row_send.at[5 + d], row_recv.at[2 + d], "row", flip(me, d)) for d in range(1, nr)
    ]
    for i in range(pieces):
        arrive(i)
        square = raise_rows(i)
        lend(i).start()
        if group_of(i) > 2:
            lend_over(i).start()
        for g, group in enumerate(groups):
            if group[1] == i + 1:
                pair(g, 0, near_recv).start()
        if i < 2 * per:
            running = square if i % per == 0 else running + square
            if i % per == per - 1:
                m = i // per
                ss[0, m:m + 1] = running
                if m == 1:
                    for copy in ss_copies:
                        copy.start()
    relay(0)
    relay(1)
    for copy in ss_copies:
        copy.wait_recv()
    sums = ss[0]
    for d in range(1, nr):
        sums = sums + ss[d]
    scales = jnp.sqrt(sums[2:4] + 1e-06) / jnp.sqrt(sums[0:2] + 1e-06)
    own_keys = keys_of(0, (slice(0, tokens),))
    own_norm = token_norm(own_keys)
    wide = own_keys.astype(F32)
    scaled = [(wide * scales[m:m + 1]).astype(BF16) for m in range(2)]

    def apply(slot):
        first = dot(scaled[0], news[slot, :hid], NT) * own_norm
        third = dot(scaled[1], news[slot, hid:2 * hid], NT) * own_norm
        return (first * jax.nn.sigmoid(first) * third).astype(BF16)

    applied = [apply(0)]
    parts_here(0, 0, near_recv)
    applied.append(apply(1))
    applied.append(apply(2))
    relay(2)
    parts_here(0, 2, on_recv)
    applied.append(apply(3))
    total = dot(applied[0], news[0, 2 * hid:])
    parts_here(1, 0, near_recv)
    total = total + dot(applied[1], news[1, 2 * hid:])
    lent = span((groups[3][0], pieces))
    remote(news.at[0, lent], news.at[2, lent], row_send.at[5], far_recv.at[3], "row", across).wait_recv()
    total = total + dot(applied[2], news[2, 2 * hid:])
    parts_here(1, 2, on_recv)
    total = total + dot(applied[3], news[3, 2 * hid:])
    out_ref[...] = total.astype(BF16)

    @pl.when(has_above)
    def _():
        up_halo.wait_send()

    @pl.when(has_below)
    def _():
        down_halo.wait_send()

    s_near.wait_send()
    remote(raw.at[0], raw.at[1], row_send.at[3], row_recv.at[0], "row", partner).wait_send()
    remote(gout, gside, row_send.at[4], row_recv.at[0], "row", across).wait_send()
    sent = pl.ds(0, 3 * hid - (pieces - groups[3][0]) * piece)
    remote(news.at[pl.ds(0, 2)], news.at[pl.ds(0, 2)], row_send.at[5], row_recv.at[0], "row", partner).wait_send()
    remote(news.at[2, sent], news.at[3, sent], row_send.at[6 + nr], row_recv.at[0], "row", partner).wait_send()
    remote(news.at[0, lent], news.at[3, lent], row_send.at[5 + nr], row_recv.at[0], "row", partner).wait_send()
    for copy in ss_copies:
        copy.wait_send()
    remote(gsum, gin, view_send.at[2], row_recv.at[0], "view", inner).wait_send()
    cnt_up.wait_send()

    @pl.when(center)
    def _():
        cnt_down.wait_send()
        remote(gtot, gtot, view_send.at[3], row_recv.at[0], "view", outer).wait_send()


def fused_step(
    nr, nz,
    query_feats, key_feats, value_feats, target, token_rates, row_reach, view_counts,
    w_first, w_third, w_second,
):
    _, row_count, cols, width = query_feats.shape
    tokens = row_count * cols
    hid = width // nr
    edge = HALO * cols
    heads = width // ATT_HD
    pieces = 3 * PER
    anywhere = pl.BlockSpec(memory_space=pl.ANY)
    flat = lambda a: a.reshape(tokens, width)
    out = pl.pallas_call(
        functools.partial(step_kernel, nr, nz, cols),
        out_shape=pltpu.VMEM((tokens, width), BF16),
        in_specs=[anywhere] * 5 + [pl.BlockSpec(memory_space=pltpu.HBM)] * 2 + [anywhere] * 3,
        out_specs=pl.BlockSpec(memory_space=pltpu.VMEM),
        scratch_shapes=[
            pltpu.VMEM((tokens, width), BF16),
            pltpu.VMEM((2, tokens, width), BF16),
            pltpu.VMEM((tokens, width), BF16),
            pltpu.VMEM((1, tokens), F32),
            pltpu.SMEM((row_count,), jnp.int32),
            pltpu.SMEM((1,), jnp.int32),
            pltpu.VMEM((width, 4 * hid), BF16),
            pltpu.VMEM((2 * hid, width), BF16),
            pltpu.VMEM((2, 2 * edge, width), BF16),
            pltpu.VMEM((2, heads, tokens, ATT_HD), BF16),
            pltpu.VMEM((2, tokens, width), BF16),
            pltpu.VMEM((4, 8, 128), F32),
            pltpu.VMEM((3 * hid, width), BF16),
            pltpu.VMEM((3 * hid, width), BF16),
            pltpu.VMEM((3 * hid, width), BF16),
            pltpu.VMEM((3 * hid, width), F32),
            pltpu.VMEM((3 * hid, width), BF16),
            pltpu.VMEM((3 * hid, width), BF16),
            pltpu.VMEM((3 * hid, width), BF16),
            pltpu.VMEM((3 * hid, width), F32),
            pltpu.VMEM((nr, 3 * hid, width), BF16),
            pltpu.VMEM((nr, 4, width), F32),
            pltpu.SemaphoreType.DMA((9,)),
            pltpu.SemaphoreType.DMA((7 + nr,)),
            pltpu.SemaphoreType.DMA((2 + nr,)),
            pltpu.SemaphoreType.DMA((2, 2)),
            pltpu.SemaphoreType.DMA((2,)),
            pltpu.SemaphoreType.DMA((4,)),
            pltpu.SemaphoreType.DMA((pieces,)),
            pltpu.SemaphoreType.DMA((pieces,)),
            pltpu.SemaphoreType.DMA((2,)),
            pltpu.SemaphoreType.DMA((4,)),
            pltpu.SemaphoreType.DMA((2,)),
        ],
        compiler_params=pltpu.CompilerParams(collective_id=0, has_side_effects=True),
    )(
        flat(query_feats), flat(key_feats), flat(value_feats), flat(target),
        token_rates.reshape(1, tokens), row_reach, view_counts,
        w_first.reshape(width, width), w_third.reshape(width, width), w_second.reshape(width, width),
    )
    return out.reshape(query_feats.shape)


def solution(mesh):
    placed = (
        P("view", "row", None, "head"),
        P("view", "row", None, "head"),
        P("view", "row", None, "head"),
        P("view", "row", None, "head"),
        P("view", "head", "row"),
        P("row"),
        P("view"),
        P("head", None, None),
        P("head", None, None),
        P("head", None, None),
    )
    nr, nz = mesh.shape["row"], mesh.shape["view"]
    fits = nr == 4 and nz == 4 and HD % (128 * nr) == 0 and HD % (16 * nr * PER) == 0
    return jax.shard_map(
        functools.partial(fused_step, nr, nz) if fits else per_device,
        mesh=mesh,
        in_specs=placed,
        out_specs=P("view", "row", None, "head"),
        check_vma=False,
    )
```

```python
import functools
import math

import jax
import jax.numpy as jnp
from jax import lax
from jax.experimental import pallas as pl
from jax.experimental.pallas import tpu as pltpu
from jax.sharding import PartitionSpec as P

HD = 512
ATT_HD = 128
HALO = 2
PER = 8
SKIP = 4
DIRECT = 2
LAGS = (9, 8)
LEADS = (24, 24)
MESH = pl.DeviceIdType.MESH
BF16 = jnp.bfloat16
F32 = jnp.float32
NT = (((1,), (1,)), ((), ()))
TN = (((0,), (0,)), ((), ()))


def with_halo(value, sides, width):
    for axis, dim in sides:
        size, length = (lax.axis_size(axis), value.shape[dim])
        up = [(i, (i + 1) % size) for i in range(size - 1)]
        down = [(j, i) for i, j in up]
        last = lax.slice_in_dim(value, length - width, length, axis=dim)
        leading = lax.slice_in_dim(value, 0, width, axis=dim)
        before = lax.ppermute(last, axis, up)
        after = lax.ppermute(leading, axis, down)
        value = jnp.concatenate([before, value, after], axis=dim)
    return value


def silu_slope(values_in):
    sigmoid_x = jax.nn.sigmoid(values_in)
    return sigmoid_x * (1.0 + values_in * (1.0 - sigmoid_x))


def attend(
    query_rows,
    key_rows,
    value_rows,
    q_row_ids,
    k_row_ids,
    q_tok,
    k_tok,
    k_valid,
    q_reach,
    grid_rows,
):
    count_q = query_rows.shape[0]
    count_k = key_rows.shape[0]
    groups = query_rows.shape[1] // ATT_HD
    query_heads = query_rows.reshape(count_q, groups, ATT_HD)
    key_heads = key_rows.reshape(count_k, groups, ATT_HD)
    value_heads = value_rows.reshape(count_k, groups, ATT_HD)
    scores = jnp.einsum(
        "qhd,khd->hqk", query_heads, key_heads, preferred_element_type=jnp.float32
    ) / math.sqrt(ATT_HD)
    inside = (k_row_ids >= 0) & (k_row_ids < grid_rows)
    in_band = jnp.abs(k_row_ids[None, :] - q_row_ids[:, None]) <= q_reach[:, None]
    allowed = in_band & inside[None, :] & (k_valid[None, :] | (k_tok[None, :] == q_tok[:, None]))
    scores = jnp.where(allowed[None], scores, -1e30)
    row_top = jnp.max(scores, -1, keepdims=True)
    powers = jnp.exp(scores - row_top)
    weights = (powers / jnp.sum(powers, -1, keepdims=True)).astype(jnp.bfloat16)
    output_rows = jnp.einsum(
        "hqk,khd->qhd", weights, value_heads, preferred_element_type=jnp.float32
    )
    return output_rows.reshape(count_q, groups * ATT_HD).astype(jnp.bfloat16)


def renorm(old_matrix, grad, total_valid):
    old_rows = old_matrix.astype(jnp.float32)
    raised = old_rows + grad / total_valid
    rescale = jnp.sqrt(jnp.sum(old_rows * old_rows, -1, keepdims=True) + 1e-06) / jnp.sqrt(
        jnp.sum(raised * raised, -1, keepdims=True) + 1e-06
    )
    return (raised * rescale).astype(jnp.bfloat16)


def per_device(
    query_feats,
    key_feats,
    value_feats,
    target,
    token_rates,
    row_reach,
    view_counts,
    w_first,
    w_third,
    w_second,
):
    row_count = query_feats.shape[1]
    col_count = query_feats.shape[2]
    feat_width = query_feats.shape[3]
    heads_here = feat_width // HD
    tokens_here = row_count * col_count
    key_span = row_count + 2 * HALO
    grid_rows = lax.axis_size("row") * row_count
    row_base = lax.axis_index("row") * row_count
    view_total = view_counts[0]
    total_valid = lax.psum(view_total.astype(jnp.float32), "view")
    paired = jnp.stack([key_feats[0], value_feats[0]], 0)
    padded = with_halo(paired, (("row", 1),), HALO)
    q_row_ids = row_base + jnp.repeat(jnp.arange(row_count, dtype=jnp.int32), col_count)
    k_row_ids = row_base - HALO + jnp.repeat(jnp.arange(key_span, dtype=jnp.int32), col_count)
    q_tok = q_row_ids * col_count + jnp.tile(jnp.arange(col_count, dtype=jnp.int32), row_count)
    k_tok = k_row_ids * col_count + jnp.tile(jnp.arange(col_count, dtype=jnp.int32), key_span)
    k_valid = k_tok < view_total
    q_reach = jnp.repeat(row_reach, col_count)
    attended = attend(
        query_feats[0].reshape(tokens_here, feat_width),
        padded[0].reshape(key_span * col_count, feat_width),
        padded[1].reshape(key_span * col_count, feat_width),
        q_row_ids,
        k_row_ids,
        q_tok,
        k_tok,
        k_valid,
        q_reach,
        grid_rows,
    )
    attended = attended.reshape(tokens_here, heads_here, HD).astype(jnp.float32)
    fast_keys = (
        attended * lax.rsqrt(jnp.mean(attended * attended, -1, keepdims=True) + 1e-06)
    ).astype(jnp.bfloat16)
    valid_mask = (q_tok < view_total).astype(jnp.float32)
    rates_tok = token_rates[0].T
    scaled = (
        rates_tok[:, :, None]
        * valid_mask[:, None, None]
        * target[0].reshape(tokens_here, heads_here, HD).astype(jnp.float32)
    ).astype(jnp.bfloat16)
    first_proj = jnp.einsum("thi,hij->thj", fast_keys, w_first, preferred_element_type=jnp.float32)
    third_proj = jnp.einsum("thi,hij->thj", fast_keys, w_third, preferred_element_type=jnp.float32)
    gated_rows = (jax.nn.silu(first_proj) * third_proj).astype(jnp.bfloat16)
    back_rows = jnp.einsum("tho,hjo->thj", scaled, w_second, preferred_element_type=jnp.float32)
    back_first = (back_rows * third_proj * silu_slope(first_proj)).astype(jnp.bfloat16)
    back_third = (back_rows * jax.nn.silu(first_proj)).astype(jnp.bfloat16)
    grad_first = jnp.einsum(
        "thi,thj->hij", fast_keys, back_first, preferred_element_type=jnp.float32
    )
    grad_third = jnp.einsum(
        "thi,thj->hij", fast_keys, back_third, preferred_element_type=jnp.float32
    )
    grad_second = jnp.einsum("thj,tho->hjo", gated_rows, scaled, preferred_element_type=jnp.float32)
    grad_first, grad_third, grad_second = lax.psum(
        (grad_first, grad_third, grad_second), ("view", "row")
    )
    new_first = renorm(w_first, grad_first, total_valid)
    new_third = renorm(w_third, grad_third, total_valid)
    new_second = renorm(w_second, grad_second, total_valid)
    applied = (
        jax.nn.silu(
            jnp.einsum("thi,hij->thj", fast_keys, new_first, preferred_element_type=jnp.float32)
        )
        * jnp.einsum("thi,hij->thj", fast_keys, new_third, preferred_element_type=jnp.float32)
    ).astype(jnp.bfloat16)
    fast_out = jnp.einsum(
        "thj,hjo->tho", applied, new_second, preferred_element_type=jnp.float32
    ).astype(jnp.bfloat16)
    return fast_out.reshape(1, row_count, col_count, feat_width)


def halve(values_in, size):
    if size & (size - 1) == 0:
        return values_in >> (size.bit_length() - 1)
    return lax.div(values_in, jnp.int32(size))


def dot(left, right, dims=(((1,), (0,)), ((), ()))):
    return lax.dot_general(left, right, dims, preferred_element_type=F32)


def flip(index, bits):
    bit = 1
    while bit <= bits:
        if bits & bit:
            index = index + bit - 2 * bit * lax.rem(lax.div(index, bit), 2)
        bit *= 2
    return index


def step_kernel(
    nr, nz, cols,
    q_hbm, k_hbm, v_hbm, t_hbm, rates_hbm, reach_hbm, count_hbm, wf_hbm, wt_hbm, ws_hbm,
    out_ref,
    q_ref, kv_ref, t_ref, rates_ref, reach_ref, count_ref, wft, ws, halo, raw, sall, cnt, gout, gside, gslant, gfull, gsum, gin, gtot,
    wold, news, ss,
    load_sem, row_send, row_recv, halo_recv, k_recv, view_send, side_recv, total_recv, near_recv, far_recv, on_recv,
):
    tokens, width = q_ref.shape
    rows_here = tokens // cols
    hid = width // nr
    edge = HALO * cols
    heads = width // ATT_HD
    pieces = total_recv.shape[0]
    piece = 3 * hid // pieces
    per = pieces // 3
    me = lax.axis_index("row")
    mz = lax.axis_index("view")
    partner, across = flip(me, 1), flip(me, 2)
    above, below = me + 1, me - 1
    mine = pl.ds(pl.multiple_of(me * hid, hid), hid)
    theirs = pl.ds(pl.multiple_of(across * hid, hid), hid)
    low = mz < nz // 2
    inner = jnp.where(low, mz + 1, mz - 1)
    outer = jnp.where(low, mz - 1, mz + 1)
    center = (mz > 0) & (mz < nz - 1)
    leaf = (mz == 0) | (mz == nz - 1)
    has_above = me < nr - 1
    has_below = me > 0

    barrier = pltpu.get_barrier_semaphore()
    for d in range(1, nr):
        pl.semaphore_signal(barrier, inc=1, device_id={"row": flip(me, d)}, device_id_type=MESH)
    pl.semaphore_signal(barrier, inc=1, device_id={"view": inner}, device_id_type=MESH)

    slant = jnp.where(center, outer, inner)
    pl.semaphore_signal(barrier, inc=1, device_id={"row": across, "view": slant}, device_id_type=MESH)

    @pl.when(center)
    def _():
        pl.semaphore_signal(barrier, inc=1, device_id={"view": outer}, device_id_type=MESH)

    loads = [
        pltpu.make_async_copy(source, target, load_sem.at[max(min(i, 7) if i < 11 else 8, 1) - 1])
        for i, (source, target) in enumerate((
            (k_hbm, kv_ref.at[0]), (v_hbm, kv_ref.at[1]), (count_hbm, count_ref), (reach_hbm, reach_ref),
            (t_hbm, t_ref), (rates_hbm, rates_ref), (q_hbm, q_ref),
            (wf_hbm.at[:, theirs], wft.at[:, pl.ds(0, hid)]), (wt_hbm.at[:, theirs], wft.at[:, pl.ds(hid, hid)]),
            (wf_hbm.at[:, mine], wft.at[:, pl.ds(2 * hid, hid)]), (wt_hbm.at[:, mine], wft.at[:, pl.ds(3 * hid, hid)]),
            (ws_hbm.at[theirs, :], ws.at[pl.ds(0, hid)]), (ws_hbm.at[mine, :], ws.at[pl.ds(hid, hid)]),
        ))
    ]
    for load in loads:
        load.start()

    def remote(source, target, sends, receives, axis, peer):
        return pltpu.make_async_remote_copy(
            src_ref=source, dst_ref=target, send_sem=sends, recv_sem=receives,
            device_id={axis: peer}, device_id_type=MESH,
        )

    @pl.when(me == 0)
    def _():
        halo[:, :edge] = jnp.zeros((2, edge, width), BF16)

    @pl.when(me == nr - 1)
    def _():
        halo[:, edge:] = jnp.zeros((2, edge, width), BF16)

    row_base = me * rows_here
    tok_base = me * tokens

    pl.semaphore_wait(barrier, nr + 1 + jnp.where(center, 1, 0))

    @pl.when(has_above)
    def _():
        for i, source in enumerate((k_hbm, v_hbm)):
            remote(
                source.at[pl.ds(tokens - edge, edge)], halo.at[i, pl.ds(0, edge)], row_send.at[0], halo_recv.at[0, i], "row", above
            ).start()

    @pl.when(has_below)
    def _():
        for i, source in enumerate((k_hbm, v_hbm)):
            remote(
                source.at[pl.ds(0, edge)], halo.at[i, pl.ds(edge, edge)], row_send.at[1], halo_recv.at[1, i], "row", below
            ).start()

    up_halo = remote(halo.at[:, pl.ds(edge, edge)], halo.at[:, pl.ds(0, edge)], row_send.at[0], row_recv.at[0], "row", above)
    down_halo = remote(halo.at[:, pl.ds(0, edge)], halo.at[:, pl.ds(edge, edge)], row_send.at[1], row_recv.at[1], "row", below)

    for load in loads[2:4]:
        load.wait()
    view_total = count_ref[0]
    cnt[0] = jnp.full((8, 128), view_total, jnp.int32).astype(F32)
    sub = lax.broadcasted_iota(jnp.int32, (tokens, tokens), 0)
    lane = lax.broadcasted_iota(jnp.int32, (tokens, tokens), 1)
    tok_col = tok_base + lax.broadcasted_iota(jnp.int32, (tokens, 1), 0)
    valid_col = (tok_col < view_total).astype(F32)
    for load in loads[4:6]:
        load.wait()
    rate_col = jnp.sum(jnp.where(sub == lane, rates_ref[...], 0.0), axis=1, keepdims=True)
    sall[0] = (rate_col * valid_col * t_ref[...].astype(F32)).astype(BF16)
    s_near = remote(sall.at[0], sall.at[1], row_send.at[2], row_recv.at[0], "row", partner)
    s_near.start()
    cnt_up = remote(cnt.at[0], cnt.at[1], view_send.at[0], row_recv.at[1], "view", inner)
    cnt_mid = remote(cnt.at[2], cnt.at[3], view_send.at[0], row_recv.at[2], "view", inner)
    cnt_down = remote(cnt.at[3], cnt.at[3], view_send.at[1], row_recv.at[2], "view", outer)

    @pl.when(leaf)
    def _():
        cnt_up.start()

    def allowed(q_tok, k_tok):
        q_row = halve(q_tok, cols)
        k_row = halve(k_tok + edge, cols) - HALO
        reach = jnp.zeros(q_tok.shape, jnp.int32)
        for r in range(rows_here):
            reach = jnp.where(q_row == r, reach_ref[r], reach)
        k_abs = k_row + row_base
        return (
            (jnp.abs(k_row - q_row) <= reach)
            & (k_abs >= 0)
            & (k_abs < nr * rows_here)
            & ((k_tok + tok_base < view_total) | (k_tok == q_tok))
        )

    near_ok = allowed(sub, lane)
    far_q = lax.broadcasted_iota(jnp.int32, (2 * edge, 2 * edge), 0)
    far_k = lax.broadcasted_iota(jnp.int32, (2 * edge, 2 * edge), 1)
    far_ok = allowed(
        jnp.where(far_q < edge, far_q, far_q - 2 * edge + tokens),
        jnp.where(far_k < edge, far_k - edge, far_k - edge + tokens),
    )
    root = 1.0 / math.sqrt(ATT_HD)
    spans = [slice(h * ATT_HD, (h + 1) * ATT_HD) for h in range(heads)]
    pltpu.make_async_copy(kv_ref, kv_ref, load_sem.at[0]).wait()
    loads[6].wait()
    inside = slice(edge, tokens - edge)
    ends = (slice(0, edge), slice(tokens - edge, tokens))

    def outer_rows(value):
        return jnp.concatenate([value[e] for e in ends], axis=0)

    def pass_keys(at, receives):
        return remote(raw.at[0, :, at], raw.at[1, :, at], row_send.at[2], receives, "row", partner)

    near = []
    for h, hs in enumerate(spans):
        scores = jnp.where(near_ok, dot(q_ref[:, hs], kv_ref[0, :, hs], NT) * root, -1e30)
        top = jnp.max(scores, axis=-1, keepdims=True)
        power = jnp.exp(scores - top)
        total = jnp.sum(power, axis=-1, keepdims=True)
        mix = dot(power.astype(BF16), kv_ref[1, :, hs])
        raw[0, h, inside] = (mix[inside] * (1.0 / total[inside])).astype(BF16)
        near.append((outer_rows(top), outer_rows(total), outer_rows(mix), outer_rows(q_ref.at[:, hs])))
    middle = pass_keys(pl.ds(edge, tokens - 2 * edge), k_recv.at[0])
    middle.start()
    pltpu.make_async_copy(wft, wft, load_sem.at[6]).wait()
    pltpu.make_async_copy(ws, ws, load_sem.at[7]).wait()
    def halo_here(i):
        @pl.when(has_below)
        def _():
            remote(halo.at[i, pl.ds(edge, edge)], halo.at[i, pl.ds(0, edge)], row_send.at[0], halo_recv.at[0, i], "row", above).wait_recv()

        @pl.when(has_above)
        def _():
            remote(halo.at[i, pl.ds(0, edge)], halo.at[i, pl.ds(edge, edge)], row_send.at[1], halo_recv.at[1, i], "row", below).wait_recv()

    def keys_of(d, rows_at):
        return jnp.concatenate(
            [jnp.concatenate([raw[d, h, at] for h in range(heads)], axis=1) for at in rows_at], axis=0
        )

    def token_norm(keys):
        total_sq = jnp.zeros((keys.shape[0], ATT_HD), F32)
        for hs in spans:
            part = keys[:, hs].astype(F32)
            total_sq = total_sq + part * part
        return lax.rsqrt(jnp.sum(total_sq, axis=-1, keepdims=True) * (1.0 / width) + 1e-06)

    def block(keys, steps, norm, half):
        both = dot(keys, wft[:, half * 2 * hid:(half + 1) * 2 * hid])
        back = dot(steps, ws[half * hid:(half + 1) * hid], NT)
        first = both[:, :hid] * norm
        third = both[:, hid:] * norm
        sig = jax.nn.sigmoid(first)
        gate = first * sig
        pulled = back * norm
        left = jnp.concatenate(
            [
                (pulled * third * (sig * (1.0 + first * (1.0 - sig)))).astype(BF16),
                (pulled * gate).astype(BF16),
            ],
            axis=1,
        )
        return left, (gate * third).astype(BF16)

    def token_set(rows_at):
        keys = jnp.concatenate([keys_of(d, rows_at) for d in range(2)], axis=0)
        steps = jnp.concatenate([sall[d, at] for d in range(2) for at in rows_at], axis=0)
        return keys, steps, token_norm(keys)

    s_near.wait_recv()
    middle.wait_recv()
    inner_set = token_set((inside,))
    inner_blocks = [block(*inner_set, half) for half in range(2)]
    halo_here(0)
    partly = []
    for h, hs in enumerate(spans):
        near_top, near_sum, near_out, queries = near[h]
        far = jnp.where(far_ok, dot(queries, halo[0, :, hs], NT) * root, -1e30)
        top = jnp.maximum(near_top, jnp.max(far, axis=-1, keepdims=True))
        power = jnp.exp(far - top)
        keep = jnp.exp(near_top - top)
        inverse = 1.0 / (keep * near_sum + jnp.sum(power, axis=-1, keepdims=True))
        partly.append((power.astype(BF16), keep * near_out, inverse))
    halo_here(1)
    for h, hs in enumerate(spans):
        power, kept, inverse = partly[h]
        mix = ((kept + dot(power, halo[1, :, hs])) * inverse).astype(BF16)
        raw[0, h, ends[0]] = mix[:edge]
        raw[0, h, ends[1]] = mix[edge:]
    for e in ends:
        pass_keys(pl.ds(e.start, edge), k_recv.at[1]).start()

    def rows(i):
        return pl.ds(i * piece, piece)

    def skew(i):
        return pltpu.make_async_remote_copy(
            src_ref=gout.at[rows(i)], dst_ref=gslant.at[rows(i)], send_sem=row_send.at[4], recv_sem=side_recv.at[i],
            device_id={"row": across, "view": inner}, device_id_type=MESH,
        )

    def early(i):
        return remote(gsum.at[rows(i)], gin.at[rows(i)], view_send.at[2], side_recv.at[i], "view", inner)

    def aside(i):
        return remote(gout.at[rows(i)], gside.at[rows(i)], row_send.at[4], side_recv.at[i], "row", across)

    @pl.when(center)
    def _():
        cnt_up.wait_recv()
        cnt[2] = cnt[0] + cnt[1]
        cnt_mid.start()

    inner_left, inner_gated = inner_blocks[0]
    gfull[: 2 * hid] = dot(inner_left, inner_set[0], TN)
    gfull[2 * hid:] = dot(inner_gated, inner_set[1], TN)
    pass_keys(pl.ds(0, 2 * edge), k_recv.at[1]).wait_recv()
    outer_set = token_set(ends)
    left, gated = block(*outer_set, 0)
    for m in range(2):
        at = slice(m * hid, (m + 1) * hid)
        gout[at] = (gfull[at] + dot(left[:, at], outer_set[0], TN)).astype(BF16)
        if m == 0:
            @pl.when(leaf)
            def _():
                for i in range(SKIP):
                    skew(i).start()

            @pl.when(center)
            def _():
                for i in range(SKIP):
                    aside(i).start()

        for i in range(SKIP if m == 0 else per, (m + 1) * per):
            aside(i).start()
    gout[2 * hid:] = (gfull[2 * hid:] + dot(gated, outer_set[1], TN)).astype(BF16)
    for i in range(2 * per, 3 * per):
        aside(i).start()
    keys, steps = (jnp.concatenate(pair, axis=0) for pair in zip(inner_set[:2], outer_set[:2]))
    left, gated = (jnp.concatenate(pair, axis=0) for pair in zip(inner_blocks[1], block(*outer_set, 1)))
    gfull[: 2 * hid] = dot(left, keys, TN)

    @pl.when(leaf)
    def _():
        for i in range(SKIP):
            gsum[rows(i)] = gfull[rows(i)].astype(BF16)
            early(i).start()

    gfull[2 * hid:] = dot(gated, steps, TN)

    @pl.when(center)
    def _():
        cnt_mid.wait_recv()
        cnt[3] = cnt[2] + cnt[3]
        cnt_down.start()

    wold[0:hid] = wft[:, 2 * hid:3 * hid].astype(F32).T
    wold[hid:2 * hid] = wft[:, 3 * hid:].astype(F32).T
    wold[2 * hid:] = ws[hid:].astype(F32)
    ss[0, 2:3] = jnp.sum(wold[:hid] * wold[:hid], axis=0, keepdims=True)
    ss[0, 3:4] = jnp.sum(wold[hid:2 * hid] * wold[hid:2 * hid], axis=0, keepdims=True)
    second_old = wold[2 * hid:]
    second_size = jnp.sqrt(jnp.sum(second_old * second_old, axis=-1, keepdims=True) + 1e-06)

    def here(i, count):
        at = gin.at[pl.ds(0, count * piece)]
        return remote(at, at, view_send.at[2], side_recv.at[i], "view", inner)

    def rise(i, target, receives):
        return remote(gsum.at[rows(i)], target.at[rows(i)], view_send.at[2], receives.at[i], "view", inner)

    def fall(i):
        return remote(gtot.at[rows(i)], gtot.at[rows(i)], view_send.at[3], total_recv.at[i], "view", outer)

    def lift(i):
        if i < SKIP:
            return
        aside(i).wait_recv()
        gsum[rows(i)] = (gfull[rows(i)] + gside[rows(i)].astype(F32)).astype(BF16)
        rise(i, gin, side_recv).start()

    def join(i):
        here(i, 3 if i < SKIP else 2).wait_recv()
        partial = gfull[rows(i)] + gside[rows(i)].astype(F32)
        if i < SKIP:
            partial = partial + gslant[rows(i)].astype(F32)
        gsum[rows(i)] = (partial + gin[rows(i)].astype(F32)).astype(BF16)
        rise(i, gtot, total_recv).start()

    def finish(i):
        rise(i, gtot, total_recv).wait_recv()
        gtot[rows(i)] = (gsum[rows(i)].astype(F32) + gtot[rows(i)].astype(F32)).astype(BF16)
        fall(i).start()

    roles = (
        (low & center, join, finish, LAGS[0]),
        (~low & center, join, finish, LAGS[1]),
        (low & leaf, lift, None, LEADS[0]),
        (~low & leaf, lift, None, LEADS[1]),
    )
    for role, begin, _, ahead in roles:
        @pl.when(role)
        def _():
            for i in range(ahead):
                begin(i)
            if begin is lift:
                cnt_down.wait_recv()

    share_total = 1.0 / cnt[3, 0:1, 0:1]

    def arrive(i):
        for role, begin, end, ahead in roles:
            @pl.when(role)
            def _():
                if i + ahead < pieces:
                    begin(i + ahead)
                if end is None:
                    fall(i).wait_recv()
                else:
                    end(i)

    def raise_rows(i):
        raised = wold[rows(i)] + gtot[rows(i)].astype(F32) * share_total
        if i < 2 * per:
            news[0, rows(i)] = raised.astype(BF16)
            return jnp.sum(raised * raised, axis=0, keepdims=True)
        at = (i - 2 * per) * piece
        size = jnp.sqrt(jnp.sum(raised * raised, axis=-1, keepdims=True) + 1e-06)
        news[0, rows(i)] = (raised * (second_size[at:at + piece] / size)).astype(BF16)

    groups = [(0, per), (per, 2 * per), (2 * per, 3 * per - DIRECT), (3 * per - DIRECT, 3 * per)]

    def span(group):
        return pl.ds(group[0] * piece, (group[1] - group[0]) * piece)

    def group_of(i):
        return [g for g, group in enumerate(groups) if group[0] <= i < group[1]][0]

    def lend(i):
        return remote(news.at[0, rows(i)], news.at[2, rows(i)], row_send.at[4], far_recv.at[min(group_of(i), 3)], "row", across)

    def lend_over(i):
        return remote(news.at[0, rows(i)], news.at[3, rows(i)], row_send.at[4], on_recv.at[1], "row", flip(me, 3))

    def pair(g, slot, receives, sends=4):
        return remote(
            news.at[slot, span(groups[g])], news.at[slot + 1, span(groups[g])], row_send.at[sends], receives.at[g // 2 if g < 2 else 1], "row", partner
        )

    def parts_here(part, slot, receives):
        at = pl.ds(part * 2 * hid, (2 - part) * hid)
        remote(news.at[slot, at], news.at[slot + 1, at], row_send.at[4], receives.at[part], "row", partner).wait_recv()

    def relay(g):
        remote(
            news.at[0, span(groups[g])], news.at[2, span(groups[g])], row_send.at[4], far_recv.at[g], "row", across
        ).wait_recv()
        pair(g, 2, on_recv).start()

    ss_copies = [
        remote(ss.at[0], ss.at[d], row_send.at[3], row_recv.at[3], "row", flip(me, d)) for d in range(1, nr)
    ]
    for i in range(pieces):
        arrive(i)
        square = raise_rows(i)
        lend(i).start()
        if group_of(i) > 2:
            lend_over(i).start()
        for g, group in enumerate(groups):
            if group[1] == i + 1:
                pair(g, 0, near_recv).start()
        if i < 2 * per:
            running = square if i % per == 0 else running + square
            if i % per == per - 1:
                m = i // per
                ss[0, m:m + 1] = running
                if m == 1:
                    for copy in ss_copies:
                        copy.start()
    relay(0)
    relay(1)
    remote(ss.at[pl.ds(0, nr - 1)], ss.at[pl.ds(1, nr - 1)], row_send.at[3], row_recv.at[3], "row", partner).wait_recv()
    sums = ss[0]
    for d in range(1, nr):
        sums = sums + ss[d]
    scales = jnp.sqrt(sums[2:4] + 1e-06) / jnp.sqrt(sums[0:2] + 1e-06)
    own_keys = keys_of(0, (slice(0, tokens),))
    own_norm = token_norm(own_keys)
    wide = own_keys.astype(F32)
    scaled = [(wide * scales[m:m + 1]).astype(BF16) for m in range(2)]

    def apply(slot):
        first = dot(scaled[0], news[slot, :hid], NT) * own_norm
        third = dot(scaled[1], news[slot, hid:2 * hid], NT) * own_norm
        return (first * jax.nn.sigmoid(first) * third).astype(BF16)

    applied = [apply(0)]
    parts_here(0, 0, near_recv)
    applied.append(apply(1))
    applied.append(apply(2))
    relay(2)
    parts_here(0, 2, on_recv)
    applied.append(apply(3))
    total = dot(applied[0], news[0, 2 * hid:])
    parts_here(1, 0, near_recv)
    total = total + dot(applied[1], news[1, 2 * hid:])
    lent = span((groups[3][0], pieces))
    remote(news.at[0, lent], news.at[2, lent], row_send.at[4], far_recv.at[3], "row", across).wait_recv()
    total = total + dot(applied[2], news[2, 2 * hid:])
    parts_here(1, 2, on_recv)
    total = total + dot(applied[3], news[3, 2 * hid:])
    out_ref[...] = total.astype(BF16)

    @pl.when(has_above)
    def _():
        up_halo.wait_send()

    @pl.when(has_below)
    def _():
        down_halo.wait_send()

    remote(kv_ref, kv_ref, row_send.at[2], row_recv.at[0], "row", partner).wait_send()
    remote(news, news, row_send.at[4], row_recv.at[0], "row", partner).wait_send()
    remote(ss.at[pl.ds(0, nr - 1)], ss.at[pl.ds(1, nr - 1)], row_send.at[3], row_recv.at[3], "row", partner).wait_send()
    remote(gsum, gin, view_send.at[2], row_recv.at[0], "view", inner).wait_send()
    cnt_up.wait_send()

    @pl.when(center)
    def _():
        cnt_down.wait_send()
        remote(gtot, gtot, view_send.at[3], row_recv.at[0], "view", outer).wait_send()


def fused_step(
    nr, nz,
    query_feats, key_feats, value_feats, target, token_rates, row_reach, view_counts,
    w_first, w_third, w_second,
):
    _, row_count, cols, width = query_feats.shape
    tokens = row_count * cols
    hid = width // nr
    edge = HALO * cols
    heads = width // ATT_HD
    pieces = 3 * PER
    anywhere = pl.BlockSpec(memory_space=pl.ANY)
    flat = lambda a: a.reshape(tokens, width)
    out = pl.pallas_call(
        functools.partial(step_kernel, nr, nz, cols),
        out_shape=pltpu.VMEM((tokens, width), BF16),
        in_specs=[anywhere] * 5 + [pl.BlockSpec(memory_space=pltpu.HBM)] * 2 + [anywhere] * 3,
        out_specs=pl.BlockSpec(memory_space=pltpu.VMEM),
        scratch_shapes=[
            pltpu.VMEM((tokens, width), BF16),
            pltpu.VMEM((2, tokens, width), BF16),
            pltpu.VMEM((tokens, width), BF16),
            pltpu.VMEM((1, tokens), F32),
            pltpu.SMEM((row_count,), jnp.int32),
            pltpu.SMEM((1,), jnp.int32),
            pltpu.VMEM((width, 4 * hid), BF16),
            pltpu.VMEM((2 * hid, width), BF16),
            pltpu.VMEM((2, 2 * edge, width), BF16),
            pltpu.VMEM((2, heads, tokens, ATT_HD), BF16),
            pltpu.VMEM((2, tokens, width), BF16),
            pltpu.VMEM((4, 8, 128), F32),
            pltpu.VMEM((3 * hid, width), BF16),
            pltpu.VMEM((3 * hid, width), BF16),
            pltpu.VMEM((3 * hid, width), BF16),
            pltpu.VMEM((3 * hid, width), F32),
            pltpu.VMEM((3 * hid, width), BF16),
            pltpu.VMEM((3 * hid, width), BF16),
            pltpu.VMEM((3 * hid, width), BF16),
            pltpu.VMEM((3 * hid, width), F32),
            pltpu.VMEM((nr, 3 * hid, width), BF16),
            pltpu.VMEM((nr, 4, width), F32),
            pltpu.SemaphoreType.DMA((8,)),
            pltpu.SemaphoreType.DMA((5,)),
            pltpu.SemaphoreType.DMA((4,)),
            pltpu.SemaphoreType.DMA((2, 2)),
            pltpu.SemaphoreType.DMA((2,)),
            pltpu.SemaphoreType.DMA((4,)),
            pltpu.SemaphoreType.DMA((pieces,)),
            pltpu.SemaphoreType.DMA((pieces,)),
            pltpu.SemaphoreType.DMA((2,)),
            pltpu.SemaphoreType.DMA((4,)),
            pltpu.SemaphoreType.DMA((2,)),
        ],
        compiler_params=pltpu.CompilerParams(collective_id=0, has_side_effects=True),
    )(
        flat(query_feats), flat(key_feats), flat(value_feats), flat(target),
        token_rates.reshape(1, tokens), row_reach, view_counts,
        w_first.reshape(width, width), w_third.reshape(width, width), w_second.reshape(width, width),
    )
    return out.reshape(query_feats.shape)


def solution(mesh):
    placed = (
        P("view", "row", None, "head"),
        P("view", "row", None, "head"),
        P("view", "row", None, "head"),
        P("view", "row", None, "head"),
        P("view", "head", "row"),
        P("row"),
        P("view"),
        P("head", None, None),
        P("head", None, None),
        P("head", None, None),
    )
    nr, nz = mesh.shape["row"], mesh.shape["view"]
    fits = nr == 4 and nz == 4 and HD % (128 * nr) == 0 and HD % (16 * nr * PER) == 0
    return jax.shard_map(
        functools.partial(fused_step, nr, nz) if fits else per_device,
        mesh=mesh,
        in_specs=placed,
        out_specs=P("view", "row", None, "head"),
        check_vma=False,
    )
```

```python
import functools
import math

import jax
import jax.numpy as jnp
from jax import lax
from jax.experimental import pallas as pl
from jax.experimental.pallas import tpu as pltpu
from jax.sharding import PartitionSpec as P

HD = 512
ATT_HD = 128
HALO = 2
PER = 8
SKIP = 3
DIRECT = 2
LAGS = (9, 8)
LEADS = (24, 24)
MESH = pl.DeviceIdType.MESH
BF16 = jnp.bfloat16
F32 = jnp.float32
NT = (((1,), (1,)), ((), ()))
TN = (((0,), (0,)), ((), ()))


def with_halo(value, sides, width):
    for axis, dim in sides:
        size, length = (lax.axis_size(axis), value.shape[dim])
        up = [(i, (i + 1) % size) for i in range(size - 1)]
        down = [(j, i) for i, j in up]
        last = lax.slice_in_dim(value, length - width, length, axis=dim)
        leading = lax.slice_in_dim(value, 0, width, axis=dim)
        before = lax.ppermute(last, axis, up)
        after = lax.ppermute(leading, axis, down)
        value = jnp.concatenate([before, value, after], axis=dim)
    return value


def silu_slope(values_in):
    sigmoid_x = jax.nn.sigmoid(values_in)
    return sigmoid_x * (1.0 + values_in * (1.0 - sigmoid_x))


def attend(
    query_rows,
    key_rows,
    value_rows,
    q_row_ids,
    k_row_ids,
    q_tok,
    k_tok,
    k_valid,
    q_reach,
    grid_rows,
):
    count_q = query_rows.shape[0]
    count_k = key_rows.shape[0]
    groups = query_rows.shape[1] // ATT_HD
    query_heads = query_rows.reshape(count_q, groups, ATT_HD)
    key_heads = key_rows.reshape(count_k, groups, ATT_HD)
    value_heads = value_rows.reshape(count_k, groups, ATT_HD)
    scores = jnp.einsum(
        "qhd,khd->hqk", query_heads, key_heads, preferred_element_type=jnp.float32
    ) / math.sqrt(ATT_HD)
    inside = (k_row_ids >= 0) & (k_row_ids < grid_rows)
    in_band = jnp.abs(k_row_ids[None, :] - q_row_ids[:, None]) <= q_reach[:, None]
    allowed = in_band & inside[None, :] & (k_valid[None, :] | (k_tok[None, :] == q_tok[:, None]))
    scores = jnp.where(allowed[None], scores, -1e30)
    row_top = jnp.max(scores, -1, keepdims=True)
    powers = jnp.exp(scores - row_top)
    weights = (powers / jnp.sum(powers, -1, keepdims=True)).astype(jnp.bfloat16)
    output_rows = jnp.einsum(
        "hqk,khd->qhd", weights, value_heads, preferred_element_type=jnp.float32
    )
    return output_rows.reshape(count_q, groups * ATT_HD).astype(jnp.bfloat16)


def renorm(old_matrix, grad, total_valid):
    old_rows = old_matrix.astype(jnp.float32)
    raised = old_rows + grad / total_valid
    rescale = jnp.sqrt(jnp.sum(old_rows * old_rows, -1, keepdims=True) + 1e-06) / jnp.sqrt(
        jnp.sum(raised * raised, -1, keepdims=True) + 1e-06
    )
    return (raised * rescale).astype(jnp.bfloat16)


def per_device(
    query_feats,
    key_feats,
    value_feats,
    target,
    token_rates,
    row_reach,
    view_counts,
    w_first,
    w_third,
    w_second,
):
    row_count = query_feats.shape[1]
    col_count = query_feats.shape[2]
    feat_width = query_feats.shape[3]
    heads_here = feat_width // HD
    tokens_here = row_count * col_count
    key_span = row_count + 2 * HALO
    grid_rows = lax.axis_size("row") * row_count
    row_base = lax.axis_index("row") * row_count
    view_total = view_counts[0]
    total_valid = lax.psum(view_total.astype(jnp.float32), "view")
    paired = jnp.stack([key_feats[0], value_feats[0]], 0)
    padded = with_halo(paired, (("row", 1),), HALO)
    q_row_ids = row_base + jnp.repeat(jnp.arange(row_count, dtype=jnp.int32), col_count)
    k_row_ids = row_base - HALO + jnp.repeat(jnp.arange(key_span, dtype=jnp.int32), col_count)
    q_tok = q_row_ids * col_count + jnp.tile(jnp.arange(col_count, dtype=jnp.int32), row_count)
    k_tok = k_row_ids * col_count + jnp.tile(jnp.arange(col_count, dtype=jnp.int32), key_span)
    k_valid = k_tok < view_total
    q_reach = jnp.repeat(row_reach, col_count)
    attended = attend(
        query_feats[0].reshape(tokens_here, feat_width),
        padded[0].reshape(key_span * col_count, feat_width),
        padded[1].reshape(key_span * col_count, feat_width),
        q_row_ids,
        k_row_ids,
        q_tok,
        k_tok,
        k_valid,
        q_reach,
        grid_rows,
    )
    attended = attended.reshape(tokens_here, heads_here, HD).astype(jnp.float32)
    fast_keys = (
        attended * lax.rsqrt(jnp.mean(attended * attended, -1, keepdims=True) + 1e-06)
    ).astype(jnp.bfloat16)
    valid_mask = (q_tok < view_total).astype(jnp.float32)
    rates_tok = token_rates[0].T
    scaled = (
        rates_tok[:, :, None]
        * valid_mask[:, None, None]
        * target[0].reshape(tokens_here, heads_here, HD).astype(jnp.float32)
    ).astype(jnp.bfloat16)
    first_proj = jnp.einsum("thi,hij->thj", fast_keys, w_first, preferred_element_type=jnp.float32)
    third_proj = jnp.einsum("thi,hij->thj", fast_keys, w_third, preferred_element_type=jnp.float32)
    gated_rows = (jax.nn.silu(first_proj) * third_proj).astype(jnp.bfloat16)
    back_rows = jnp.einsum("tho,hjo->thj", scaled, w_second, preferred_element_type=jnp.float32)
    back_first = (back_rows * third_proj * silu_slope(first_proj)).astype(jnp.bfloat16)
    back_third = (back_rows * jax.nn.silu(first_proj)).astype(jnp.bfloat16)
    grad_first = jnp.einsum(
        "thi,thj->hij", fast_keys, back_first, preferred_element_type=jnp.float32
    )
    grad_third = jnp.einsum(
        "thi,thj->hij", fast_keys, back_third, preferred_element_type=jnp.float32
    )
    grad_second = jnp.einsum("thj,tho->hjo", gated_rows, scaled, preferred_element_type=jnp.float32)
    grad_first, grad_third, grad_second = lax.psum(
        (grad_first, grad_third, grad_second), ("view", "row")
    )
    new_first = renorm(w_first, grad_first, total_valid)
    new_third = renorm(w_third, grad_third, total_valid)
    new_second = renorm(w_second, grad_second, total_valid)
    applied = (
        jax.nn.silu(
            jnp.einsum("thi,hij->thj", fast_keys, new_first, preferred_element_type=jnp.float32)
        )
        * jnp.einsum("thi,hij->thj", fast_keys, new_third, preferred_element_type=jnp.float32)
    ).astype(jnp.bfloat16)
    fast_out = jnp.einsum(
        "thj,hjo->tho", applied, new_second, preferred_element_type=jnp.float32
    ).astype(jnp.bfloat16)
    return fast_out.reshape(1, row_count, col_count, feat_width)


def halve(values_in, size):
    if size & (size - 1) == 0:
        return values_in >> (size.bit_length() - 1)
    return lax.div(values_in, jnp.int32(size))


def dot(left, right, dims=(((1,), (0,)), ((), ()))):
    return lax.dot_general(left, right, dims, preferred_element_type=F32)


def flip(index, bits):
    bit = 1
    while bit <= bits:
        if bits & bit:
            index = index + bit - 2 * bit * lax.rem(lax.div(index, bit), 2)
        bit *= 2
    return index


def step_kernel(
    nr, nz, cols,
    q_hbm, k_hbm, v_hbm, t_hbm, rates_hbm, reach_hbm, count_hbm, wf_hbm, wt_hbm, ws_hbm,
    out_ref,
    q_ref, kv_ref, t_ref, rates_ref, reach_ref, count_ref, wft, ws, halo, raw, sall, cnt, gout, gside, gslant, gfull, gsum, gin, gtot,
    wold, news, ss,
    load_sem, row_send, row_recv, halo_recv, k_recv, view_send, side_recv, total_recv, near_recv, far_recv, on_recv,
):
    tokens, width = q_ref.shape
    rows_here = tokens // cols
    hid = width // nr
    edge = HALO * cols
    heads = width // ATT_HD
    pieces = total_recv.shape[0]
    piece = 3 * hid // pieces
    per = pieces // 3
    me = lax.axis_index("row")
    mz = lax.axis_index("view")
    partner, across = flip(me, 1), flip(me, 2)
    above, below = me + 1, me - 1
    mine = pl.ds(pl.multiple_of(me * hid, hid), hid)
    theirs = pl.ds(pl.multiple_of(across * hid, hid), hid)
    low = mz < nz // 2
    inner = jnp.where(low, mz + 1, mz - 1)
    outer = jnp.where(low, mz - 1, mz + 1)
    center = (mz > 0) & (mz < nz - 1)
    leaf = (mz == 0) | (mz == nz - 1)
    has_above = me < nr - 1
    has_below = me > 0

    barrier = pltpu.get_barrier_semaphore()
    for d in range(1, nr):
        pl.semaphore_signal(barrier, inc=1, device_id={"row": flip(me, d)}, device_id_type=MESH)
    pl.semaphore_signal(barrier, inc=1, device_id={"view": inner}, device_id_type=MESH)

    slant = jnp.where(center, outer, inner)
    pl.semaphore_signal(barrier, inc=1, device_id={"row": across, "view": slant}, device_id_type=MESH)

    @pl.when(center)
    def _():
        pl.semaphore_signal(barrier, inc=1, device_id={"view": outer}, device_id_type=MESH)

    loads = [
        pltpu.make_async_copy(source, target, load_sem.at[max(min(i, 7) if i < 11 else 8, 1) - 1])
        for i, (source, target) in enumerate((
            (k_hbm, kv_ref.at[0]), (v_hbm, kv_ref.at[1]), (count_hbm, count_ref), (reach_hbm, reach_ref),
            (t_hbm, t_ref), (rates_hbm, rates_ref), (q_hbm, q_ref),
            (wf_hbm.at[:, theirs], wft.at[:, pl.ds(0, hid)]), (wt_hbm.at[:, theirs], wft.at[:, pl.ds(hid, hid)]),
            (wf_hbm.at[:, mine], wft.at[:, pl.ds(2 * hid, hid)]), (wt_hbm.at[:, mine], wft.at[:, pl.ds(3 * hid, hid)]),
            (ws_hbm.at[theirs, :], ws.at[pl.ds(0, hid)]), (ws_hbm.at[mine, :], ws.at[pl.ds(hid, hid)]),
        ))
    ]
    for load in loads:
        load.start()

    def remote(source, target, sends, receives, axis, peer):
        return pltpu.make_async_remote_copy(
            src_ref=source, dst_ref=target, send_sem=sends, recv_sem=receives,
            device_id={axis: peer}, device_id_type=MESH,
        )

    @pl.when(me == 0)
    def _():
        halo[:, :edge] = jnp.zeros((2, edge, width), BF16)

    @pl.when(me == nr - 1)
    def _():
        halo[:, edge:] = jnp.zeros((2, edge, width), BF16)

    row_base = me * rows_here
    tok_base = me * tokens

    pl.semaphore_wait(barrier, nr + 1 + jnp.where(center, 1, 0))

    @pl.when(has_above)
    def _():
        for i, source in enumerate((k_hbm, v_hbm)):
            remote(
                source.at[pl.ds(tokens - edge, edge)], halo.at[i, pl.ds(0, edge)], row_send.at[0], halo_recv.at[0, i], "row", above
            ).start()

    @pl.when(has_below)
    def _():
        for i, source in enumerate((k_hbm, v_hbm)):
            remote(
                source.at[pl.ds(0, edge)], halo.at[i, pl.ds(edge, edge)], row_send.at[1], halo_recv.at[1, i], "row", below
            ).start()

    up_halo = remote(halo.at[:, pl.ds(edge, edge)], halo.at[:, pl.ds(0, edge)], row_send.at[0], row_recv.at[0], "row", above)
    down_halo = remote(halo.at[:, pl.ds(0, edge)], halo.at[:, pl.ds(edge, edge)], row_send.at[1], row_recv.at[1], "row", below)

    for load in loads[2:4]:
        load.wait()
    view_total = count_ref[0]
    cnt[0] = jnp.full((8, 128), view_total, jnp.int32).astype(F32)
    sub = lax.broadcasted_iota(jnp.int32, (tokens, tokens), 0)
    lane = lax.broadcasted_iota(jnp.int32, (tokens, tokens), 1)
    tok_col = tok_base + lax.broadcasted_iota(jnp.int32, (tokens, 1), 0)
    valid_col = (tok_col < view_total).astype(F32)
    for load in loads[4:6]:
        load.wait()
    rate_col = jnp.sum(jnp.where(sub == lane, rates_ref[...], 0.0), axis=1, keepdims=True)
    sall[0] = (rate_col * valid_col * t_ref[...].astype(F32)).astype(BF16)
    s_near = remote(sall.at[0], sall.at[1], row_send.at[2], row_recv.at[0], "row", partner)
    s_near.start()
    cnt_up = remote(cnt.at[0], cnt.at[1], view_send.at[0], row_recv.at[1], "view", inner)
    cnt_mid = remote(cnt.at[2], cnt.at[3], view_send.at[0], row_recv.at[2], "view", inner)
    cnt_down = remote(cnt.at[3], cnt.at[3], view_send.at[1], row_recv.at[2], "view", outer)

    @pl.when(leaf)
    def _():
        cnt_up.start()

    def allowed(q_tok, k_tok):
        q_row = halve(q_tok, cols)
        k_row = halve(k_tok + edge, cols) - HALO
        reach = jnp.zeros(q_tok.shape, jnp.int32)
        for r in range(rows_here):
            reach = jnp.where(q_row == r, reach_ref[r], reach)
        k_abs = k_row + row_base
        return (
            (jnp.abs(k_row - q_row) <= reach)
            & (k_abs >= 0)
            & (k_abs < nr * rows_here)
            & ((k_tok + tok_base < view_total) | (k_tok == q_tok))
        )

    near_ok = allowed(sub, lane)
    far_q = lax.broadcasted_iota(jnp.int32, (2 * edge, 2 * edge), 0)
    far_k = lax.broadcasted_iota(jnp.int32, (2 * edge, 2 * edge), 1)
    far_ok = allowed(
        jnp.where(far_q < edge, far_q, far_q - 2 * edge + tokens),
        jnp.where(far_k < edge, far_k - edge, far_k - edge + tokens),
    )
    root = 1.0 / math.sqrt(ATT_HD)
    spans = [slice(h * ATT_HD, (h + 1) * ATT_HD) for h in range(heads)]
    pltpu.make_async_copy(kv_ref, kv_ref, load_sem.at[0]).wait()
    loads[6].wait()
    inside = slice(edge, tokens - edge)
    ends = (slice(0, edge), slice(tokens - edge, tokens))

    def outer_rows(value):
        return jnp.concatenate([value[e] for e in ends], axis=0)

    def pass_keys(at, receives):
        return remote(raw.at[0, :, at], raw.at[1, :, at], row_send.at[2], receives, "row", partner)

    near = []
    for h, hs in enumerate(spans):
        scores = jnp.where(near_ok, dot(q_ref[:, hs], kv_ref[0, :, hs], NT) * root, -1e30)
        top = jnp.max(scores, axis=-1, keepdims=True)
        power = jnp.exp(scores - top)
        total = jnp.sum(power, axis=-1, keepdims=True)
        mix = dot(power.astype(BF16), kv_ref[1, :, hs])
        raw[0, h, inside] = (mix[inside] * (1.0 / total[inside])).astype(BF16)
        near.append((outer_rows(top), outer_rows(total), outer_rows(mix), outer_rows(q_ref.at[:, hs])))
    middle = pass_keys(pl.ds(edge, tokens - 2 * edge), k_recv.at[0])
    middle.start()
    pltpu.make_async_copy(wft, wft, load_sem.at[6]).wait()
    pltpu.make_async_copy(ws, ws, load_sem.at[7]).wait()
    def halo_here(i):
        @pl.when(has_below)
        def _():
            remote(halo.at[i, pl.ds(edge, edge)], halo.at[i, pl.ds(0, edge)], row_send.at[0], halo_recv.at[0, i], "row", above).wait_recv()

        @pl.when(has_above)
        def _():
            remote(halo.at[i, pl.ds(0, edge)], halo.at[i, pl.ds(edge, edge)], row_send.at[1], halo_recv.at[1, i], "row", below).wait_recv()

    def keys_of(d, rows_at):
        return jnp.concatenate(
            [jnp.concatenate([raw[d, h, at] for h in range(heads)], axis=1) for at in rows_at], axis=0
        )

    def token_norm(keys):
        total_sq = jnp.zeros((keys.shape[0], ATT_HD), F32)
        for hs in spans:
            part = keys[:, hs].astype(F32)
            total_sq = total_sq + part * part
        return lax.rsqrt(jnp.sum(total_sq, axis=-1, keepdims=True) * (1.0 / width) + 1e-06)

    def block(keys, steps, norm, half):
        both = dot(keys, wft[:, half * 2 * hid:(half + 1) * 2 * hid])
        back = dot(steps, ws[half * hid:(half + 1) * hid], NT)
        first = both[:, :hid] * norm
        third = both[:, hid:] * norm
        sig = jax.nn.sigmoid(first)
        gate = first * sig
        pulled = back * norm
        left = jnp.concatenate(
            [
                (pulled * third * (sig * (1.0 + first * (1.0 - sig)))).astype(BF16),
                (pulled * gate).astype(BF16),
            ],
            axis=1,
        )
        return left, (gate * third).astype(BF16)

    def token_set(rows_at):
        keys = jnp.concatenate([keys_of(d, rows_at) for d in range(2)], axis=0)
        steps = jnp.concatenate([sall[d, at] for d in range(2) for at in rows_at], axis=0)
        return keys, steps, token_norm(keys)

    def attend_edges():
        halo_here(0)
        partly = []
        for h, hs in enumerate(spans):
            near_top, near_sum, near_out, queries = near[h]
            far = jnp.where(far_ok, dot(queries, halo[0, :, hs], NT) * root, -1e30)
            top = jnp.maximum(near_top, jnp.max(far, axis=-1, keepdims=True))
            power = jnp.exp(far - top)
            keep = jnp.exp(near_top - top)
            inverse = 1.0 / (keep * near_sum + jnp.sum(power, axis=-1, keepdims=True))
            partly.append((power.astype(BF16), keep * near_out, inverse))
        halo_here(1)
        for h, hs in enumerate(spans):
            power, kept, inverse = partly[h]
            mix = ((kept + dot(power, halo[1, :, hs])) * inverse).astype(BF16)
            raw[0, h, ends[0]] = mix[:edge]
            raw[0, h, ends[1]] = mix[edge:]
        for e in ends:
            pass_keys(pl.ds(e.start, edge), k_recv.at[1]).start()

    @pl.when(~(has_above & has_below))
    def _():
        attend_edges()

    s_near.wait_recv()
    middle.wait_recv()
    inner_set = token_set((inside,))
    inner_blocks = [block(*inner_set, half) for half in range(2)]

    @pl.when(has_above & has_below)
    def _():
        attend_edges()

    def rows(i):
        return pl.ds(i * piece, piece)

    def skew(i):
        return pltpu.make_async_remote_copy(
            src_ref=gout.at[rows(i)], dst_ref=gslant.at[rows(i)], send_sem=row_send.at[4], recv_sem=side_recv.at[i],
            device_id={"row": across, "view": inner}, device_id_type=MESH,
        )

    def early(i):
        return remote(gsum.at[rows(i)], gin.at[rows(i)], view_send.at[2], side_recv.at[i], "view", inner)

    def aside(i):
        return remote(gout.at[rows(i)], gside.at[rows(i)], row_send.at[4], side_recv.at[i], "row", across)

    @pl.when(center)
    def _():
        cnt_up.wait_recv()
        cnt[2] = cnt[0] + cnt[1]
        cnt_mid.start()

    inner_left, inner_gated = inner_blocks[0]
    gfull[: 2 * hid] = dot(inner_left, inner_set[0], TN)
    gfull[2 * hid:] = dot(inner_gated, inner_set[1], TN)
    pass_keys(pl.ds(0, 2 * edge), k_recv.at[1]).wait_recv()
    outer_set = token_set(ends)
    left, gated = block(*outer_set, 0)
    for m in range(2):
        at = slice(m * hid, (m + 1) * hid)
        gout[at] = (gfull[at] + dot(left[:, at], outer_set[0], TN)).astype(BF16)
        if m == 0:
            @pl.when(leaf)
            def _():
                for i in range(SKIP):
                    skew(i).start()

            @pl.when(center)
            def _():
                for i in range(SKIP):
                    aside(i).start()

        for i in range(SKIP if m == 0 else per, (m + 1) * per):
            aside(i).start()
    gout[2 * hid:] = (gfull[2 * hid:] + dot(gated, outer_set[1], TN)).astype(BF16)
    for i in range(2 * per, 3 * per):
        aside(i).start()
    keys, steps = (jnp.concatenate(pair, axis=0) for pair in zip(inner_set[:2], outer_set[:2]))
    left, gated = (jnp.concatenate(pair, axis=0) for pair in zip(inner_blocks[1], block(*outer_set, 1)))
    gfull[: 2 * hid] = dot(left, keys, TN)

    @pl.when(leaf)
    def _():
        for i in range(SKIP):
            gsum[rows(i)] = gfull[rows(i)].astype(BF16)
            early(i).start()

    gfull[2 * hid:] = dot(gated, steps, TN)

    @pl.when(center)
    def _():
        cnt_mid.wait_recv()
        cnt[3] = cnt[2] + cnt[3]
        cnt_down.start()

    wold[0:hid] = wft[:, 2 * hid:3 * hid].astype(F32).T
    wold[hid:2 * hid] = wft[:, 3 * hid:].astype(F32).T
    wold[2 * hid:] = ws[hid:].astype(F32)
    ss[0, 2:3] = jnp.sum(wold[:hid] * wold[:hid], axis=0, keepdims=True)
    ss[0, 3:4] = jnp.sum(wold[hid:2 * hid] * wold[hid:2 * hid], axis=0, keepdims=True)
    second_old = wold[2 * hid:]
    second_size = jnp.sqrt(jnp.sum(second_old * second_old, axis=-1, keepdims=True) + 1e-06)

    def here(i, count):
        at = gin.at[pl.ds(0, count * piece)]
        return remote(at, at, view_send.at[2], side_recv.at[i], "view", inner)

    def rise(i, target, receives):
        return remote(gsum.at[rows(i)], target.at[rows(i)], view_send.at[2], receives.at[i], "view", inner)

    def fall(i):
        return remote(gtot.at[rows(i)], gtot.at[rows(i)], view_send.at[3], total_recv.at[i], "view", outer)

    def lift(i):
        if i < SKIP:
            return
        aside(i).wait_recv()
        gsum[rows(i)] = (gfull[rows(i)] + gside[rows(i)].astype(F32)).astype(BF16)
        rise(i, gin, side_recv).start()

    def join(i):
        here(i, 3 if i < SKIP else 2).wait_recv()
        partial = gfull[rows(i)] + gside[rows(i)].astype(F32)
        if i < SKIP:
            partial = partial + gslant[rows(i)].astype(F32)
        gsum[rows(i)] = (partial + gin[rows(i)].astype(F32)).astype(BF16)
        rise(i, gtot, total_recv).start()

    def finish(i):
        rise(i, gtot, total_recv).wait_recv()
        gtot[rows(i)] = (gsum[rows(i)].astype(F32) + gtot[rows(i)].astype(F32)).astype(BF16)
        fall(i).start()

    roles = (
        (low & center, join, finish, LAGS[0]),
        (~low & center, join, finish, LAGS[1]),
        (low & leaf, lift, None, LEADS[0]),
        (~low & leaf, lift, None, LEADS[1]),
    )
    for role, begin, _, ahead in roles:
        @pl.when(role)
        def _():
            for i in range(ahead):
                begin(i)
            if begin is lift:
                cnt_down.wait_recv()

    share_total = 1.0 / cnt[3, 0:1, 0:1]

    def arrive(i):
        for role, begin, end, ahead in roles:
            @pl.when(role)
            def _():
                if i + ahead < pieces:
                    begin(i + ahead)
                if end is None:
                    fall(i).wait_recv()
                else:
                    end(i)

    def raise_rows(i):
        raised = wold[rows(i)] + gtot[rows(i)].astype(F32) * share_total
        if i < 2 * per:
            news[0, rows(i)] = raised.astype(BF16)
            return jnp.sum(raised * raised, axis=0, keepdims=True)
        at = (i - 2 * per) * piece
        size = jnp.sqrt(jnp.sum(raised * raised, axis=-1, keepdims=True) + 1e-06)
        news[0, rows(i)] = (raised * (second_size[at:at + piece] / size)).astype(BF16)

    groups = [(0, per), (per, 2 * per), (2 * per, 3 * per - DIRECT), (3 * per - DIRECT, 3 * per)]

    def span(group):
        return pl.ds(group[0] * piece, (group[1] - group[0]) * piece)

    def group_of(i):
        return [g for g, group in enumerate(groups) if group[0] <= i < group[1]][0]

    def lend(i):
        return remote(news.at[0, rows(i)], news.at[2, rows(i)], row_send.at[4], far_recv.at[min(group_of(i), 3)], "row", across)

    def lend_over(i):
        return remote(news.at[0, rows(i)], news.at[3, rows(i)], row_send.at[4], on_recv.at[1], "row", flip(me, 3))

    def pair(g, slot, receives, sends=4):
        return remote(
            news.at[slot, span(groups[g])], news.at[slot + 1, span(groups[g])], row_send.at[sends], receives.at[g // 2 if g < 2 else 1], "row", partner
        )

    def parts_here(part, slot, receives):
        at = pl.ds(part * 2 * hid, (2 - part) * hid)
        remote(news.at[slot, at], news.at[slot + 1, at], row_send.at[4], receives.at[part], "row", partner).wait_recv()

    def relay(g):
        remote(
            news.at[0, span(groups[g])], news.at[2, span(groups[g])], row_send.at[4], far_recv.at[g], "row", across
        ).wait_recv()
        pair(g, 2, on_recv).start()

    ss_copies = [
        remote(ss.at[0], ss.at[d], row_send.at[3], row_recv.at[3], "row", flip(me, d)) for d in range(1, nr)
    ]
    for i in range(pieces):
        arrive(i)
        square = raise_rows(i)
        lend(i).start()
        if group_of(i) > 2:
            lend_over(i).start()
        for g, group in enumerate(groups):
            if group[1] == i + 1:
                pair(g, 0, near_recv).start()
        if i < 2 * per:
            running = square if i % per == 0 else running + square
            if i % per == per - 1:
                m = i // per
                ss[0, m:m + 1] = running
                if m == 1:
                    for copy in ss_copies:
                        copy.start()
    relay(0)
    relay(1)
    remote(ss.at[pl.ds(0, nr - 1)], ss.at[pl.ds(1, nr - 1)], row_send.at[3], row_recv.at[3], "row", partner).wait_recv()
    sums = ss[0]
    for d in range(1, nr):
        sums = sums + ss[d]
    scales = jnp.sqrt(sums[2:4] + 1e-06) / jnp.sqrt(sums[0:2] + 1e-06)
    own_keys = keys_of(0, (slice(0, tokens),))
    own_norm = token_norm(own_keys)
    wide = own_keys.astype(F32)
    scaled = [(wide * scales[m:m + 1]).astype(BF16) for m in range(2)]

    def apply(slot):
        first = dot(scaled[0], news[slot, :hid], NT) * own_norm
        third = dot(scaled[1], news[slot, hid:2 * hid], NT) * own_norm
        return (first * jax.nn.sigmoid(first) * third).astype(BF16)

    applied = [apply(0)]
    parts_here(0, 0, near_recv)
    applied.append(apply(1))
    applied.append(apply(2))
    relay(2)
    parts_here(0, 2, on_recv)
    applied.append(apply(3))
    total = dot(applied[0], news[0, 2 * hid:])
    parts_here(1, 0, near_recv)
    total = total + dot(applied[1], news[1, 2 * hid:])
    lent = span((groups[3][0], pieces))
    remote(news.at[0, lent], news.at[2, lent], row_send.at[4], far_recv.at[3], "row", across).wait_recv()
    total = total + dot(applied[2], news[2, 2 * hid:])
    parts_here(1, 2, on_recv)
    total = total + dot(applied[3], news[3, 2 * hid:])
    out_ref[...] = total.astype(BF16)

    @pl.when(has_above)
    def _():
        up_halo.wait_send()

    @pl.when(has_below)
    def _():
        down_halo.wait_send()

    remote(kv_ref, kv_ref, row_send.at[2], row_recv.at[0], "row", partner).wait_send()
    remote(news, news, row_send.at[4], row_recv.at[0], "row", partner).wait_send()
    remote(ss.at[pl.ds(0, nr - 1)], ss.at[pl.ds(1, nr - 1)], row_send.at[3], row_recv.at[3], "row", partner).wait_send()
    remote(gsum, gin, view_send.at[2], row_recv.at[0], "view", inner).wait_send()
    cnt_up.wait_send()

    @pl.when(center)
    def _():
        cnt_down.wait_send()
        remote(gtot, gtot, view_send.at[3], row_recv.at[0], "view", outer).wait_send()


def fused_step(
    nr, nz,
    query_feats, key_feats, value_feats, target, token_rates, row_reach, view_counts,
    w_first, w_third, w_second,
):
    _, row_count, cols, width = query_feats.shape
    tokens = row_count * cols
    hid = width // nr
    edge = HALO * cols
    heads = width // ATT_HD
    pieces = 3 * PER
    anywhere = pl.BlockSpec(memory_space=pl.ANY)
    flat = lambda a: a.reshape(tokens, width)
    out = pl.pallas_call(
        functools.partial(step_kernel, nr, nz, cols),
        out_shape=pltpu.VMEM((tokens, width), BF16),
        in_specs=[anywhere] * 5 + [pl.BlockSpec(memory_space=pltpu.HBM)] * 2 + [anywhere] * 3,
        out_specs=pl.BlockSpec(memory_space=pltpu.VMEM),
        scratch_shapes=[
            pltpu.VMEM((tokens, width), BF16),
            pltpu.VMEM((2, tokens, width), BF16),
            pltpu.VMEM((tokens, width), BF16),
            pltpu.VMEM((1, tokens), F32),
            pltpu.SMEM((row_count,), jnp.int32),
            pltpu.SMEM((1,), jnp.int32),
            pltpu.VMEM((width, 4 * hid), BF16),
            pltpu.VMEM((2 * hid, width), BF16),
            pltpu.VMEM((2, 2 * edge, width), BF16),
            pltpu.VMEM((2, heads, tokens, ATT_HD), BF16),
            pltpu.VMEM((2, tokens, width), BF16),
            pltpu.VMEM((4, 8, 128), F32),
            pltpu.VMEM((3 * hid, width), BF16),
            pltpu.VMEM((3 * hid, width), BF16),
            pltpu.VMEM((3 * hid, width), BF16),
            pltpu.VMEM((3 * hid, width), F32),
            pltpu.VMEM((3 * hid, width), BF16),
            pltpu.VMEM((3 * hid, width), BF16),
            pltpu.VMEM((3 * hid, width), BF16),
            pltpu.VMEM((3 * hid, width), F32),
            pltpu.VMEM((nr, 3 * hid, width), BF16),
            pltpu.VMEM((nr, 4, width), F32),
            pltpu.SemaphoreType.DMA((8,)),
            pltpu.SemaphoreType.DMA((5,)),
            pltpu.SemaphoreType.DMA((4,)),
            pltpu.SemaphoreType.DMA((2, 2)),
            pltpu.SemaphoreType.DMA((2,)),
            pltpu.SemaphoreType.DMA((4,)),
            pltpu.SemaphoreType.DMA((pieces,)),
            pltpu.SemaphoreType.DMA((pieces,)),
            pltpu.SemaphoreType.DMA((2,)),
            pltpu.SemaphoreType.DMA((4,)),
            pltpu.SemaphoreType.DMA((2,)),
        ],
        compiler_params=pltpu.CompilerParams(collective_id=0, has_side_effects=True),
    )(
        flat(query_feats), flat(key_feats), flat(value_feats), flat(target),
        token_rates.reshape(1, tokens), row_reach, view_counts,
        w_first.reshape(width, width), w_third.reshape(width, width), w_second.reshape(width, width),
    )
    return out.reshape(query_feats.shape)


def solution(mesh):
    placed = (
        P("view", "row", None, "head"),
        P("view", "row", None, "head"),
        P("view", "row", None, "head"),
        P("view", "row", None, "head"),
        P("view", "head", "row"),
        P("row"),
        P("view"),
        P("head", None, None),
        P("head", None, None),
        P("head", None, None),
    )
    nr, nz = mesh.shape["row"], mesh.shape["view"]
    fits = nr == 4 and nz == 4 and HD % (128 * nr) == 0 and HD % (16 * nr * PER) == 0
    return jax.shard_map(
        functools.partial(fused_step, nr, nz) if fits else per_device,
        mesh=mesh,
        in_specs=placed,
        out_specs=P("view", "row", None, "head"),
        check_vma=False,
    )
```

```python
import functools
import math

import jax
import jax.numpy as jnp
from jax import lax
from jax.experimental import pallas as pl
from jax.experimental.pallas import tpu as pltpu
from jax.sharding import PartitionSpec as P

HD = 512
ATT_HD = 128
HALO = 2
PER = 8
SKIP = 3
DIRECT = 2
LAGS = (9, 8)
LEADS = (24, 24)
MESH = pl.DeviceIdType.MESH
BF16 = jnp.bfloat16
F32 = jnp.float32
NT = (((1,), (1,)), ((), ()))
TN = (((0,), (0,)), ((), ()))


def with_halo(value, sides, width):
    for axis, dim in sides:
        size, length = (lax.axis_size(axis), value.shape[dim])
        up = [(i, (i + 1) % size) for i in range(size - 1)]
        down = [(j, i) for i, j in up]
        last = lax.slice_in_dim(value, length - width, length, axis=dim)
        leading = lax.slice_in_dim(value, 0, width, axis=dim)
        before = lax.ppermute(last, axis, up)
        after = lax.ppermute(leading, axis, down)
        value = jnp.concatenate([before, value, after], axis=dim)
    return value


def silu_slope(values_in):
    sigmoid_x = jax.nn.sigmoid(values_in)
    return sigmoid_x * (1.0 + values_in * (1.0 - sigmoid_x))


def attend(
    query_rows,
    key_rows,
    value_rows,
    q_row_ids,
    k_row_ids,
    q_tok,
    k_tok,
    k_valid,
    q_reach,
    grid_rows,
):
    count_q = query_rows.shape[0]
    count_k = key_rows.shape[0]
    groups = query_rows.shape[1] // ATT_HD
    query_heads = query_rows.reshape(count_q, groups, ATT_HD)
    key_heads = key_rows.reshape(count_k, groups, ATT_HD)
    value_heads = value_rows.reshape(count_k, groups, ATT_HD)
    scores = jnp.einsum(
        "qhd,khd->hqk", query_heads, key_heads, preferred_element_type=jnp.float32
    ) / math.sqrt(ATT_HD)
    inside = (k_row_ids >= 0) & (k_row_ids < grid_rows)
    in_band = jnp.abs(k_row_ids[None, :] - q_row_ids[:, None]) <= q_reach[:, None]
    allowed = in_band & inside[None, :] & (k_valid[None, :] | (k_tok[None, :] == q_tok[:, None]))
    scores = jnp.where(allowed[None], scores, -1e30)
    row_top = jnp.max(scores, -1, keepdims=True)
    powers = jnp.exp(scores - row_top)
    weights = (powers / jnp.sum(powers, -1, keepdims=True)).astype(jnp.bfloat16)
    output_rows = jnp.einsum(
        "hqk,khd->qhd", weights, value_heads, preferred_element_type=jnp.float32
    )
    return output_rows.reshape(count_q, groups * ATT_HD).astype(jnp.bfloat16)


def renorm(old_matrix, grad, total_valid):
    old_rows = old_matrix.astype(jnp.float32)
    raised = old_rows + grad / total_valid
    rescale = jnp.sqrt(jnp.sum(old_rows * old_rows, -1, keepdims=True) + 1e-06) / jnp.sqrt(
        jnp.sum(raised * raised, -1, keepdims=True) + 1e-06
    )
    return (raised * rescale).astype(jnp.bfloat16)


def per_device(
    query_feats,
    key_feats,
    value_feats,
    target,
    token_rates,
    row_reach,
    view_counts,
    w_first,
    w_third,
    w_second,
):
    row_count = query_feats.shape[1]
    col_count = query_feats.shape[2]
    feat_width = query_feats.shape[3]
    heads_here = feat_width // HD
    tokens_here = row_count * col_count
    key_span = row_count + 2 * HALO
    grid_rows = lax.axis_size("row") * row_count
    row_base = lax.axis_index("row") * row_count
    view_total = view_counts[0]
    total_valid = lax.psum(view_total.astype(jnp.float32), "view")
    paired = jnp.stack([key_feats[0], value_feats[0]], 0)
    padded = with_halo(paired, (("row", 1),), HALO)
    q_row_ids = row_base + jnp.repeat(jnp.arange(row_count, dtype=jnp.int32), col_count)
    k_row_ids = row_base - HALO + jnp.repeat(jnp.arange(key_span, dtype=jnp.int32), col_count)
    q_tok = q_row_ids * col_count + jnp.tile(jnp.arange(col_count, dtype=jnp.int32), row_count)
    k_tok = k_row_ids * col_count + jnp.tile(jnp.arange(col_count, dtype=jnp.int32), key_span)
    k_valid = k_tok < view_total
    q_reach = jnp.repeat(row_reach, col_count)
    attended = attend(
        query_feats[0].reshape(tokens_here, feat_width),
        padded[0].reshape(key_span * col_count, feat_width),
        padded[1].reshape(key_span * col_count, feat_width),
        q_row_ids,
        k_row_ids,
        q_tok,
        k_tok,
        k_valid,
        q_reach,
        grid_rows,
    )
    attended = attended.reshape(tokens_here, heads_here, HD).astype(jnp.float32)
    fast_keys = (
        attended * lax.rsqrt(jnp.mean(attended * attended, -1, keepdims=True) + 1e-06)
    ).astype(jnp.bfloat16)
    valid_mask = (q_tok < view_total).astype(jnp.float32)
    rates_tok = token_rates[0].T
    scaled = (
        rates_tok[:, :, None]
        * valid_mask[:, None, None]
        * target[0].reshape(tokens_here, heads_here, HD).astype(jnp.float32)
    ).astype(jnp.bfloat16)
    first_proj = jnp.einsum("thi,hij->thj", fast_keys, w_first, preferred_element_type=jnp.float32)
    third_proj = jnp.einsum("thi,hij->thj", fast_keys, w_third, preferred_element_type=jnp.float32)
    gated_rows = (jax.nn.silu(first_proj) * third_proj).astype(jnp.bfloat16)
    back_rows = jnp.einsum("tho,hjo->thj", scaled, w_second, preferred_element_type=jnp.float32)
    back_first = (back_rows * third_proj * silu_slope(first_proj)).astype(jnp.bfloat16)
    back_third = (back_rows * jax.nn.silu(first_proj)).astype(jnp.bfloat16)
    grad_first = jnp.einsum(
        "thi,thj->hij", fast_keys, back_first, preferred_element_type=jnp.float32
    )
    grad_third = jnp.einsum(
        "thi,thj->hij", fast_keys, back_third, preferred_element_type=jnp.float32
    )
    grad_second = jnp.einsum("thj,tho->hjo", gated_rows, scaled, preferred_element_type=jnp.float32)
    grad_first, grad_third, grad_second = lax.psum(
        (grad_first, grad_third, grad_second), ("view", "row")
    )
    new_first = renorm(w_first, grad_first, total_valid)
    new_third = renorm(w_third, grad_third, total_valid)
    new_second = renorm(w_second, grad_second, total_valid)
    applied = (
        jax.nn.silu(
            jnp.einsum("thi,hij->thj", fast_keys, new_first, preferred_element_type=jnp.float32)
        )
        * jnp.einsum("thi,hij->thj", fast_keys, new_third, preferred_element_type=jnp.float32)
    ).astype(jnp.bfloat16)
    fast_out = jnp.einsum(
        "thj,hjo->tho", applied, new_second, preferred_element_type=jnp.float32
    ).astype(jnp.bfloat16)
    return fast_out.reshape(1, row_count, col_count, feat_width)


def halve(values_in, size):
    if size & (size - 1) == 0:
        return values_in >> (size.bit_length() - 1)
    return lax.div(values_in, jnp.int32(size))


def dot(left, right, dims=(((1,), (0,)), ((), ()))):
    return lax.dot_general(left, right, dims, preferred_element_type=F32)


def flip(index, bits):
    bit = 1
    while bit <= bits:
        if bits & bit:
            index = index + bit - 2 * bit * lax.rem(lax.div(index, bit), 2)
        bit *= 2
    return index


def step_kernel(
    nr, nz, cols,
    q_hbm, k_hbm, v_hbm, t_hbm, rates_hbm, reach_hbm, count_hbm, wf_hbm, wt_hbm, ws_hbm,
    out_ref,
    q_ref, kv_ref, t_ref, rates_ref, reach_ref, count_ref, wft, ws, halo, raw, sall, cnt, gout, gside, gslant, gfull, gsum, gin, gtot,
    wold, news, ss,
    load_sem, row_send, row_recv, halo_recv, k_recv, view_send, side_recv, total_recv, near_recv, far_recv, on_recv,
):
    tokens, width = q_ref.shape
    rows_here = tokens // cols
    hid = width // nr
    edge = HALO * cols
    heads = width // ATT_HD
    pieces = total_recv.shape[0]
    piece = 3 * hid // pieces
    per = pieces // 3
    me = lax.axis_index("row")
    mz = lax.axis_index("view")
    partner, across = flip(me, 1), flip(me, 2)
    above, below = me + 1, me - 1
    mine = pl.ds(pl.multiple_of(me * hid, hid), hid)
    theirs = pl.ds(pl.multiple_of(across * hid, hid), hid)
    low = mz < nz // 2
    inner = jnp.where(low, mz + 1, mz - 1)
    outer = jnp.where(low, mz - 1, mz + 1)
    center = (mz > 0) & (mz < nz - 1)
    leaf = (mz == 0) | (mz == nz - 1)
    has_above = me < nr - 1
    has_below = me > 0

    barrier = pltpu.get_barrier_semaphore()
    for d in range(1, nr):
        pl.semaphore_signal(barrier, inc=1, device_id={"row": flip(me, d)}, device_id_type=MESH)
    pl.semaphore_signal(barrier, inc=1, device_id={"view": inner}, device_id_type=MESH)

    slant = jnp.where(center, outer, inner)
    pl.semaphore_signal(barrier, inc=1, device_id={"row": across, "view": slant}, device_id_type=MESH)

    @pl.when(center)
    def _():
        pl.semaphore_signal(barrier, inc=1, device_id={"view": outer}, device_id_type=MESH)

    loads = [
        pltpu.make_async_copy(source, target, load_sem.at[max(min(i, 7) if i < 11 else 8, 1) - 1])
        for i, (source, target) in enumerate((
            (k_hbm, kv_ref.at[0]), (v_hbm, kv_ref.at[1]), (count_hbm, count_ref), (reach_hbm, reach_ref),
            (t_hbm, t_ref), (rates_hbm, rates_ref), (q_hbm, q_ref),
            (wf_hbm.at[:, theirs], wft.at[:, pl.ds(0, hid)]), (wt_hbm.at[:, theirs], wft.at[:, pl.ds(hid, hid)]),
            (wf_hbm.at[:, mine], wft.at[:, pl.ds(2 * hid, hid)]), (wt_hbm.at[:, mine], wft.at[:, pl.ds(3 * hid, hid)]),
            (ws_hbm.at[theirs, :], ws.at[pl.ds(0, hid)]), (ws_hbm.at[mine, :], ws.at[pl.ds(hid, hid)]),
        ))
    ]
    for load in loads:
        load.start()

    def remote(source, target, sends, receives, axis, peer):
        return pltpu.make_async_remote_copy(
            src_ref=source, dst_ref=target, send_sem=sends, recv_sem=receives,
            device_id={axis: peer}, device_id_type=MESH,
        )

    @pl.when(me == 0)
    def _():
        halo[:, :edge] = jnp.zeros((2, edge, width), BF16)

    @pl.when(me == nr - 1)
    def _():
        halo[:, edge:] = jnp.zeros((2, edge, width), BF16)

    row_base = me * rows_here
    tok_base = me * tokens

    pl.semaphore_wait(barrier, nr + 1 + jnp.where(center, 1, 0))

    @pl.when(has_above)
    def _():
        for i, source in enumerate((k_hbm, v_hbm)):
            remote(
                source.at[pl.ds(tokens - edge, edge)], halo.at[i, pl.ds(0, edge)], row_send.at[0], halo_recv.at[0, i], "row", above
            ).start()

    @pl.when(has_below)
    def _():
        for i, source in enumerate((k_hbm, v_hbm)):
            remote(
                source.at[pl.ds(0, edge)], halo.at[i, pl.ds(edge, edge)], row_send.at[1], halo_recv.at[1, i], "row", below
            ).start()

    up_halo = remote(halo.at[:, pl.ds(edge, edge)], halo.at[:, pl.ds(0, edge)], row_send.at[0], row_recv.at[0], "row", above)
    down_halo = remote(halo.at[:, pl.ds(0, edge)], halo.at[:, pl.ds(edge, edge)], row_send.at[1], row_recv.at[1], "row", below)

    for load in loads[2:4]:
        load.wait()
    view_total = count_ref[0]
    cnt[0] = jnp.full((8, 128), view_total, jnp.int32).astype(F32)
    sub = lax.broadcasted_iota(jnp.int32, (tokens, tokens), 0)
    lane = lax.broadcasted_iota(jnp.int32, (tokens, tokens), 1)
    tok_col = tok_base + lax.broadcasted_iota(jnp.int32, (tokens, 1), 0)
    valid_col = (tok_col < view_total).astype(F32)
    for load in loads[4:6]:
        load.wait()
    rate_col = jnp.sum(jnp.where(sub == lane, rates_ref[...], 0.0), axis=1, keepdims=True)
    sall[0] = (rate_col * valid_col * t_ref[...].astype(F32)).astype(BF16)
    s_near = remote(sall.at[0], sall.at[1], row_send.at[2], row_recv.at[0], "row", partner)
    s_near.start()
    cnt_up = remote(cnt.at[0], cnt.at[1], view_send.at[0], row_recv.at[1], "view", inner)
    cnt_mid = remote(cnt.at[2], cnt.at[3], view_send.at[0], row_recv.at[2], "view", inner)
    cnt_down = remote(cnt.at[3], cnt.at[3], view_send.at[1], row_recv.at[2], "view", outer)

    @pl.when(leaf)
    def _():
        cnt_up.start()

    def allowed(q_tok, k_tok):
        q_row = halve(q_tok, cols)
        k_row = halve(k_tok + edge, cols) - HALO
        reach = jnp.zeros(q_tok.shape, jnp.int32)
        for r in range(rows_here):
            reach = jnp.where(q_row == r, reach_ref[r], reach)
        k_abs = k_row + row_base
        return (
            (jnp.abs(k_row - q_row) <= reach)
            & (k_abs >= 0)
            & (k_abs < nr * rows_here)
            & ((k_tok + tok_base < view_total) | (k_tok == q_tok))
        )

    near_ok = allowed(sub, lane)
    far_q = lax.broadcasted_iota(jnp.int32, (2 * edge, 2 * edge), 0)
    far_k = lax.broadcasted_iota(jnp.int32, (2 * edge, 2 * edge), 1)
    far_ok = allowed(
        jnp.where(far_q < edge, far_q, far_q - 2 * edge + tokens),
        jnp.where(far_k < edge, far_k - edge, far_k - edge + tokens),
    )
    root = 1.0 / math.sqrt(ATT_HD)
    spans = [slice(h * ATT_HD, (h + 1) * ATT_HD) for h in range(heads)]
    pltpu.make_async_copy(kv_ref, kv_ref, load_sem.at[0]).wait()
    loads[6].wait()
    inside = slice(edge, tokens - edge)
    ends = (slice(0, edge), slice(tokens - edge, tokens))

    def outer_rows(value):
        return jnp.concatenate([value[e] for e in ends], axis=0)

    def pass_keys(at, receives):
        return remote(raw.at[0, :, at], raw.at[1, :, at], row_send.at[2], receives, "row", partner)

    near = []
    for h, hs in enumerate(spans):
        scores = jnp.where(near_ok, dot(q_ref[:, hs], kv_ref[0, :, hs], NT) * root, -1e30)
        top = jnp.max(scores, axis=-1, keepdims=True)
        power = jnp.exp(scores - top)
        total = jnp.sum(power, axis=-1, keepdims=True)
        mix = dot(power.astype(BF16), kv_ref[1, :, hs])
        raw[0, h, inside] = (mix[inside] * (1.0 / total[inside])).astype(BF16)
        near.append((outer_rows(top), outer_rows(total), outer_rows(mix), outer_rows(q_ref.at[:, hs])))
    middle = pass_keys(pl.ds(edge, tokens - 2 * edge), k_recv.at[0])
    middle.start()
    pltpu.make_async_copy(wft, wft, load_sem.at[6]).wait()
    pltpu.make_async_copy(ws, ws, load_sem.at[7]).wait()
    def halo_here(i):
        @pl.when(has_below)
        def _():
            remote(halo.at[i, pl.ds(edge, edge)], halo.at[i, pl.ds(0, edge)], row_send.at[0], halo_recv.at[0, i], "row", above).wait_recv()

        @pl.when(has_above)
        def _():
            remote(halo.at[i, pl.ds(0, edge)], halo.at[i, pl.ds(edge, edge)], row_send.at[1], halo_recv.at[1, i], "row", below).wait_recv()

    def keys_of(d, rows_at):
        return jnp.concatenate(
            [jnp.concatenate([raw[d, h, at] for h in range(heads)], axis=1) for at in rows_at], axis=0
        )

    def token_norm(keys):
        total_sq = jnp.zeros((keys.shape[0], ATT_HD), F32)
        for hs in spans:
            part = keys[:, hs].astype(F32)
            total_sq = total_sq + part * part
        return lax.rsqrt(jnp.sum(total_sq, axis=-1, keepdims=True) * (1.0 / width) + 1e-06)

    def block(keys, steps, norm, half):
        both = dot(keys, wft[:, half * 2 * hid:(half + 1) * 2 * hid])
        back = dot(steps, ws[half * hid:(half + 1) * hid], NT)
        first = both[:, :hid] * norm
        third = both[:, hid:] * norm
        sig = jax.nn.sigmoid(first)
        gate = first * sig
        pulled = back * norm
        left = jnp.concatenate(
            [
                (pulled * third * (sig * (1.0 + first * (1.0 - sig)))).astype(BF16),
                (pulled * gate).astype(BF16),
            ],
            axis=1,
        )
        return left, (gate * third).astype(BF16)

    def token_set(rows_at):
        keys = jnp.concatenate([keys_of(d, rows_at) for d in range(2)], axis=0)
        steps = jnp.concatenate([sall[d, at] for d in range(2) for at in rows_at], axis=0)
        return keys, steps, token_norm(keys)

    def attend_edges():
        halo_here(0)
        partly = []
        for h, hs in enumerate(spans):
            near_top, near_sum, near_out, queries = near[h]
            far = jnp.where(far_ok, dot(queries, halo[0, :, hs], NT) * root, -1e30)
            top = jnp.maximum(near_top, jnp.max(far, axis=-1, keepdims=True))
            power = jnp.exp(far - top)
            keep = jnp.exp(near_top - top)
            inverse = 1.0 / (keep * near_sum + jnp.sum(power, axis=-1, keepdims=True))
            partly.append((power.astype(BF16), keep * near_out, inverse))
        halo_here(1)
        for h, hs in enumerate(spans):
            power, kept, inverse = partly[h]
            mix = ((kept + dot(power, halo[1, :, hs])) * inverse).astype(BF16)
            raw[0, h, ends[0]] = mix[:edge]
            raw[0, h, ends[1]] = mix[edge:]
        for e in ends:
            pass_keys(pl.ds(e.start, edge), k_recv.at[1]).start()

    @pl.when(~(has_above & has_below) | (me < nr // 2))
    def _():
        attend_edges()

    s_near.wait_recv()
    middle.wait_recv()
    inner_set = token_set((inside,))
    inner_blocks = [block(*inner_set, half) for half in range(2)]

    @pl.when(has_above & has_below & (me >= nr // 2))
    def _():
        attend_edges()

    def rows(i):
        return pl.ds(i * piece, piece)

    def skew(i):
        return pltpu.make_async_remote_copy(
            src_ref=gout.at[rows(i)], dst_ref=gslant.at[rows(i)], send_sem=row_send.at[4], recv_sem=side_recv.at[i],
            device_id={"row": across, "view": inner}, device_id_type=MESH,
        )

    def early(i):
        return remote(gsum.at[rows(i)], gin.at[rows(i)], view_send.at[2], side_recv.at[i], "view", inner)

    def aside(i):
        return remote(gout.at[rows(i)], gside.at[rows(i)], row_send.at[4], side_recv.at[i], "row", across)

    @pl.when(center)
    def _():
        cnt_up.wait_recv()
        cnt[2] = cnt[0] + cnt[1]
        cnt_mid.start()

    inner_left, inner_gated = inner_blocks[0]
    gfull[: 2 * hid] = dot(inner_left, inner_set[0], TN)
    gfull[2 * hid:] = dot(inner_gated, inner_set[1], TN)
    pass_keys(pl.ds(0, 2 * edge), k_recv.at[1]).wait_recv()
    outer_set = token_set(ends)
    left, gated = block(*outer_set, 0)
    for m in range(2):
        at = slice(m * hid, (m + 1) * hid)
        gout[at] = (gfull[at] + dot(left[:, at], outer_set[0], TN)).astype(BF16)
        if m == 0:
            @pl.when(leaf)
            def _():
                for i in range(SKIP):
                    skew(i).start()

            @pl.when(center)
            def _():
                for i in range(SKIP):
                    aside(i).start()

        for i in range(SKIP if m == 0 else per, (m + 1) * per):
            aside(i).start()
    gout[2 * hid:] = (gfull[2 * hid:] + dot(gated, outer_set[1], TN)).astype(BF16)
    for i in range(2 * per, 3 * per):
        aside(i).start()
    keys, steps = (jnp.concatenate(pair, axis=0) for pair in zip(inner_set[:2], outer_set[:2]))
    left, gated = (jnp.concatenate(pair, axis=0) for pair in zip(inner_blocks[1], block(*outer_set, 1)))
    gfull[: 2 * hid] = dot(left, keys, TN)

    @pl.when(leaf)
    def _():
        for i in range(SKIP):
            gsum[rows(i)] = gfull[rows(i)].astype(BF16)
            early(i).start()

    gfull[2 * hid:] = dot(gated, steps, TN)

    @pl.when(center)
    def _():
        cnt_mid.wait_recv()
        cnt[3] = cnt[2] + cnt[3]
        cnt_down.start()

    wold[0:hid] = wft[:, 2 * hid:3 * hid].astype(F32).T
    wold[hid:2 * hid] = wft[:, 3 * hid:].astype(F32).T
    wold[2 * hid:] = ws[hid:].astype(F32)
    ss[0, 2:3] = jnp.sum(wold[:hid] * wold[:hid], axis=0, keepdims=True)
    ss[0, 3:4] = jnp.sum(wold[hid:2 * hid] * wold[hid:2 * hid], axis=0, keepdims=True)
    second_old = wold[2 * hid:]
    second_size = jnp.sqrt(jnp.sum(second_old * second_old, axis=-1, keepdims=True) + 1e-06)

    def here(i, count):
        at = gin.at[pl.ds(0, count * piece)]
        return remote(at, at, view_send.at[2], side_recv.at[i], "view", inner)

    def rise(i, target, receives):
        return remote(gsum.at[rows(i)], target.at[rows(i)], view_send.at[2], receives.at[i], "view", inner)

    def fall(i):
        return remote(gtot.at[rows(i)], gtot.at[rows(i)], view_send.at[3], total_recv.at[i], "view", outer)

    def lift(i):
        if i < SKIP:
            return
        aside(i).wait_recv()
        gsum[rows(i)] = (gfull[rows(i)] + gside[rows(i)].astype(F32)).astype(BF16)
        rise(i, gin, side_recv).start()

    def join(i):
        here(i, 3 if i < SKIP else 2).wait_recv()
        partial = gfull[rows(i)] + gside[rows(i)].astype(F32)
        if i < SKIP:
            partial = partial + gslant[rows(i)].astype(F32)
        gsum[rows(i)] = (partial + gin[rows(i)].astype(F32)).astype(BF16)
        rise(i, gtot, total_recv).start()

    def finish(i):
        rise(i, gtot, total_recv).wait_recv()
        gtot[rows(i)] = (gsum[rows(i)].astype(F32) + gtot[rows(i)].astype(F32)).astype(BF16)
        fall(i).start()

    roles = (
        (low & center, join, finish, LAGS[0]),
        (~low & center, join, finish, LAGS[1]),
        (low & leaf, lift, None, LEADS[0]),
        (~low & leaf, lift, None, LEADS[1]),
    )
    for role, begin, _, ahead in roles:
        @pl.when(role)
        def _():
            for i in range(ahead):
                begin(i)
            if begin is lift:
                cnt_down.wait_recv()

    share_total = 1.0 / cnt[3, 0:1, 0:1]

    def arrive(i):
        for role, begin, end, ahead in roles:
            @pl.when(role)
            def _():
                if i + ahead < pieces:
                    begin(i + ahead)
                if end is None:
                    fall(i).wait_recv()
                else:
                    end(i)

    def raise_rows(i):
        raised = wold[rows(i)] + gtot[rows(i)].astype(F32) * share_total
        if i < 2 * per:
            news[0, rows(i)] = raised.astype(BF16)
            return jnp.sum(raised * raised, axis=0, keepdims=True)
        at = (i - 2 * per) * piece
        size = jnp.sqrt(jnp.sum(raised * raised, axis=-1, keepdims=True) + 1e-06)
        news[0, rows(i)] = (raised * (second_size[at:at + piece] / size)).astype(BF16)

    groups = [(0, per), (per, 2 * per), (2 * per, 3 * per - DIRECT), (3 * per - DIRECT, 3 * per)]

    def span(group):
        return pl.ds(group[0] * piece, (group[1] - group[0]) * piece)

    def group_of(i):
        return [g for g, group in enumerate(groups) if group[0] <= i < group[1]][0]

    def lend(i):
        return remote(news.at[0, rows(i)], news.at[2, rows(i)], row_send.at[4], far_recv.at[min(group_of(i), 3)], "row", across)

    def lend_over(i):
        return remote(news.at[0, rows(i)], news.at[3, rows(i)], row_send.at[4], on_recv.at[1], "row", flip(me, 3))

    def pair(g, slot, receives, sends=4):
        return remote(
            news.at[slot, span(groups[g])], news.at[slot + 1, span(groups[g])], row_send.at[sends], receives.at[g // 2 if g < 2 else 1], "row", partner
        )

    def parts_here(part, slot, receives):
        at = pl.ds(part * 2 * hid, (2 - part) * hid)
        remote(news.at[slot, at], news.at[slot + 1, at], row_send.at[4], receives.at[part], "row", partner).wait_recv()

    def relay(g):
        remote(
            news.at[0, span(groups[g])], news.at[2, span(groups[g])], row_send.at[4], far_recv.at[g], "row", across
        ).wait_recv()
        pair(g, 2, on_recv).start()

    ss_copies = [
        remote(ss.at[0], ss.at[d], row_send.at[3], row_recv.at[3], "row", flip(me, d)) for d in range(1, nr)
    ]
    for i in range(pieces):
        arrive(i)
        square = raise_rows(i)
        lend(i).start()
        if group_of(i) > 2:
            lend_over(i).start()
        for g, group in enumerate(groups):
            if group[1] == i + 1:
                pair(g, 0, near_recv).start()
        if i < 2 * per:
            running = square if i % per == 0 else running + square
            if i % per == per - 1:
                m = i // per
                ss[0, m:m + 1] = running
                if m == 1:
                    for copy in ss_copies:
                        copy.start()
    relay(0)
    relay(1)
    remote(ss.at[pl.ds(0, nr - 1)], ss.at[pl.ds(1, nr - 1)], row_send.at[3], row_recv.at[3], "row", partner).wait_recv()
    sums = ss[0]
    for d in range(1, nr):
        sums = sums + ss[d]
    scales = jnp.sqrt(sums[2:4] + 1e-06) / jnp.sqrt(sums[0:2] + 1e-06)
    own_keys = keys_of(0, (slice(0, tokens),))
    own_norm = token_norm(own_keys)
    wide = own_keys.astype(F32)
    scaled = [(wide * scales[m:m + 1]).astype(BF16) for m in range(2)]

    def apply(slot):
        first = dot(scaled[0], news[slot, :hid], NT) * own_norm
        third = dot(scaled[1], news[slot, hid:2 * hid], NT) * own_norm
        return (first * jax.nn.sigmoid(first) * third).astype(BF16)

    applied = [apply(0)]
    parts_here(0, 0, near_recv)
    applied.append(apply(1))
    applied.append(apply(2))
    relay(2)
    parts_here(0, 2, on_recv)
    applied.append(apply(3))
    total = dot(applied[0], news[0, 2 * hid:])
    parts_here(1, 0, near_recv)
    total = total + dot(applied[1], news[1, 2 * hid:])
    lent = span((groups[3][0], pieces))
    remote(news.at[0, lent], news.at[2, lent], row_send.at[4], far_recv.at[3], "row", across).wait_recv()
    total = total + dot(applied[2], news[2, 2 * hid:])
    parts_here(1, 2, on_recv)
    total = total + dot(applied[3], news[3, 2 * hid:])
    out_ref[...] = total.astype(BF16)

    @pl.when(has_above)
    def _():
        up_halo.wait_send()

    @pl.when(has_below)
    def _():
        down_halo.wait_send()

    remote(kv_ref, kv_ref, row_send.at[2], row_recv.at[0], "row", partner).wait_send()
    remote(news, news, row_send.at[4], row_recv.at[0], "row", partner).wait_send()
    remote(ss.at[pl.ds(0, nr - 1)], ss.at[pl.ds(1, nr - 1)], row_send.at[3], row_recv.at[3], "row", partner).wait_send()
    remote(gsum, gin, view_send.at[2], row_recv.at[0], "view", inner).wait_send()
    cnt_up.wait_send()

    @pl.when(center)
    def _():
        cnt_down.wait_send()
        remote(gtot, gtot, view_send.at[3], row_recv.at[0], "view", outer).wait_send()


def fused_step(
    nr, nz,
    query_feats, key_feats, value_feats, target, token_rates, row_reach, view_counts,
    w_first, w_third, w_second,
):
    _, row_count, cols, width = query_feats.shape
    tokens = row_count * cols
    hid = width // nr
    edge = HALO * cols
    heads = width // ATT_HD
    pieces = 3 * PER
    anywhere = pl.BlockSpec(memory_space=pl.ANY)
    flat = lambda a: a.reshape(tokens, width)
    out = pl.pallas_call(
        functools.partial(step_kernel, nr, nz, cols),
        out_shape=pltpu.VMEM((tokens, width), BF16),
        in_specs=[anywhere] * 5 + [pl.BlockSpec(memory_space=pltpu.HBM)] * 2 + [anywhere] * 3,
        out_specs=pl.BlockSpec(memory_space=pltpu.VMEM),
        scratch_shapes=[
            pltpu.VMEM((tokens, width), BF16),
            pltpu.VMEM((2, tokens, width), BF16),
            pltpu.VMEM((tokens, width), BF16),
            pltpu.VMEM((1, tokens), F32),
            pltpu.SMEM((row_count,), jnp.int32),
            pltpu.SMEM((1,), jnp.int32),
            pltpu.VMEM((width, 4 * hid), BF16),
            pltpu.VMEM((2 * hid, width), BF16),
            pltpu.VMEM((2, 2 * edge, width), BF16),
            pltpu.VMEM((2, heads, tokens, ATT_HD), BF16),
            pltpu.VMEM((2, tokens, width), BF16),
            pltpu.VMEM((4, 8, 128), F32),
            pltpu.VMEM((3 * hid, width), BF16),
            pltpu.VMEM((3 * hid, width), BF16),
            pltpu.VMEM((3 * hid, width), BF16),
            pltpu.VMEM((3 * hid, width), F32),
            pltpu.VMEM((3 * hid, width), BF16),
            pltpu.VMEM((3 * hid, width), BF16),
            pltpu.VMEM((3 * hid, width), BF16),
            pltpu.VMEM((3 * hid, width), F32),
            pltpu.VMEM((nr, 3 * hid, width), BF16),
            pltpu.VMEM((nr, 4, width), F32),
            pltpu.SemaphoreType.DMA((8,)),
            pltpu.SemaphoreType.DMA((5,)),
            pltpu.SemaphoreType.DMA((4,)),
            pltpu.SemaphoreType.DMA((2, 2)),
            pltpu.SemaphoreType.DMA((2,)),
            pltpu.SemaphoreType.DMA((4,)),
            pltpu.SemaphoreType.DMA((pieces,)),
            pltpu.SemaphoreType.DMA((pieces,)),
            pltpu.SemaphoreType.DMA((2,)),
            pltpu.SemaphoreType.DMA((4,)),
            pltpu.SemaphoreType.DMA((2,)),
        ],
        compiler_params=pltpu.CompilerParams(collective_id=0, has_side_effects=True),
    )(
        flat(query_feats), flat(key_feats), flat(value_feats), flat(target),
        token_rates.reshape(1, tokens), row_reach, view_counts,
        w_first.reshape(width, width), w_third.reshape(width, width), w_second.reshape(width, width),
    )
    return out.reshape(query_feats.shape)


def solution(mesh):
    placed = (
        P("view", "row", None, "head"),
        P("view", "row", None, "head"),
        P("view", "row", None, "head"),
        P("view", "row", None, "head"),
        P("view", "head", "row"),
        P("row"),
        P("view"),
        P("head", None, None),
        P("head", None, None),
        P("head", None, None),
    )
    nr, nz = mesh.shape["row"], mesh.shape["view"]
    fits = nr == 4 and nz == 4 and HD % (128 * nr) == 0 and HD % (16 * nr * PER) == 0
    return jax.shard_map(
        functools.partial(fused_step, nr, nz) if fits else per_device,
        mesh=mesh,
        in_specs=placed,
        out_specs=P("view", "row", None, "head"),
        check_vma=False,
    )
```
